32 devices in a mesh: ctx: 8 (over z, x), seq: 2 (over y), tp: 2 (over core).
Axes of the slice: x: 2, y: 2, z: 4, core: 2. Of those that a mesh axis runs over, the one named last changes fastest.
Arguments:
- tokens: bfloat16 [4, 1024, 1024], P('seq', 'ctx'), may hold values from -6 to 6
- positions: int32 [4, 1024], P('seq', 'ctx'), may hold values from 0 to 1023, as said below
- attn_gain: float32 [1024], replicated, may hold values from 0.5 to 1.5
- ffn_gain: float32 [1024], replicated, may hold values from 0.5 to 1.5
- q_gain: float32 [64], replicated, may hold values from 0.5 to 1.5, as said below
- k_gain: float32 [64], replicated, may hold values from 0.5 to 1.5, as said below
- w_query: bfloat16 [1024, 1024], P(None, 'tp'), may hold values from -0.1875 to 0.1875
- w_key: bfloat16 [1024, 512], P(None, 'tp'), may hold values from -0.1875 to 0.1875
- w_value: bfloat16 [1024, 512], P(None, 'tp'), may hold values from -0.1875 to 0.1875
- w_out: bfloat16 [1024, 1024], P(None, 'tp'), may hold values from -1.5 to 1.5
- w_gate: bfloat16 [1024, 4608], P(None, 'tp'), may hold values from -0.1875 to 0.1875
- w_up: bfloat16 [1024, 4608], P(None, 'tp'), may hold values from -0.1875 to 0.1875
- w_down: bfloat16 [1024, 4608], P(None, 'tp'), may hold values from -0.09375 to 0.09375
- cotangent: bfloat16 [4, 1024, 1024], P('seq', 'ctx'), may hold values from -6 to 6
Outputs:
- layer_output: float32 [4, 1024, 1024], P('seq', 'ctx')
- input_grad: float32 [4, 1024, 1024], P('seq', 'ctx')
- wq_grad: float32 [1024, 1024], P(('ctx', 'seq'), 'tp')
- wk_grad: float32 [1024, 512], P(('ctx', 'seq'), 'tp')
- wv_grad: float32 [1024, 512], P(('ctx', 'seq'), 'tp')
- wo_grad: float32 [1024, 1024], P(('ctx', 'seq'), 'tp')
- wgate_grad: float32 [1024, 4608], P(('ctx', 'seq'), 'tp')
- wup_grad: float32 [1024, 4608], P(('ctx', 'seq'), 'tp')
- wdown_grad: float32 [1024, 4608], P(('ctx', 'seq'), 'tp')
- attngain_grad: float32 [1024], P(('ctx', 'seq'))
- ffngain_grad: float32 [1024], P(('ctx', 'seq'))
- qgain_grad: float32 [64], replicated
- kgain_grad: float32 [64], replicated
The draws below stay inside these ranges and needn't reach their ends.
Inputs may be any that keep to these rules, and one draw needn't show every extreme that they name: positions[b, i] is i minus the first index of the document that holds token i of sequence b: 0 at a document's first token and at i = 0, else one more than at i - 1; sequence 0 is one document. `q_gain`: positive entries. `k_gain`: positive entries.
All inputs are finite; a program needn't handle non-finite values.
Results may differ from the reference program's by a relative error of at most 0.011.
Values may be sent and summed in bfloat16 or wider, within the bound.
No kernel may reach another device: no remote copies, remote signals or barrier semaphores. Data moves between devices by JAX's collectives and lax.ppermute only.
A program may use at most 192 MiB of HBM per device.

```python
import jax
import jax.numpy as jnp
from jax import lax

D = 1024
HD = 64
FF = 4608
QW = 1024
KW = 512
BATCH = 4
LENGTH = 1024


def draw_positions(key, part):
    period = max(4, LENGTH // 8)
    breaks = jax.random.randint(key, (BATCH, LENGTH), 0, period) == 0
    index_row = jnp.arange(LENGTH, dtype=jnp.int32)
    later_rows = (jnp.arange(BATCH, dtype=jnp.int32) > 0)[:, None]
    starts = breaks & later_rows | (index_row == 0)[None, :]
    marked = jnp.where(starts, index_row[None, :], 0)
    return (index_row[None, :] - lax.cummax(marked, axis=1)).astype(jnp.int32)


def head_gain(key, salt_value):
    folded = jax.random.fold_in(key, salt_value)
    return jax.random.uniform(folded, (HD,), jnp.float32, 0.6, 1.4)


def draw_q_gain(key, part):
    return head_gain(key, 11)


def draw_k_gain(key, part):
    return head_gain(key, 23)


def with_spikes(entries, own_key, source, target, parts, factor):
    owner, partner = [(jnp.arange(entries.shape[dim]) // (entries.shape[dim] // parts)).reshape([-1 if axis == dim else 1 for axis in range(entries.ndim)]) for dim in (source, target)]
    chosen = jax.random.permutation(own_key, parts)[partner]
    strong = (owner == chosen) | (owner == (partner + parts // 2) % parts)
    return jnp.where(strong, factor * entries, entries)


def shard_levels(rng, extent, shards, low, top_value):
    def one(dim, shards_of):
        steps = jax.random.uniform(jax.random.fold_in(jax.random.fold_in(rng, 6), dim), (shards_of,), jnp.float32, low / len(shards), top_value / len(shards))
        return jnp.repeat(jnp.exp(steps), extent[dim] // shards_of).reshape((-1,) + (1,) * (len(extent) - dim - 1))

    loudness = one(*shards[0])
    for cut in shards[1:]:
        loudness = loudness * one(*cut)
    return loudness


def noise(rng, shape, scale, limit, split=(), kind=jnp.bfloat16):
    gain = shard_levels(rng, shape, split, -0.22, 0.18) if split else 1.0
    entries = jax.random.normal(rng, shape, jnp.float32) * scale * gain
    return jnp.minimum(jnp.maximum(entries, -limit), limit).astype(kind)


def heavy_noise(rng, extent, deviation, limit, split, heavy, kind=jnp.bfloat16):
    values = deviation * jax.random.normal(rng, extent, jnp.float32)
    if split:
        values = values * shard_levels(rng, extent, split, -0.22, 0.18)
    return jnp.clip(with_spikes(values, jax.random.fold_in(rng, 3), *heavy), -limit, limit).astype(kind)


def setup_inputs(seed: int = 0) -> dict:
    seeds = jax.random.split(jax.random.key(seed), 15)
    tokens = noise(seeds[0], (BATCH, LENGTH, D), 1.0, 6.0, ((0, 2), (1, 8)))
    positions = draw_positions(jax.random.fold_in(seeds[14], 71), 0)
    attn_gain = jnp.clip(1.0 + 0.1 * jax.random.normal(seeds[2], (D,), jnp.float32), 0.5, 1.5)
    ffn_gain = jnp.clip(1.0 + 0.1 * jax.random.normal(seeds[3], (D,), jnp.float32), 0.5, 1.5)
    q_gain = draw_q_gain(jax.random.fold_in(seeds[14], 71), 0)
    k_gain = draw_k_gain(jax.random.fold_in(seeds[14], 71), 0)
    w_query = noise(seeds[6], (D, QW), D ** -0.5, 0.1875, ((1, 2),))
    w_key = noise(seeds[7], (D, KW), D ** -0.5, 0.1875, ((1, 2),))
    w_value = noise(seeds[8], (D, KW), D ** -0.5, 0.1875, ((1, 2),))
    w_out = noise(seeds[9], (D, QW), 16 ** -0.5, 1.5, ((1, 2),))
    w_gate = noise(seeds[10], (D, FF), D ** -0.5, 0.1875, ((1, 2),))
    w_up = noise(seeds[11], (D, FF), D ** -0.5, 0.1875, ((1, 2),))
    w_down = noise(seeds[12], (D, FF), FF ** -0.5, 0.09375, ((1, 2),))
    cotangent = heavy_noise(seeds[13], (BATCH, LENGTH, D), 1.0, 6.0, ((0, 2), (1, 8)), (1, 2, 8, 2.0))
    return {"tokens": tokens, "positions": positions, "attn_gain": attn_gain, "ffn_gain": ffn_gain, "q_gain": q_gain, "k_gain": k_gain, "w_query": w_query, "w_key": w_key, "w_value": w_value, "w_out": w_out, "w_gate": w_gate, "w_up": w_up, "w_down": w_down, "cotangent": cotangent}


eps_norm = 1e-05
theta_base = 1000000.0
highest = lax.Precision.HIGHEST
negative = -1e+30

def rms_stat(values):
    return lax.rsqrt(lax.optimization_barrier(jnp.mean(values * values, axis=-1, keepdims=True)) + eps_norm)

def rms_back(grad_in, values, stat_val):
    return stat_val * grad_in - values * stat_val ** 3 * lax.optimization_barrier(jnp.mean(grad_in * values, axis=-1, keepdims=True))

def rope_tables(positions, head_dim):
    half_dim = head_dim // 2
    frequency = theta_base ** (-(jnp.arange(half_dim, dtype=jnp.float32) * 2.0) / head_dim)
    angles = positions.astype(jnp.float32)[..., None] * frequency
    return (jnp.cos(angles), jnp.sin(angles))

def rotate(values, cosine, sine_part):
    half_dim = values.shape[-1] // 2
    first_half = values[..., :half_dim]
    second_half = values[..., half_dim:]
    cos_full = cosine[..., None, :]
    sin_full = sine_part[..., None, :]
    return jnp.concatenate([first_half * cos_full - second_half * sin_full, second_half * cos_full + first_half * sin_full], axis=-1)

def unrotate(values, cosine, sine_part):
    half_dim = values.shape[-1] // 2
    first_half = values[..., :half_dim]
    second_half = values[..., half_dim:]
    cos_full = cosine[..., None, :]
    sin_full = sine_part[..., None, :]
    return jnp.concatenate([first_half * cos_full + second_half * sin_full, second_half * cos_full - first_half * sin_full], axis=-1)

def one_sequence(tokens, positions, cotangent, attn_gain, ffn_gain, q_gain, k_gain, w_query, w_key, w_value, w_out, w_gate, w_up, w_down):
    seq_len = tokens.shape[0]
    head_dim = q_gain.shape[0]
    q_heads = w_query.shape[1] // head_dim
    kv_heads = w_key.shape[1] // head_dim
    group_size = q_heads // kv_heads
    scale_factor = head_dim ** (-0.5)
    cosine, sine_part = rope_tables(positions, head_dim)
    flat_in = tokens.astype(jnp.float32)
    stat_one = rms_stat(flat_in)
    normed_one = (flat_in * stat_one * attn_gain).astype(jnp.bfloat16)
    query_raw = jnp.dot(normed_one, w_query, preferred_element_type=jnp.float32).reshape(seq_len, q_heads, head_dim)
    key_raw = jnp.dot(normed_one, w_key, preferred_element_type=jnp.float32).reshape(seq_len, kv_heads, head_dim)
    value_split = jnp.dot(normed_one, w_value, preferred_element_type=jnp.float32).astype(jnp.bfloat16).reshape(seq_len, kv_heads, head_dim)
    query_stat = rms_stat(query_raw)
    key_stat = rms_stat(key_raw)
    query_rot = rotate(query_raw * query_stat * q_gain, cosine, sine_part).astype(jnp.bfloat16)
    key_rot = rotate(key_raw * key_stat * k_gain, cosine, sine_part).astype(jnp.bfloat16)
    query_all = query_rot.reshape(seq_len, kv_heads, group_size, head_dim).astype(jnp.float32)
    key_all = key_rot.astype(jnp.float32)
    value_all = value_split.astype(jnp.float32)
    token_index = jnp.arange(seq_len, dtype=jnp.int32)
    lowest_key = token_index - positions
    block_len = min(512, seq_len)
    block_total = seq_len // block_len

    def block_scores(start_row):
        query_pos = start_row + jnp.arange(block_len, dtype=jnp.int32)
        lowest_pos = lax.dynamic_slice_in_dim(lowest_key, start_row, block_len, 0)
        allowed = (token_index[None, :] <= query_pos[:, None]) & (token_index[None, :] >= lowest_pos[:, None])
        allowed = allowed[None, None]
        query_block = lax.dynamic_slice_in_dim(query_all, start_row, block_len, 0)
        scores = jnp.einsum('qhgd,khd->hgqk', query_block, key_all, precision=highest) * scale_factor
        return (jnp.where(allowed, scores, negative), allowed, query_block)

    def forward_block(block_index):
        start_row = block_index * block_len
        scores, allowed, query_block = block_scores(start_row)
        top_score = lax.optimization_barrier(jnp.max(scores, axis=-1))
        weights = jnp.where(allowed, jnp.exp(scores - top_score[..., None]), 0.0)
        row_total = lax.optimization_barrier(jnp.sum(weights, axis=-1))
        summed = jnp.einsum('hgqk,khd->qhgd', weights, value_all, precision=highest)
        result = summed / jnp.transpose(row_total, (2, 0, 1))[..., None]
        return (result.astype(jnp.bfloat16), top_score + jnp.log(row_total))
    attended_blocks, lse_blocks = lax.map(forward_block, jnp.arange(block_total, dtype=jnp.int32))
    attended = attended_blocks.reshape(seq_len, q_heads * head_dim)
    log_sum = jnp.transpose(lse_blocks, (0, 3, 1, 2)).reshape(seq_len, kv_heads, group_size)
    mixed = flat_in + jnp.dot(attended, w_out.T, preferred_element_type=jnp.float32)
    stat_two = rms_stat(mixed)
    normed_two = (mixed * stat_two * ffn_gain).astype(jnp.bfloat16)
    gate_pre = jnp.dot(normed_two, w_gate, preferred_element_type=jnp.float32)
    up_pre = jnp.dot(normed_two, w_up, preferred_element_type=jnp.float32)
    sigmoid_val = jax.nn.sigmoid(gate_pre)
    silu_val = gate_pre * sigmoid_val
    hidden = (silu_val * up_pre).astype(jnp.bfloat16)
    layer_output = mixed + jnp.dot(hidden, w_down.T, preferred_element_type=jnp.float32)
    wdown_part = jnp.dot(cotangent.T, hidden, preferred_element_type=jnp.float32)
    grad_hidden = jnp.dot(cotangent, w_down, preferred_element_type=jnp.float32)
    dsilu = sigmoid_val * (1.0 + gate_pre * (1.0 - sigmoid_val))
    grad_gate_pre = (grad_hidden * up_pre * dsilu).astype(jnp.bfloat16)
    grad_up_pre = (grad_hidden * silu_val).astype(jnp.bfloat16)
    wgate_part = jnp.dot(normed_two.T, grad_gate_pre, preferred_element_type=jnp.float32)
    wup_part = jnp.dot(normed_two.T, grad_up_pre, preferred_element_type=jnp.float32)
    grad_normed_two = jnp.dot(grad_gate_pre, w_gate.T, preferred_element_type=jnp.float32) + jnp.dot(grad_up_pre, w_up.T, preferred_element_type=jnp.float32)
    ffngain_part = lax.optimization_barrier(jnp.sum(grad_normed_two * mixed * stat_two, axis=0))
    grad_mixed = cotangent.astype(jnp.float32) + rms_back(grad_normed_two * ffn_gain, mixed, stat_two)
    grad_mixed_bf = grad_mixed.astype(jnp.bfloat16)
    wout_part = jnp.dot(grad_mixed_bf.T, attended, preferred_element_type=jnp.float32)
    grad_attended = jnp.dot(grad_mixed_bf, w_out, preferred_element_type=jnp.float32).astype(jnp.bfloat16)
    grad_all = grad_attended.reshape(seq_len, kv_heads, group_size, head_dim).astype(jnp.float32)
    attended_all = attended.reshape(seq_len, kv_heads, group_size, head_dim).astype(jnp.float32)
    delta_stat = lax.optimization_barrier(jnp.sum(grad_all * attended_all, axis=-1))

    def backward_block(carry_pair, block_index):
        key_acc, value_acc = carry_pair
        start_row = block_index * block_len
        scores, allowed, query_block = block_scores(start_row)
        lse_block = jnp.transpose(lax.dynamic_slice_in_dim(log_sum, start_row, block_len, 0), (1, 2, 0))
        delta_block = jnp.transpose(lax.dynamic_slice_in_dim(delta_stat, start_row, block_len, 0), (1, 2, 0))
        grad_block = lax.dynamic_slice_in_dim(grad_all, start_row, block_len, 0)
        probs = jnp.where(allowed, jnp.exp(scores - lse_block[..., None]), 0.0)
        grad_probs = jnp.einsum('qhgd,khd->hgqk', grad_block, value_all, precision=highest)
        grad_scores = probs * (grad_probs - delta_block[..., None])
        query_grad = jnp.einsum('hgqk,khd->qhgd', grad_scores, key_all, precision=highest) * scale_factor
        key_acc = key_acc + jnp.einsum('hgqk,qhgd->khd', grad_scores, query_block, precision=highest) * scale_factor
        value_acc = value_acc + jnp.einsum('hgqk,qhgd->khd', probs, grad_block, precision=highest)
        return ((key_acc, value_acc), query_grad)
    zero_keys = jnp.zeros((seq_len, kv_heads, head_dim), jnp.float32)
    (key_grad_rot, value_grad), query_blocks = lax.scan(backward_block, (zero_keys, zero_keys), jnp.arange(block_total, dtype=jnp.int32))
    query_grad_rot = query_blocks.reshape(seq_len, q_heads, head_dim)
    grad_query_norm = unrotate(query_grad_rot, cosine, sine_part)
    grad_key_norm = unrotate(key_grad_rot, cosine, sine_part)
    qgain_part = lax.optimization_barrier(jnp.sum(grad_query_norm * query_raw * query_stat, axis=(0, 1)))
    kgain_part = lax.optimization_barrier(jnp.sum(grad_key_norm * key_raw * key_stat, axis=(0, 1)))
    grad_query_raw = rms_back(grad_query_norm * q_gain, query_raw, query_stat).astype(jnp.bfloat16).reshape(seq_len, q_heads * head_dim)
    grad_key_raw = rms_back(grad_key_norm * k_gain, key_raw, key_stat).astype(jnp.bfloat16).reshape(seq_len, kv_heads * head_dim)
    grad_value_raw = value_grad.astype(jnp.bfloat16).reshape(seq_len, kv_heads * head_dim)
    wq_part = jnp.dot(normed_one.T, grad_query_raw, preferred_element_type=jnp.float32)
    wk_part = jnp.dot(normed_one.T, grad_key_raw, preferred_element_type=jnp.float32)
    wv_part = jnp.dot(normed_one.T, grad_value_raw, preferred_element_type=jnp.float32)
    grad_normed_one = jnp.dot(grad_query_raw, w_query.T, preferred_element_type=jnp.float32)
    grad_normed_one = grad_normed_one + jnp.dot(grad_key_raw, w_key.T, preferred_element_type=jnp.float32)
    grad_normed_one = grad_normed_one + jnp.dot(grad_value_raw, w_value.T, preferred_element_type=jnp.float32)
    attngain_part = lax.optimization_barrier(jnp.sum(grad_normed_one * flat_in * stat_one, axis=0))
    input_grad = grad_mixed + rms_back(grad_normed_one * attn_gain, flat_in, stat_one)
    parts_all = (wq_part, wk_part, wv_part, wout_part, wgate_part, wup_part, wdown_part, attngain_part, ffngain_part, qgain_part, kgain_part)
    return (layer_output, input_grad, parts_all)

def reference(tokens, positions, attn_gain, ffn_gain, q_gain, k_gain, w_query, w_key, w_value, w_out, w_gate, w_up, w_down, cotangent):

    def sequence_step(carry_sum, inputs_one):
        tok_seq, pos_seq, cot_seq = inputs_one
        out_seq, grad_seq, parts_all = one_sequence(tok_seq, pos_seq, cot_seq, attn_gain, ffn_gain, q_gain, k_gain, w_query, w_key, w_value, w_out, w_gate, w_up, w_down)
        return (jax.tree.map(jnp.add, carry_sum, parts_all), (out_seq, grad_seq))
    start_sum = (jnp.zeros(w_query.shape, jnp.float32), jnp.zeros(w_key.shape, jnp.float32), jnp.zeros(w_value.shape, jnp.float32), jnp.zeros(w_out.shape, jnp.float32), jnp.zeros(w_gate.shape, jnp.float32), jnp.zeros(w_up.shape, jnp.float32), jnp.zeros(w_down.shape, jnp.float32), jnp.zeros(attn_gain.shape, jnp.float32), jnp.zeros(ffn_gain.shape, jnp.float32), jnp.zeros(q_gain.shape, jnp.float32), jnp.zeros(k_gain.shape, jnp.float32))
    totals, stacked = lax.scan(sequence_step, start_sum, (tokens, positions, cotangent))
    layer_output, input_grad = stacked
    wq_total, wk_total, wv_total, wo_total, wgate_total, wup_total, wdown_total, attngain_total, ffngain_total, qgain_total, kgain_total = totals
    return (layer_output, input_grad, wq_total, wk_total, wv_total, wo_total, wgate_total, wup_total, wdown_total, attngain_total, ffngain_total, qgain_total, kgain_total)
```

```python
import functools

import jax
import jax.numpy as jnp
from jax import lax
from jax.experimental import pallas as pl
from jax.experimental.pallas import tpu as pltpu
from jax.sharding import PartitionSpec as P


eps_norm = 1e-05
theta_base = 1000000.0
negative = -1e30
bf16 = jnp.bfloat16
f32 = jnp.float32
lanes = 128
pos_base = 128
pos_rows = 16


def dot_f32(lhs, rhs, lhs_dim, rhs_dim):
    return lax.dot_general(
        lhs, rhs, (((lhs_dim,), (rhs_dim,)), ((), ())), preferred_element_type=f32
    )


def rms_stat(values):
    return lax.rsqrt(jnp.mean(values * values, axis=-1, keepdims=True) + eps_norm)


def rms_back(grad_in, values, stat_val):
    return stat_val * grad_in - values * stat_val**3 * jnp.mean(
        grad_in * values, axis=-1, keepdims=True
    )


def rope_tables(positions, head_dim):
    half_dim = head_dim // 2
    frequency = theta_base ** (-(jnp.arange(half_dim, dtype=f32) * 2.0) / head_dim)
    angles = positions.astype(f32)[..., None] * frequency
    return (jnp.cos(angles), jnp.sin(angles))


def rotate(values, cosine, sine_part):
    half_dim = values.shape[-1] // 2
    first_half = values[..., :half_dim]
    second_half = values[..., half_dim:]
    cos_full = cosine[..., None, :]
    sin_full = sine_part[..., None, :]
    return jnp.concatenate(
        [
            first_half * cos_full - second_half * sin_full,
            second_half * cos_full + first_half * sin_full,
        ],
        axis=-1,
    )


def xor_swap(value, axis, flip):
    size = lax.axis_size(axis)
    return lax.ppermute(value, axis, [(index, index ^ flip) for index in range(size)])


def tp_sum(part):
    sent = lax.reduce_precision(part, 8, 7)
    other = xor_swap(sent.astype(bf16), "tp", 1)
    return sent + other.astype(f32)


def pick(value, index, axis=0):
    return lax.dynamic_index_in_dim(value, index, axis, keepdims=False)


def xor_order(stacked, index):
    count = stacked.shape[0]
    rest = stacked.shape[1:]
    bits = count.bit_length() - 1
    shaped = stacked.reshape((2,) * bits + rest)
    for bit in range(bits):
        axis = bits - 1 - bit
        shaped = jnp.where((index >> bit) & 1 == 1, jnp.flip(shaped, axis), shaped)
    return shaped.reshape(stacked.shape)


def ctx_exchange(blocks):
    count = blocks.shape[0]
    here = lax.axis_index("ctx")
    found = [pick(blocks, here)] + [None] * (count - 1)
    for flip in range(count - 1, 0, -1):
        found[flip] = xor_swap(pick(blocks, here ^ flip), "ctx", flip)
    return found


def head_masked(scores, low_row, query_start, key_count):
    query_count = scores.shape[1]
    key_index = lax.broadcasted_iota(jnp.int32, scores.shape, 0)
    query_index = query_start + lax.broadcasted_iota(jnp.int32, scores.shape, 1)
    return (key_index <= query_index) & (key_index >= low_row)


def gather_blocks(order_ref, block_refs, query_buf, key_buf, value_buf, low_buf):
    block_len = block_refs[0].shape[0] - pos_rows
    head_dim = key_buf.shape[1]
    query_width = query_buf.shape[1]
    for flip, block_ref in enumerate(block_refs):
        place = order_ref[flip]
        row_start = pl.multiple_of(place * block_len, block_len)
        rows = pl.ds(row_start, block_len)
        query_buf[rows, :] = block_ref[:block_len, :query_width]
        key_buf[rows, :] = block_ref[:block_len, query_width : query_width + head_dim]
        value_buf[rows, :] = block_ref[:block_len, query_width + head_dim :]
        tail = block_ref[block_len:, :].astype(f32)
        found = tail[:1, :block_len] * pos_base + tail[:1, block_len : 2 * block_len]
        token = row_start + lax.broadcasted_iota(jnp.int32, (1, block_len), 1)
        low_buf[place, :, :] = token - found.astype(jnp.int32)


def attend_kernel(count, *refs):
    order_ref = refs[0]
    block_refs = refs[1 : 1 + count]
    out_ref, lse_ref, query_buf, key_buf, value_buf, low_buf = refs[1 + count :]
    gather_blocks(order_ref, block_refs, query_buf, key_buf, value_buf, low_buf)
    total, head_dim = key_buf.shape
    block_len = total // count
    group = query_buf.shape[1] // head_dim
    tile = min(256, total)
    per_tile = tile // block_len
    for start in range(0, total, tile):
        key_count = start + tile
        low_row = jnp.concatenate(
            [low_buf[start // block_len + n] for n in range(per_tile)], axis=1
        )
        keys = key_buf[:key_count, :]
        vals = value_buf[:key_count, :]
        turned = []
        for head in range(group):
            query = query_buf[start : start + tile, head * head_dim : (head + 1) * head_dim]
            scores = dot_f32(keys, query, 1, 1) * head_dim ** (-0.5)
            allowed = head_masked(scores, low_row, start, key_count)
            scores = jnp.where(allowed, scores, negative)
            top = jnp.max(scores, axis=0, keepdims=True)
            weights = jnp.exp(scores - top)
            row_sum = jnp.sum(weights, axis=0, keepdims=True)
            lse_ref[head : head + 1, start : start + tile] = top + jnp.log(row_sum)
            turned.append(dot_f32(vals, weights.astype(bf16), 0, 0) / row_sum)
        merged = jnp.concatenate(turned, axis=0).T.astype(bf16)
        for n in range(per_tile):
            out_ref[start // block_len + n] = merged[n * block_len : (n + 1) * block_len]


def attend_back_kernel(count, *refs):
    order_ref = refs[0]
    block_refs = refs[1 : 1 + count]
    grad_refs = refs[1 + count : 1 + 2 * count]
    (out_ref, lse_ref, packed_ref, query_buf, key_buf, value_buf, low_buf, grad_buf, key_acc, value_acc) = refs[
        1 + 2 * count :
    ]
    gather_blocks(order_ref, block_refs, query_buf, key_buf, value_buf, low_buf)
    total, head_dim = key_buf.shape
    block_len = total // count
    group = query_buf.shape[1] // head_dim
    for flip, grad_ref in enumerate(grad_refs):
        row_start = pl.multiple_of(order_ref[flip] * block_len, block_len)
        grad_buf[pl.ds(row_start, block_len), :] = grad_ref[...]
    key_acc[...] = jnp.zeros_like(key_acc)
    value_acc[...] = jnp.zeros_like(value_acc)
    tile = min(256, total)
    per_tile = tile // block_len
    scale = head_dim ** (-0.5)
    ones_row = jnp.ones((8, head_dim), f32)
    for start in range(0, total, tile):
        key_count = start + tile
        first_block = start // block_len
        low_row = jnp.concatenate([low_buf[first_block + n] for n in range(per_tile)], axis=1)
        keys = key_buf[:key_count, :]
        vals = value_buf[:key_count, :]
        turned = []
        for head in range(group):
            cols = slice(head * head_dim, (head + 1) * head_dim)
            query = query_buf[start : start + tile, cols]
            grad = grad_buf[start : start + tile, cols]
            out = jnp.concatenate([out_ref[first_block + n] for n in range(per_tile)], axis=0)[:, cols]
            product = grad.astype(f32) * out.astype(f32)
            delta = lax.dot_general(
                ones_row,
                product,
                (((1,), (1,)), ((), ())),
                precision=lax.Precision.HIGHEST,
                preferred_element_type=f32,
            )[:1, :]
            scores = dot_f32(keys, query, 1, 1) * scale
            allowed = head_masked(scores, low_row, start, key_count)
            lse_row = lse_ref[head : head + 1, start : start + tile]
            probs = jnp.where(allowed, jnp.exp(scores - lse_row), 0.0)
            grad_scores = (probs * (dot_f32(vals, grad, 1, 1) - delta)).astype(bf16)
            value_acc[:key_count, :] += dot_f32(probs.astype(bf16), grad, 1, 0)
            key_acc[:key_count, :] += dot_f32(grad_scores, query, 1, 0)
            turned.append(dot_f32(keys, grad_scores, 0, 0) * scale)
        merged = jnp.concatenate(turned, axis=0).T.astype(bf16)
        for n in range(per_tile):
            packed_ref[first_block + n, :, : group * head_dim] = merged[
                n * block_len : (n + 1) * block_len
            ]
    for n in range(count):
        rows = slice(n * block_len, (n + 1) * block_len)
        both = jnp.concatenate([key_acc[rows, :] * scale, value_acc[rows, :]], axis=1)
        packed_ref[n, :, group * head_dim :] = both.astype(bf16)


def smem_spec():
    return pl.BlockSpec(memory_space=pltpu.SMEM)


def vmem_spec():
    return pl.BlockSpec(memory_space=pltpu.VMEM)


def head_forward(order, blocks, head_dim, group):
    count = len(blocks)
    block_len = blocks[0].shape[0] - pos_rows
    total = count * block_len
    return pl.pallas_call(
        functools.partial(attend_kernel, count),
        out_shape=(
            jax.ShapeDtypeStruct((count, block_len, group * head_dim), bf16),
            jax.ShapeDtypeStruct((group, total), f32),
        ),
        in_specs=[smem_spec()] + [vmem_spec()] * count,
        out_specs=(vmem_spec(), vmem_spec()),
        scratch_shapes=[
            pltpu.VMEM((total, group * head_dim), bf16),
            pltpu.VMEM((total, head_dim), bf16),
            pltpu.VMEM((total, head_dim), bf16),
            pltpu.VMEM((count, 1, block_len), jnp.int32),
        ],
        cost_estimate=pl.CostEstimate(
            flops=4 * total * total * head_dim * group,
            bytes_accessed=2 * total * 512,
            transcendentals=total * total * group,
        ),
        name="attend",
    )(order, *blocks)


def head_backward(order, blocks, grads, out, log_sum, head_dim, group):
    count = len(blocks)
    block_len = grads[0].shape[0]
    total = count * block_len
    return pl.pallas_call(
        functools.partial(attend_back_kernel, count),
        out_shape=jax.ShapeDtypeStruct((count, block_len, (group + 2) * head_dim), bf16),
        in_specs=[smem_spec()] + [vmem_spec()] * (2 * count + 2),
        out_specs=vmem_spec(),
        scratch_shapes=[
            pltpu.VMEM((total, group * head_dim), bf16),
            pltpu.VMEM((total, head_dim), bf16),
            pltpu.VMEM((total, head_dim), bf16),
            pltpu.VMEM((count, 1, block_len), jnp.int32),
            pltpu.VMEM((total, group * head_dim), bf16),
            pltpu.VMEM((total, head_dim), f32),
            pltpu.VMEM((total, head_dim), f32),
        ],
        cost_estimate=pl.CostEstimate(
            flops=10 * total * total * head_dim * group,
            bytes_accessed=2 * total * 1024,
            transcendentals=total * total * group,
        ),
        name="attend_back",
    )(order, *blocks, *grads, out, log_sum)


def gathered_scores(query_grouped, key_piece, query_pos, lowest_pos, key_pos):
    head_dim = query_grouped.shape[-1]
    keys_split = key_piece.reshape(
        key_piece.shape[0], key_piece.shape[1], query_grouped.shape[2], head_dim
    )
    scores = jnp.einsum(
        "sqhgd,skhd->shgqk", query_grouped, keys_split, preferred_element_type=f32
    ) * head_dim ** (-0.5)
    allowed = (key_pos[None, None, :] <= query_pos[None, :, None]) & (
        key_pos[None, None, :] >= lowest_pos[:, :, None]
    )
    allowed = allowed[:, None, None, :, :]
    return (jnp.where(allowed, scores, negative), allowed, keys_split)


def gathered_forward(query_grouped, key_rows, value_rows, query_index, lowest_key):
    key_all = lax.all_gather(key_rows, "ctx", axis=1, tiled=True)
    value_all = lax.all_gather(value_rows, "ctx", axis=1, tiled=True)
    key_pos = jnp.arange(key_all.shape[1], dtype=jnp.int32)
    scores, allowed, keys_split = gathered_scores(
        query_grouped, key_all, query_index, lowest_key, key_pos
    )
    top = jnp.max(scores, axis=-1)
    weights = jnp.where(allowed, jnp.exp(scores - top[..., None]), 0.0)
    row_sum = jnp.sum(weights, axis=-1)
    summed = jnp.einsum(
        "shgqk,skhd->shgqd",
        weights.astype(bf16),
        value_all.reshape(keys_split.shape),
        preferred_element_type=f32,
    )
    attended = (summed / row_sum[..., None]).astype(bf16)
    return (jnp.transpose(attended, (0, 3, 1, 2, 4)), top + jnp.log(row_sum), key_all, value_all)


def gathered_backward(
    query_grouped, grad_grouped, attended, log_sum, key_all, value_all, query_index, lowest_key
):
    scale = query_grouped.shape[-1] ** (-0.5)
    key_pos = jnp.arange(key_all.shape[1], dtype=jnp.int32)
    delta_rows = jnp.sum(grad_grouped.astype(f32) * attended.astype(f32), axis=-1)
    delta_stat = jnp.transpose(delta_rows, (0, 2, 3, 1))
    scores, allowed, keys_split = gathered_scores(
        query_grouped, key_all, query_index, lowest_key, key_pos
    )
    probs = jnp.where(allowed, jnp.exp(scores - log_sum[..., None]), 0.0)
    grad_probs = jnp.einsum(
        "sqhgd,skhd->shgqk",
        grad_grouped,
        value_all.reshape(keys_split.shape),
        preferred_element_type=f32,
    )
    grad_scores = (probs * (grad_probs - delta_stat[..., None])).astype(bf16)
    query_grad = (
        jnp.einsum("shgqk,skhd->sqhgd", grad_scores, keys_split, preferred_element_type=f32) * scale
    )
    key_grad = (
        jnp.einsum("shgqk,sqhgd->skhd", grad_scores, query_grouped, preferred_element_type=f32)
        * scale
    )
    value_grad = jnp.einsum(
        "shgqk,sqhgd->skhd", probs.astype(bf16), grad_grouped, preferred_element_type=f32
    )
    key_own, value_own = (
        lax.psum_scatter(part.reshape(key_all.shape), "ctx", scatter_dimension=1, tiled=True)
        for part in (key_grad, value_grad)
    )
    return (query_grad, key_own, value_own)


everywhere = ("ctx", "seq")
plane = 4


def plane_gather(rows, core):
    half = rows.shape[0] // 2
    mine = lax.dynamic_slice_in_dim(rows, core * half, half, 0)
    found = jnp.stack([xor_swap(mine, everywhere, flip) for flip in range(1, plane)])
    other = xor_swap(found, "tp", 1)
    first = jnp.where(core == 0, found, other)
    second = jnp.where(core == 0, other, found)
    rest = jnp.concatenate([first, second], axis=1).reshape((plane - 1) * rows.shape[0], -1)
    return jnp.concatenate([rows, rest], axis=0)


def window(cols):
    half = cols // 2
    width = min(half, -(-half // (2 * lanes)) * lanes)
    return (half, width)


def plane_exchange(value, place, start_of, width):
    own = lax.dynamic_slice_in_dim(value, start_of(place), width, 1)
    parts = [own]
    for flip in range(1, plane):
        sent = lax.dynamic_slice_in_dim(value, start_of(place ^ flip), width, 1)
        parts.append(xor_swap(sent, everywhere, flip))
    return jnp.concatenate(parts, axis=0)


def halve_rows(row_factor, col_factor, index, total, extra=None):
    bits = (total // plane).bit_length() - 1
    tokens_count, row_count = row_factor.shape
    block_index = index // plane
    width = col_factor.shape[1]
    low = block_index & 1
    parts = row_factor.reshape(tokens_count, (total // plane) // 2, 2, row_count * plane // total)
    kept_rows = pick(parts, low, 2).reshape(tokens_count, row_count // 2)
    sent_rows = pick(parts, 1 - low, 2).reshape(tokens_count, row_count // 2)
    sent = dot_f32(sent_rows, col_factor, 0, 0)
    kept = dot_f32(kept_rows, col_factor, 0, 0)
    if extra is not None:
        shaped = extra.reshape((total // plane) // 2, 2, row_count * plane // total, -1)
        sent = jnp.concatenate(
            [sent, pick(shaped, 1 - low, 1).reshape(row_count // 2, -1)], axis=1
        )
        kept = jnp.concatenate([kept, pick(shaped, low, 1).reshape(row_count // 2, -1)], axis=1)
    width = kept.shape[1]
    kept = kept + xor_swap(sent.astype(bf16), everywhere, plane).astype(f32)
    for bit in range(1, bits):
        own_bit = (block_index >> bit) & 1
        shaped = kept.reshape((total // plane) >> (bit + 1), 2, -1, width)
        sent = pick(shaped, 1 - own_bit, 1).reshape(-1, width).astype(bf16)
        kept = pick(shaped, own_bit, 1).reshape(-1, width)
        kept = kept + xor_swap(sent, everywhere, plane << bit).astype(f32)
    return kept


def return_rows(summed, place):
    width = summed.shape[1]
    shaped = summed.reshape(plane, -1, width)
    found = [pick(shaped, place)]
    for flip in range(1, plane):
        sent = pick(shaped, place ^ flip).astype(bf16)
        found.append(xor_swap(sent, everywhere, flip).astype(f32))
    return xor_order(jnp.stack(found), place)


def shards(
    tokens,
    positions,
    attn_gain,
    ffn_gain,
    q_gain,
    k_gain,
    w_query,
    w_key,
    w_value,
    w_out,
    w_gate,
    w_up,
    w_down,
    cotangent,
):
    seq_count, block_len, model_width = tokens.shape
    row_count = seq_count * block_len
    head_dim = q_gain.shape[0]
    q_heads = w_query.shape[1] // head_dim
    kv_heads = w_key.shape[1] // head_dim
    key_width = kv_heads * head_dim
    query_width = q_heads * head_dim
    group_size = q_heads // kv_heads
    hidden_width = w_gate.shape[1]
    ctx_size = lax.axis_size("ctx")
    total = ctx_size * lax.axis_size("seq")
    here_index = lax.axis_index("ctx")
    index = lax.axis_index(everywhere)
    core = lax.axis_index("tp")
    place = index % plane
    by_head = ctx_size == seq_count * kv_heads

    cot_rows = cotangent.reshape(row_count, model_width)
    cot_plane = plane_gather(cot_rows, core)

    cosine, sine_part = rope_tables(positions, head_dim)
    flat_in = tokens.reshape(row_count, model_width).astype(f32)
    stat_one = rms_stat(flat_in)
    normed_one = (flat_in * stat_one * attn_gain).astype(bf16)
    query_raw = jnp.dot(normed_one, w_query, preferred_element_type=f32).reshape(
        seq_count, block_len, q_heads, head_dim
    )
    key_raw = jnp.dot(normed_one, w_key, preferred_element_type=f32).reshape(
        seq_count, block_len, kv_heads, head_dim
    )
    value_rows = (
        jnp.dot(normed_one, w_value, preferred_element_type=f32)
        .astype(bf16)
        .reshape(seq_count, block_len, key_width)
    )
    query_stat = rms_stat(query_raw)
    key_stat = rms_stat(key_raw)
    query_rot = rotate(query_raw * query_stat * q_gain, cosine, sine_part).astype(bf16)
    key_rot = rotate(key_raw * key_stat * k_gain, cosine, sine_part).astype(bf16)

    if by_head:
        packed = jnp.concatenate(
            [
                query_rot.reshape(seq_count, block_len, kv_heads, group_size * head_dim),
                key_rot,
                value_rows.reshape(seq_count, block_len, kv_heads, head_dim),
            ],
            axis=-1,
        )
        pack_width = packed.shape[-1]
        packed = jnp.transpose(packed, (0, 2, 1, 3))
        pos_row = jnp.concatenate([positions // pos_base, positions % pos_base], axis=1)
        pos_row = jnp.pad(
            pos_row.astype(bf16)[:, None, None, :],
            ((0, 0), (0, 0), (0, pos_rows - 1), (0, pack_width - 2 * block_len)),
        )
        pos_row = jnp.broadcast_to(pos_row, (seq_count, kv_heads, pos_rows, pack_width))
        packed = jnp.concatenate([packed, pos_row], axis=2)
        blocks = ctx_exchange(packed.reshape(ctx_size, block_len + pos_rows, pack_width))
        order = here_index ^ jnp.arange(ctx_size, dtype=jnp.int32)
        out_heads, log_sum = head_forward(order, blocks, head_dim, group_size)
        attended = xor_order(jnp.stack(ctx_exchange(out_heads)), here_index)
        attended = jnp.transpose(
            attended.reshape(seq_count, kv_heads, block_len, group_size * head_dim), (0, 2, 1, 3)
        ).reshape(row_count, query_width)
    else:
        query_index = here_index * block_len + jnp.arange(block_len, dtype=jnp.int32)
        lowest_key = query_index[None, :] - positions
        query_grouped = query_rot.reshape(seq_count, block_len, kv_heads, group_size, head_dim)
        attended_grouped, log_sum, key_all, value_all = gathered_forward(
            query_grouped,
            key_rot.reshape(seq_count, block_len, key_width),
            value_rows,
            query_index,
            lowest_key,
        )
        attended = attended_grouped.reshape(row_count, query_width)

    one_plane = plane_gather(normed_one, core)
    mixed = flat_in + tp_sum(dot_f32(attended, w_out, 1, 1))
    stat_two = rms_stat(mixed)
    normed_two = (mixed * stat_two * ffn_gain).astype(bf16)
    two_plane = plane_gather(normed_two, core)
    gate_pre = jnp.dot(normed_two, w_gate, preferred_element_type=f32)
    up_pre = jnp.dot(normed_two, w_up, preferred_element_type=f32)
    sigmoid_val = jax.nn.sigmoid(gate_pre)
    silu_val = gate_pre * sigmoid_val
    hidden = (silu_val * up_pre).astype(bf16)

    half, width = window(hidden_width)

    def hidden_start(member):
        return (member % 2) * half + (member // 2) * (half - width)

    hidden_plane = plane_exchange(hidden, place, hidden_start, width)
    grad_hidden = jnp.dot(cot_rows, w_down, preferred_element_type=f32)
    dsilu = sigmoid_val * (1.0 + gate_pre * (1.0 - sigmoid_val))
    grad_gate_pre = (grad_hidden * up_pre * dsilu).astype(bf16)
    grad_up_pre = (grad_hidden * silu_val).astype(bf16)
    both_pre = jnp.concatenate([grad_gate_pre, grad_up_pre], axis=1)

    def both_start(member):
        return (member % 2) * hidden_width + (member // 2) * half

    both_plane = plane_exchange(both_pre, place, both_start, half)

    layer_output = mixed + tp_sum(dot_f32(hidden, w_down, 1, 1))
    grad_normed_two = tp_sum(
        dot_f32(grad_gate_pre, w_gate, 1, 1) + dot_f32(grad_up_pre, w_up, 1, 1)
    )

    down_sum = halve_rows(cot_plane, hidden_plane, index, total)
    down_rows = return_rows(down_sum, place)
    wdown_grad = jnp.concatenate(
        [
            piece
            for side in range(2)
            for piece in (down_rows[side], down_rows[2 + side][:, 2 * width - half :])
        ],
        axis=1,
    )
    both_sum = halve_rows(two_plane, both_plane, index, total)
    both_rows = return_rows(both_sum, place)
    wgate_grad = jnp.concatenate([both_rows[0], both_rows[2]], axis=1)
    wup_grad = jnp.concatenate([both_rows[1], both_rows[3]], axis=1)

    ffn_product = grad_normed_two * mixed * stat_two
    grad_mixed = cot_rows.astype(f32) + rms_back(grad_normed_two * ffn_gain, mixed, stat_two)
    grad_mixed_bf = grad_mixed.astype(bf16)
    mixed_plane = plane_gather(grad_mixed_bf, core)
    out_width = query_width // plane
    attended_plane = plane_exchange(
        attended, place, lambda member: member * out_width, out_width
    )
    grad_attended = jnp.dot(grad_mixed_bf, w_out, preferred_element_type=f32).astype(bf16)

    if by_head:
        grad_blocks = jnp.transpose(
            grad_attended.reshape(seq_count, block_len, kv_heads, group_size * head_dim),
            (0, 2, 1, 3),
        ).reshape(ctx_size, block_len, group_size * head_dim)
        grads = ctx_exchange(grad_blocks)
        packed_grads = head_backward(
            order, blocks, grads, out_heads, log_sum, head_dim, group_size
        )
        returned = xor_order(jnp.stack(ctx_exchange(packed_grads)), here_index)
        returned = jnp.transpose(
            returned.reshape(seq_count, kv_heads, block_len, -1), (0, 2, 1, 3)
        )
        query_grad_rot = returned[..., : group_size * head_dim].reshape(query_raw.shape).astype(f32)
        key_grad_rot = returned[..., group_size * head_dim : (group_size + 1) * head_dim].astype(f32)
        grad_value_raw = returned[..., (group_size + 1) * head_dim :].reshape(row_count, key_width)
    else:
        query_grad, key_grad_own, value_grad_own = gathered_backward(
            query_grouped,
            grad_attended.reshape(query_grouped.shape),
            attended_grouped,
            log_sum,
            key_all,
            value_all,
            query_index,
            lowest_key,
        )
        query_grad_rot = query_grad.reshape(query_raw.shape)
        key_grad_rot = key_grad_own.reshape(key_raw.shape)
        grad_value_raw = value_grad_own.astype(bf16).reshape(row_count, key_width)

    grad_query_norm = rotate(query_grad_rot, cosine, -sine_part)
    grad_key_norm = rotate(key_grad_rot, cosine, -sine_part)
    qgain_part = jnp.sum(grad_query_norm * query_raw * query_stat, axis=(0, 1, 2))
    kgain_part = jnp.sum(grad_key_norm * key_raw * key_stat, axis=(0, 1, 2))
    grad_query_raw = (
        rms_back(grad_query_norm * q_gain, query_raw, query_stat)
        .astype(bf16)
        .reshape(row_count, query_width)
    )
    grad_key_raw = (
        rms_back(grad_key_norm * k_gain, key_raw, key_stat)
        .astype(bf16)
        .reshape(row_count, key_width)
    )
    grad_raw = jnp.concatenate([grad_query_raw, grad_key_raw, grad_value_raw], axis=1)
    raw_width = grad_raw.shape[1] // plane
    raw_plane = plane_exchange(grad_raw, place, lambda member: member * raw_width, raw_width)
    grad_normed_one = tp_sum(
        dot_f32(grad_query_raw, w_query, 1, 1)
        + dot_f32(grad_key_raw, w_key, 1, 1)
        + dot_f32(grad_value_raw, w_value, 1, 1)
    )
    attn_product = grad_normed_one * flat_in * stat_one
    input_grad = grad_mixed + rms_back(grad_normed_one * attn_gain, flat_in, stat_one)

    out_sum = halve_rows(mixed_plane, attended_plane, index, total)
    ffn_col = jnp.sum(ffn_product, axis=0)[:, None]
    attn_col = jnp.sum(attn_product, axis=0)[:, None]
    tiles = model_width // head_dim
    gain_cols = jnp.concatenate(
        [
            ffn_col,
            attn_col,
            jnp.tile(qgain_part, tiles)[:, None],
            jnp.tile(kgain_part, tiles)[:, None],
            jnp.zeros((model_width, lanes - 4), f32),
        ],
        axis=1,
    )
    raw_sum = halve_rows(one_plane, raw_plane, index, total, gain_cols)
    late_rows = return_rows(jnp.concatenate([out_sum, raw_sum], axis=1), place)

    def assemble(start, width_now):
        return jnp.concatenate(
            [late_rows[member][:, start : start + width_now] for member in range(plane)], axis=1
        )

    wo_grad = assemble(0, out_width)
    raw_grad = assemble(out_width, raw_width)
    wq_grad = raw_grad[:, :query_width]
    wk_grad = raw_grad[:, query_width : query_width + key_width]
    wv_grad = raw_grad[:, query_width + key_width :]
    gain_sums = jnp.sum(late_rows[:, :, out_width + raw_width :], axis=0)
    ffngain_grad = gain_sums[:, 0]
    attngain_grad = gain_sums[:, 1]
    per_block = gain_sums.shape[0]
    head_gains = lax.reduce_precision(gain_sums[:, 2:4], 8, 23)
    head_gains = head_gains + xor_swap(head_gains, "tp", 1)
    if per_block < head_dim:
        whole_gains = lax.all_gather(head_gains, everywhere, axis=0, tiled=True)[:head_dim]
    else:
        whole_gains = head_gains[:head_dim]
    return (
        layer_output.reshape(seq_count, block_len, model_width),
        input_grad.reshape(seq_count, block_len, model_width),
        wq_grad,
        wk_grad,
        wv_grad,
        wo_grad,
        wgate_grad,
        wup_grad,
        wdown_grad,
        attngain_grad,
        ffngain_grad,
        whole_gains[:, 0],
        whole_gains[:, 1],
    )


def solution(mesh):
    placed = (
        P("seq", "ctx", None),
        P("seq", "ctx"),
        P(),
        P(),
        P(),
        P(),
        P(None, "tp"),
        P(None, "tp"),
        P(None, "tp"),
        P(None, "tp"),
        P(None, "tp"),
        P(None, "tp"),
        P(None, "tp"),
        P("seq", "ctx", None),
    )
    return jax.shard_map(
        shards,
        mesh=mesh,
        in_specs=placed,
        out_specs=(
            P("seq", "ctx", None),
            P("seq", "ctx", None),
            P(("ctx", "seq"), "tp"),
            P(("ctx", "seq"), "tp"),
            P(("ctx", "seq"), "tp"),
            P(("ctx", "seq"), "tp"),
            P(("ctx", "seq"), "tp"),
            P(("ctx", "seq"), "tp"),
            P(("ctx", "seq"), "tp"),
            P(("ctx", "seq")),
            P(("ctx", "seq")),
            P(),
            P(),
        ),
        check_vma=False,
    )
```

```python
import functools

import jax
import jax.numpy as jnp
from jax import lax
from jax.experimental import pallas as pl
from jax.experimental.pallas import tpu as pltpu
from jax.sharding import PartitionSpec as P


eps_norm = 1e-05
theta_base = 1000000.0
negative = -1e30
bf16 = jnp.bfloat16
f32 = jnp.float32
lanes = 128
pos_base = 128
pos_rows = 16


def dot_f32(lhs, rhs, lhs_dim, rhs_dim):
    return lax.dot_general(
        lhs, rhs, (((lhs_dim,), (rhs_dim,)), ((), ())), preferred_element_type=f32
    )


def rms_stat(values):
    return lax.rsqrt(jnp.mean(values * values, axis=-1, keepdims=True) + eps_norm)


def rms_back(grad_in, values, stat_val):
    return stat_val * grad_in - values * stat_val**3 * jnp.mean(
        grad_in * values, axis=-1, keepdims=True
    )


def xor_swap(value, axis, flip):
    size = lax.axis_size(axis)
    return lax.ppermute(value, axis, [(index, index ^ flip) for index in range(size)])


def pick(value, index, axis=0):
    return lax.dynamic_index_in_dim(value, index, axis, keepdims=False)


def xor_order(stacked, index):
    count = stacked.shape[0]
    rest = stacked.shape[1:]
    bits = count.bit_length() - 1
    shaped = stacked.reshape((2,) * bits + rest)
    for bit in range(bits):
        axis = bits - 1 - bit
        shaped = jnp.where((index >> bit) & 1 == 1, jnp.flip(shaped, axis), shaped)
    return shaped.reshape(stacked.shape)


def ctx_exchange(blocks):
    count = blocks.shape[0]
    here = lax.axis_index("ctx")
    found = [pick(blocks, here)] + [None] * (count - 1)
    for flip in range(count - 1, 0, -1):
        found[flip] = xor_swap(pick(blocks, here ^ flip), "ctx", flip)
    return found


def head_masked(scores, low_row, query_start, key_count):
    query_count = scores.shape[1]
    key_index = lax.broadcasted_iota(jnp.int32, scores.shape, 0)
    query_index = query_start + lax.broadcasted_iota(jnp.int32, scores.shape, 1)
    return (key_index <= query_index) & (key_index >= low_row)


def gather_blocks(order_ref, block_refs, query_buf, key_buf, value_buf, low_buf):
    block_len = block_refs[0].shape[0] - pos_rows
    head_dim = key_buf.shape[1]
    query_width = query_buf.shape[1]
    for flip, block_ref in enumerate(block_refs):
        place = order_ref[flip]
        row_start = pl.multiple_of(place * block_len, block_len)
        rows = pl.ds(row_start, block_len)
        query_buf[rows, :] = block_ref[:block_len, :query_width]
        key_buf[rows, :] = block_ref[:block_len, query_width : query_width + head_dim]
        value_buf[rows, :] = block_ref[:block_len, query_width + head_dim :]
        tail = block_ref[block_len:, :].astype(f32)
        found = tail[:1, :block_len] * pos_base + tail[:1, block_len : 2 * block_len]
        token = row_start + lax.broadcasted_iota(jnp.int32, (1, block_len), 1)
        low_buf[place, :, :] = token - found.astype(jnp.int32)


def attend_kernel(count, *refs):
    order_ref = refs[0]
    block_refs = refs[1 : 1 + count]
    out_ref, lse_ref, query_buf, key_buf, value_buf, low_buf = refs[1 + count :]
    gather_blocks(order_ref, block_refs, query_buf, key_buf, value_buf, low_buf)
    total, head_dim = key_buf.shape
    block_len = total // count
    group = query_buf.shape[1] // head_dim
    tile = min(256, total)
    per_tile = tile // block_len
    for start in range(0, total, tile):
        key_count = start + tile
        low_row = jnp.concatenate(
            [low_buf[start // block_len + n] for n in range(per_tile)], axis=1
        )
        keys = key_buf[:key_count, :]
        vals = value_buf[:key_count, :]
        turned = []
        for head in range(group):
            query = query_buf[start : start + tile, head * head_dim : (head + 1) * head_dim]
            scores = dot_f32(keys, query, 1, 1) * head_dim ** (-0.5)
            allowed = head_masked(scores, low_row, start, key_count)
            scores = jnp.where(allowed, scores, negative)
            top = jnp.max(scores, axis=0, keepdims=True)
            weights = jnp.exp(scores - top)
            row_sum = jnp.sum(weights, axis=0, keepdims=True)
            lse_ref[head : head + 1, start : start + tile] = top + jnp.log(row_sum)
            turned.append(dot_f32(vals, weights.astype(bf16), 0, 0) / row_sum)
        merged = jnp.concatenate(turned, axis=0).T.astype(bf16)
        for n in range(per_tile):
            out_ref[start // block_len + n] = merged[n * block_len : (n + 1) * block_len]


def attend_back_kernel(count, *refs):
    order_ref = refs[0]
    block_refs = refs[1 : 1 + count]
    grad_refs = refs[1 + count : 1 + 2 * count]
    (out_ref, lse_ref, packed_ref, query_buf, key_buf, value_buf, low_buf, grad_buf, key_acc, value_acc) = refs[
        1 + 2 * count :
    ]
    gather_blocks(order_ref, block_refs, query_buf, key_buf, value_buf, low_buf)
    total, head_dim = key_buf.shape
    block_len = total // count
    group = query_buf.shape[1] // head_dim
    for flip, grad_ref in enumerate(grad_refs):
        row_start = pl.multiple_of(order_ref[flip] * block_len, block_len)
        grad_buf[pl.ds(row_start, block_len), :] = grad_ref[...]
    key_acc[...] = jnp.zeros_like(key_acc)
    value_acc[...] = jnp.zeros_like(value_acc)
    tile = min(256, total)
    per_tile = tile // block_len
    scale = head_dim ** (-0.5)
    ones_row = jnp.ones((8, head_dim), f32)
    for start in range(0, total, tile):
        key_count = start + tile
        first_block = start // block_len
        low_row = jnp.concatenate([low_buf[first_block + n] for n in range(per_tile)], axis=1)
        keys = key_buf[:key_count, :]
        vals = value_buf[:key_count, :]
        turned = []
        for head in range(group):
            cols = slice(head * head_dim, (head + 1) * head_dim)
            query = query_buf[start : start + tile, cols]
            grad = grad_buf[start : start + tile, cols]
            out = jnp.concatenate([out_ref[first_block + n] for n in range(per_tile)], axis=0)[:, cols]
            product = grad.astype(f32) * out.astype(f32)
            delta = lax.dot_general(
                ones_row,
                product,
                (((1,), (1,)), ((), ())),
                precision=lax.Precision.HIGHEST,
                preferred_element_type=f32,
            )[:1, :]
            scores = dot_f32(keys, query, 1, 1) * scale
            allowed = head_masked(scores, low_row, start, key_count)
            lse_row = lse_ref[head : head + 1, start : start + tile]
            probs = jnp.where(allowed, jnp.exp(scores - lse_row), 0.0)
            grad_scores = (probs * (dot_f32(vals, grad, 1, 1) - delta)).astype(bf16)
            value_acc[:key_count, :] += dot_f32(probs.astype(bf16), grad, 1, 0)
            key_acc[:key_count, :] += dot_f32(grad_scores, query, 1, 0)
            turned.append(dot_f32(keys, grad_scores, 0, 0) * scale)
        merged = jnp.concatenate(turned, axis=0).T.astype(bf16)
        for n in range(per_tile):
            packed_ref[first_block + n, :, : group * head_dim] = merged[
                n * block_len : (n + 1) * block_len
            ]
    for n in range(count):
        rows = slice(n * block_len, (n + 1) * block_len)
        both = jnp.concatenate([key_acc[rows, :] * scale, value_acc[rows, :]], axis=1)
        packed_ref[n, :, group * head_dim :] = both.astype(bf16)


def smem_spec():
    return pl.BlockSpec(memory_space=pltpu.SMEM)


def vmem_spec():
    return pl.BlockSpec(memory_space=pltpu.VMEM)


def shape_of(shape, dtype):
    return jax.ShapeDtypeStruct(shape, dtype)


def whole_call(kernel, name, outs, args, scalars=(), scratch=(), flops=0):
    moved = sum(arg.size * arg.dtype.itemsize for arg in args)
    moved += sum(out.size * jnp.dtype(out.dtype).itemsize for out in outs)
    return pl.pallas_call(
        kernel,
        out_shape=tuple(outs),
        in_specs=[smem_spec()] * len(scalars) + [vmem_spec()] * len(args),
        out_specs=tuple(vmem_spec() for _ in outs),
        scratch_shapes=list(scratch),
        cost_estimate=pl.CostEstimate(flops=flops, bytes_accessed=moved, transcendentals=0),
        name=name,
    )(*scalars, *args)


def head_forward(order, blocks, head_dim, group):
    count = len(blocks)
    block_len = blocks[0].shape[0] - pos_rows
    total = count * block_len
    return pl.pallas_call(
        functools.partial(attend_kernel, count),
        out_shape=(
            jax.ShapeDtypeStruct((count, block_len, group * head_dim), bf16),
            jax.ShapeDtypeStruct((group, total), f32),
        ),
        in_specs=[smem_spec()] + [vmem_spec()] * count,
        out_specs=(vmem_spec(), vmem_spec()),
        scratch_shapes=[
            pltpu.VMEM((total, group * head_dim), bf16),
            pltpu.VMEM((total, head_dim), bf16),
            pltpu.VMEM((total, head_dim), bf16),
            pltpu.VMEM((count, 1, block_len), jnp.int32),
        ],
        cost_estimate=pl.CostEstimate(
            flops=4 * total * total * head_dim * group,
            bytes_accessed=2 * total * 512,
            transcendentals=total * total * group,
        ),
        name="attend",
    )(order, *blocks)


def head_backward(order, blocks, grads, out, log_sum, head_dim, group):
    count = len(blocks)
    block_len = grads[0].shape[0]
    total = count * block_len
    return pl.pallas_call(
        functools.partial(attend_back_kernel, count),
        out_shape=jax.ShapeDtypeStruct((count, block_len, (group + 2) * head_dim), bf16),
        in_specs=[smem_spec()] + [vmem_spec()] * (2 * count + 2),
        out_specs=vmem_spec(),
        scratch_shapes=[
            pltpu.VMEM((total, group * head_dim), bf16),
            pltpu.VMEM((total, head_dim), bf16),
            pltpu.VMEM((total, head_dim), bf16),
            pltpu.VMEM((count, 1, block_len), jnp.int32),
            pltpu.VMEM((total, group * head_dim), bf16),
            pltpu.VMEM((total, head_dim), f32),
            pltpu.VMEM((total, head_dim), f32),
        ],
        cost_estimate=pl.CostEstimate(
            flops=10 * total * total * head_dim * group,
            bytes_accessed=2 * total * 1024,
            transcendentals=total * total * group,
        ),
        name="attend_back",
    )(order, *blocks, *grads, out, log_sum)


def gathered_scores(query_grouped, key_piece, query_pos, lowest_pos, key_pos):
    head_dim = query_grouped.shape[-1]
    keys_split = key_piece.reshape(
        key_piece.shape[0], key_piece.shape[1], query_grouped.shape[2], head_dim
    )
    scores = jnp.einsum(
        "sqhgd,skhd->shgqk", query_grouped, keys_split, preferred_element_type=f32
    ) * head_dim ** (-0.5)
    allowed = (key_pos[None, None, :] <= query_pos[None, :, None]) & (
        key_pos[None, None, :] >= lowest_pos[:, :, None]
    )
    allowed = allowed[:, None, None, :, :]
    return (jnp.where(allowed, scores, negative), allowed, keys_split)


def gathered_forward(query_grouped, key_rows, value_rows, query_index, lowest_key):
    key_all = lax.all_gather(key_rows, "ctx", axis=1, tiled=True)
    value_all = lax.all_gather(value_rows, "ctx", axis=1, tiled=True)
    key_pos = jnp.arange(key_all.shape[1], dtype=jnp.int32)
    scores, allowed, keys_split = gathered_scores(
        query_grouped, key_all, query_index, lowest_key, key_pos
    )
    top = jnp.max(scores, axis=-1)
    weights = jnp.where(allowed, jnp.exp(scores - top[..., None]), 0.0)
    row_sum = jnp.sum(weights, axis=-1)
    summed = jnp.einsum(
        "shgqk,skhd->shgqd",
        weights.astype(bf16),
        value_all.reshape(keys_split.shape),
        preferred_element_type=f32,
    )
    attended = (summed / row_sum[..., None]).astype(bf16)
    return (jnp.transpose(attended, (0, 3, 1, 2, 4)), top + jnp.log(row_sum), key_all, value_all)


def gathered_backward(
    query_grouped, grad_grouped, attended, log_sum, key_all, value_all, query_index, lowest_key
):
    scale = query_grouped.shape[-1] ** (-0.5)
    key_pos = jnp.arange(key_all.shape[1], dtype=jnp.int32)
    delta_rows = jnp.sum(grad_grouped.astype(f32) * attended.astype(f32), axis=-1)
    delta_stat = jnp.transpose(delta_rows, (0, 2, 3, 1))
    scores, allowed, keys_split = gathered_scores(
        query_grouped, key_all, query_index, lowest_key, key_pos
    )
    probs = jnp.where(allowed, jnp.exp(scores - log_sum[..., None]), 0.0)
    grad_probs = jnp.einsum(
        "sqhgd,skhd->shgqk",
        grad_grouped,
        value_all.reshape(keys_split.shape),
        preferred_element_type=f32,
    )
    grad_scores = (probs * (grad_probs - delta_stat[..., None])).astype(bf16)
    query_grad = (
        jnp.einsum("shgqk,skhd->sqhgd", grad_scores, keys_split, preferred_element_type=f32) * scale
    )
    key_grad = (
        jnp.einsum("shgqk,sqhgd->skhd", grad_scores, query_grouped, preferred_element_type=f32)
        * scale
    )
    value_grad = jnp.einsum(
        "shgqk,sqhgd->skhd", probs.astype(bf16), grad_grouped, preferred_element_type=f32
    )
    key_own, value_own = (
        lax.psum_scatter(part.reshape(key_all.shape), "ctx", scatter_dimension=1, tiled=True)
        for part in (key_grad, value_grad)
    )
    return (query_grad, key_own, value_own)


def split_dot(value, table):
    high = value.astype(bf16)
    low = (value - high.astype(f32)).astype(bf16)
    return dot_f32(high, table, 1, 0) + dot_f32(low, table, 1, 0)


def head_table(head_dim):
    row = lax.broadcasted_iota(jnp.int32, (lanes, lanes), 0) // head_dim
    col = lax.broadcasted_iota(jnp.int32, (lanes, lanes), 1) // head_dim
    return jnp.where(row == col, 1.0 / head_dim, 0.0).astype(bf16)


def swap_halves(value, head_dim):
    lane = lax.broadcasted_iota(jnp.int32, value.shape, 1)
    ahead = pltpu.roll(value, lanes - head_dim // 2, 1)
    behind = pltpu.roll(value, head_dim // 2, 1)
    return jnp.where(lane % head_dim < head_dim // 2, ahead, behind)


def front_kernel(
    head_dim,
    tokens_ref,
    gain_ref,
    query_w_ref,
    key_w_ref,
    value_w_ref,
    q_gain_ref,
    k_gain_ref,
    cos_ref,
    sin_ref,
    pos_ref,
    blocks_ref,
    normed_ref,
    query_ref,
    key_ref,
):
    rows = tokens_ref[...].astype(f32)
    stat = lax.rsqrt(jnp.mean(rows * rows, axis=1, keepdims=True) + eps_norm)
    normed = (rows * stat * gain_ref[...]).astype(bf16)
    normed_ref[...] = normed
    query = dot_f32(normed, query_w_ref[...], 1, 0)
    key = dot_f32(normed, key_w_ref[...], 1, 0)
    value = dot_f32(normed, value_w_ref[...], 1, 0).astype(bf16).astype(f32)
    query_ref[...] = query
    key_ref[...] = key
    table = head_table(head_dim)
    cosine = cos_ref[...]
    sine = sin_ref[...]
    seq_count = pos_ref.shape[0]
    block_len = rows.shape[0] // seq_count
    kv_heads = key.shape[1] // head_dim
    lane = lax.broadcasted_iota(jnp.int32, (rows.shape[0], lanes), 1)

    def turned(tile, gain):
        stat_val = lax.rsqrt(split_dot(tile * tile, table) + eps_norm)
        scaled = tile * stat_val * gain
        return scaled * cosine + swap_halves(scaled, head_dim) * sine

    for head in range(kv_heads):
        query_tile = turned(query[:, head * lanes : (head + 1) * lanes], q_gain_ref[...]).astype(bf16)
        pair = slice(head // 2 * lanes, (head // 2 + 1) * lanes)
        key_tile = turned(key[:, pair], k_gain_ref[...])
        value_tile = value[:, pair]
        if head % 2 == 0:
            value_tile = pltpu.roll(value_tile, head_dim, 1)
        else:
            key_tile = pltpu.roll(key_tile, head_dim, 1)
        both = jnp.where(lane < head_dim, key_tile, value_tile).astype(bf16)
        for seq in range(seq_count):
            part = slice(seq * block_len, (seq + 1) * block_len)
            place = seq * kv_heads + head
            blocks_ref[place, :block_len, :lanes] = query_tile[part]
            blocks_ref[place, :block_len, lanes:] = both[part]
            blocks_ref[place, block_len:, :] = pos_ref[seq]


def place_blocks(order_ref, block_refs, store):
    for flip, block_ref in enumerate(block_refs):
        store(order_ref[flip], block_ref)


def project_kernel(seq_count, order_ref, *refs):
    count = len(refs) - 3
    block_refs = refs[:count]
    weight_ref, heads_ref, part_ref = refs[count:]
    kv_heads = count // seq_count
    block_len = block_refs[0].shape[0]

    def store(place, block_ref):
        seq = place // kv_heads
        row_start = pl.multiple_of(seq * block_len, block_len)
        heads_ref[place % kv_heads, pl.ds(row_start, block_len), :] = block_ref[...]

    place_blocks(order_ref, block_refs, store)
    total = None
    for head in range(kv_heads):
        found = dot_f32(heads_ref[head], weight_ref[:, head * lanes : (head + 1) * lanes], 1, 1)
        total = found if total is None else total + found
    part_ref[...] = total.astype(bf16)


def ffn_kernel(
    steps,
    tokens_ref,
    own_ref,
    other_ref,
    gain_ref,
    cot_ref,
    gate_ref,
    up_ref,
    down_ref,
    mixed_ref,
    normed_ref,
    hidden_ref,
    both_ref,
    ffn_ref,
    back_ref,
    ffn_acc,
    back_acc,
):
    step = pl.program_id(0)

    @pl.when(step == 0)
    def _():
        mixed = tokens_ref[...].astype(f32) + (own_ref[...].astype(f32) + other_ref[...].astype(f32))
        mixed_ref[...] = mixed
        stat = lax.rsqrt(jnp.mean(mixed * mixed, axis=1, keepdims=True) + eps_norm)
        normed_ref[...] = (mixed * stat * gain_ref[...]).astype(bf16)
        ffn_acc[...] = jnp.zeros_like(ffn_acc)
        back_acc[...] = jnp.zeros_like(back_acc)

    normed = normed_ref[...]
    gate = dot_f32(normed, gate_ref[...], 1, 0)
    up = dot_f32(normed, up_ref[...], 1, 0)
    grad = dot_f32(cot_ref[...], down_ref[...], 1, 0)
    sig = jax.nn.sigmoid(gate)
    silu = gate * sig
    hidden = (silu * up).astype(bf16)
    hidden_ref[...] = hidden
    grad_gate = (grad * up * (sig * (1.0 + gate * (1.0 - sig)))).astype(bf16)
    grad_up = (grad * silu).astype(bf16)
    both_ref[0, 0] = grad_gate
    both_ref[0, 1] = grad_up
    ffn_acc[...] += dot_f32(hidden, down_ref[...], 1, 1)
    back_acc[...] += dot_f32(grad_gate, gate_ref[...], 1, 1) + dot_f32(grad_up, up_ref[...], 1, 1)

    @pl.when(step == steps - 1)
    def _():
        ffn_ref[...] = ffn_acc[...].astype(bf16)
        back_ref[...] = back_acc[...].astype(bf16)


def ffn_call(tokens_in, own, other, gain, cot, w_gate, w_up, w_down):
    row_count, model_width = tokens_in.shape
    cols = w_gate.shape[1]
    half = cols // 2
    tile = half
    while tile > 384 and (tile // lanes) % 3 == 0:
        tile //= 3
    steps = cols // tile
    per_half = half // tile
    fixed = lambda *shape: pl.BlockSpec(shape, lambda step: (0,) * len(shape))
    moving = pl.BlockSpec((model_width, tile), lambda step: (0, step))
    rows_spec = fixed(row_count, model_width)
    return pl.pallas_call(
        functools.partial(ffn_kernel, steps),
        grid=(steps,),
        out_shape=(
            shape_of((row_count, model_width), f32),
            shape_of((row_count, model_width), bf16),
            shape_of((row_count, cols), bf16),
            shape_of((2, 2, row_count, half), bf16),
            shape_of((row_count, model_width), bf16),
            shape_of((row_count, model_width), bf16),
        ),
        in_specs=[rows_spec, rows_spec, rows_spec, fixed(1, model_width), rows_spec]
        + [moving] * 3,
        out_specs=(
            rows_spec,
            rows_spec,
            pl.BlockSpec((row_count, tile), lambda step: (0, step)),
            pl.BlockSpec(
                (1, 2, row_count, tile), lambda step: (step // per_half, 0, 0, step % per_half)
            ),
            rows_spec,
            rows_spec,
        ),
        scratch_shapes=[pltpu.VMEM((row_count, model_width), f32)] * 2,
        cost_estimate=pl.CostEstimate(
            flops=16 * row_count * model_width * cols,
            bytes_accessed=6 * model_width * cols,
            transcendentals=row_count * cols,
        ),
        name="ffn",
    )(tokens_in, own, other, gain, cot, w_gate, w_up, w_down)


def middle_kernel(
    seq_count,
    mixed_ref,
    ffn_own_ref,
    ffn_other_ref,
    back_own_ref,
    back_other_ref,
    gain_ref,
    cot_ref,
    weight_ref,
    layer_ref,
    grad_ref,
    rounded_ref,
    blocks_ref,
    row_ref,
):
    mixed = mixed_ref[...]
    layer_ref[...] = mixed + (ffn_own_ref[...].astype(f32) + ffn_other_ref[...].astype(f32))
    found = back_own_ref[...].astype(f32) + back_other_ref[...].astype(f32)
    stat = lax.rsqrt(jnp.mean(mixed * mixed, axis=1, keepdims=True) + eps_norm)
    row_ref[...] = jnp.broadcast_to(
        jnp.sum(found * mixed * stat, axis=0, keepdims=True), row_ref.shape
    )
    grad = cot_ref[...].astype(f32) + rms_back(found * gain_ref[...], mixed, stat)
    grad_ref[...] = grad
    rounded = grad.astype(bf16)
    rounded_ref[...] = rounded
    attended = dot_f32(rounded, weight_ref[...], 1, 0).astype(bf16)
    count, block_len, _ = blocks_ref.shape
    kv_heads = count // seq_count
    for place in range(count):
        seq = place // kv_heads
        head = place % kv_heads
        blocks_ref[place] = attended[
            seq * block_len : (seq + 1) * block_len, head * lanes : (head + 1) * lanes
        ]


def turn_back_kernel(seq_count, head_dim, order_ref, *refs):
    count = len(refs) - 15
    block_refs = refs[:count]
    (
        query_ref,
        key_ref,
        q_gain_ref,
        k_gain_ref,
        cos_ref,
        sin_ref,
        query_w_ref,
        key_w_ref,
        value_w_ref,
        raw_ref,
        part_ref,
        gain_row_ref,
        query_buf,
        pair_buf,
        spare_buf,
    ) = refs[count:]
    kv_heads = count // seq_count
    block_len = block_refs[0].shape[0]

    def store(place, block_ref):
        rows = pl.ds(pl.multiple_of(place // kv_heads * block_len, block_len), block_len)
        query_buf[place % kv_heads, rows, :] = block_ref[:, :lanes]
        pair_buf[place % kv_heads, rows, :] = block_ref[:, lanes:]

    place_blocks(order_ref, block_refs, store)
    table = head_table(head_dim)
    cosine = cos_ref[...]
    sine = sin_ref[...]
    lane = lax.broadcasted_iota(jnp.int32, cosine.shape, 1)

    def back(grad_rot, raw, gain):
        grad_norm = grad_rot * cosine - swap_halves(grad_rot, head_dim) * sine
        stat = lax.rsqrt(split_dot(raw * raw, table) + eps_norm)
        gain_row = jnp.sum(grad_norm * raw * stat, axis=0, keepdims=True)
        grad_in = grad_norm * gain
        grad_raw = stat * grad_in - raw * stat**3 * split_dot(grad_in * raw, table)
        return (grad_raw.astype(bf16), gain_row)

    total = None
    gain_rows = [None, None]
    place = 0
    per_slot = raw_ref.shape[2] // lanes

    def emit(tile, weight, kind, gain_row):
        nonlocal total, place
        slot = place % per_slot
        raw_ref[place // per_slot, :, slot * lanes : (slot + 1) * lanes] = tile
        place += 1
        found = dot_f32(tile, weight, 1, 1)
        total = found if total is None else total + found
        if gain_row is not None:
            gain_rows[kind] = gain_row if gain_rows[kind] is None else gain_rows[kind] + gain_row

    for head in range(kv_heads):
        cols = slice(head * lanes, (head + 1) * lanes)
        tile, gain_row = back(query_buf[head].astype(f32), query_ref[:, cols], q_gain_ref[...])
        emit(tile, query_w_ref[:, cols], 0, gain_row)
    for pair in range(kv_heads // 2):
        cols = slice(pair * lanes, (pair + 1) * lanes)
        first = pair_buf[2 * pair].astype(f32)
        second = pair_buf[2 * pair + 1].astype(f32)
        merged = jnp.where(lane < head_dim, first, pltpu.roll(second, head_dim, 1))
        tile, gain_row = back(merged, key_ref[:, cols], k_gain_ref[...])
        emit(tile, key_w_ref[:, cols], 1, gain_row)
    for pair in range(kv_heads // 2):
        cols = slice(pair * lanes, (pair + 1) * lanes)
        first = pair_buf[2 * pair].astype(f32)
        second = pair_buf[2 * pair + 1].astype(f32)
        merged = jnp.where(lane < head_dim, pltpu.roll(first, head_dim, 1), second).astype(bf16)
        emit(merged, value_w_ref[:, cols], 1, None)
    part_ref[...] = total.astype(bf16)
    gain_row_ref[...] = jnp.concatenate(
        gain_rows + [jnp.zeros((6, lanes), f32)], axis=0
    )
    del spare_buf


def last_kernel(tokens_ref, grad_ref, own_ref, other_ref, gain_ref, out_ref, row_ref):
    rows = tokens_ref[...].astype(f32)
    stat = lax.rsqrt(jnp.mean(rows * rows, axis=1, keepdims=True) + eps_norm)
    found = own_ref[...].astype(f32) + other_ref[...].astype(f32)
    row_ref[...] = jnp.broadcast_to(
        jnp.sum(found * rows * stat, axis=0, keepdims=True), row_ref.shape
    )
    out_ref[...] = grad_ref[...] + rms_back(found * gain_ref[...], rows, stat)


everywhere = ("ctx", "seq")
plane = 4


def plane_gather(rows, core):
    half = rows.shape[0] // 2
    mine = lax.dynamic_slice_in_dim(rows, core * half, half, 0)
    near = [xor_swap(mine, everywhere, flip) for flip in range(1, plane)]
    far = [xor_swap(found, "tp", 1) for found in near]
    return (rows, near, far)


def window(cols):
    half = cols // 2
    width = min(half, -(-half // (2 * lanes)) * lanes)
    return (half, width)


def plane_exchange(take, place):
    parts = [take(place)]
    for flip in range(1, plane):
        parts.append(xor_swap(take(place ^ flip), everywhere, flip))
    return parts


def rows_kernel(scalars_ref, own_ref, *refs):
    near_refs = refs[: plane - 1]
    far_refs = refs[plane - 1 : 2 * plane - 2]
    col_refs = refs[2 * plane - 2 : 3 * plane - 2]
    out_ref, row_buf = refs[3 * plane - 2 :]
    step = pl.program_id(0)
    row_count = own_ref.shape[0]
    half = row_count // 2
    height = out_ref.shape[1]
    core = scalars_ref[0]
    start = pl.multiple_of((scalars_ref[1] + step * scalars_ref[2]) * height, height)
    cols = pl.ds(start, height)
    row_buf[:row_count, :] = own_ref[:, cols]
    for n in range(plane - 1):
        base = (n + 1) * row_count
        near_rows = pl.ds(pl.multiple_of(base + core * half, half), half)
        far_rows = pl.ds(pl.multiple_of(base + (1 - core) * half, half), half)
        row_buf[near_rows, :] = near_refs[n][:, cols]
        row_buf[far_rows, :] = far_refs[n][:, cols]
    total = None
    for n in range(plane):
        found = dot_f32(row_buf[n * row_count : (n + 1) * row_count, :], col_refs[n][...], 0, 0)
        total = found if total is None else total + found
    out_ref[0] = total.astype(out_ref.dtype)


def rows_call(row_pieces, col_parts, scalars, steps, height, dtype):
    own, near, far = row_pieces
    row_count, model_width = own.shape
    half = row_count // 2
    width = col_parts[0].shape[1]
    fixed = lambda *shape: pl.BlockSpec(shape, lambda step: (0,) * len(shape))
    return pl.pallas_call(
        rows_kernel,
        grid=(steps,),
        out_shape=shape_of((steps, height, width), dtype),
        in_specs=[smem_spec(), fixed(row_count, model_width)]
        + [fixed(half, model_width)] * (2 * plane - 2)
        + [fixed(row_count, width)] * plane,
        out_specs=pl.BlockSpec((1, height, width), lambda step: (step, 0, 0)),
        scratch_shapes=[pltpu.VMEM((plane * row_count, height), bf16)],
        cost_estimate=pl.CostEstimate(
            flops=2 * plane * row_count * steps * height * width,
            bytes_accessed=2 * plane * row_count * (model_width + width)
            + 4 * steps * height * width,
            transcendentals=0,
        ),
        name="rows",
    )(scalars, own, *near, *far, *col_parts)


def halve_rows(row_pieces, col_parts, index, core, total, extra=None):
    blocks = total // plane
    model_width = row_pieces[0].shape[1]
    bits = blocks.bit_length() - 1
    block_index = index // plane
    height = model_width // blocks
    fine = height % lanes == 0
    order = list(range(bits)) if fine else list(range(bits))[::-1]
    first = (block_index >> order[0]) & 1
    if fine:
        steps, scale = blocks // 2, 2
        start = lambda bit: bit
    else:
        steps, height, scale = 1, model_width // 2, 1
        start = lambda bit: bit
    table = lambda bit: jnp.stack([core, start(bit), jnp.int32(scale)]).astype(jnp.int32)
    sent = rows_call(row_pieces, col_parts, table(1 - first), steps, height, bf16)
    kept = rows_call(row_pieces, col_parts, table(first), steps, height, f32)
    if extra is not None:
        shaped = (
            extra.reshape(steps, 2, height, -1) if fine else extra.reshape(1, 2, height, -1)
        )
        sent = jnp.concatenate([sent, pick(shaped, 1 - first, 1).astype(bf16)], axis=2)
        kept = jnp.concatenate([kept, pick(shaped, first, 1)], axis=2)
    width = kept.shape[2]
    kept = kept + xor_swap(sent, everywhere, plane << order[0]).astype(f32)
    for turn, bit in enumerate(order[1:]):
        own_bit = (block_index >> bit) & 1
        if fine:
            shaped = kept.reshape(steps >> (turn + 1), 2, height, width)
        else:
            shaped = kept.reshape(1, 2, -1, width)
        sent = pick(shaped, 1 - own_bit, 1).astype(bf16)
        kept = pick(shaped, own_bit, 1)
        kept = kept + xor_swap(sent, everywhere, plane << bit).astype(f32)
    return kept.reshape(-1, width)


def return_rows(summed, place):
    width = summed.shape[1]
    shaped = summed.reshape(plane, -1, width)
    found = [pick(shaped, place)]
    for flip in range(1, plane):
        sent = pick(shaped, place ^ flip).astype(bf16)
        found.append(xor_swap(sent, everywhere, flip))
    return found


def assemble_kernel(moves, order_ref, *refs):
    part_refs = refs[:plane]
    out_refs = refs[plane:]
    for flip in range(plane):
        for member in range(plane):

            @pl.when(order_ref[flip] == member)
            def _():
                for out, out_start, start, width in moves[member]:
                    out_refs[out][:, out_start : out_start + width] = part_refs[flip][
                        :, start : start + width
                    ].astype(f32)


def assemble(parts, order, moves, widths):
    height = parts[0].shape[0]
    return whole_call(
        functools.partial(assemble_kernel, moves),
        "assemble",
        [shape_of((height, width), f32) for width in widths],
        parts,
        scalars=(order,),
    )


def shards(
    tokens,
    positions,
    attn_gain,
    ffn_gain,
    q_gain,
    k_gain,
    w_query,
    w_key,
    w_value,
    w_out,
    w_gate,
    w_up,
    w_down,
    cotangent,
):
    seq_count, block_len, model_width = tokens.shape
    row_count = seq_count * block_len
    head_dim = q_gain.shape[0]
    half_dim = head_dim // 2
    q_heads = w_query.shape[1] // head_dim
    kv_heads = w_key.shape[1] // head_dim
    key_width = kv_heads * head_dim
    query_width = q_heads * head_dim
    group_size = q_heads // kv_heads
    hidden_width = w_gate.shape[1]
    ctx_size = lax.axis_size("ctx")
    total = ctx_size * lax.axis_size("seq")
    here_index = lax.axis_index("ctx")
    index = lax.axis_index(everywhere)
    core = lax.axis_index("tp")
    place = index % plane
    count = seq_count * kv_heads
    by_head = ctx_size == count
    natural = jnp.arange(count, dtype=jnp.int32)
    order = here_index ^ natural if by_head else natural
    plane_order = place ^ jnp.arange(plane, dtype=jnp.int32)
    rows_bf = shape_of((row_count, model_width), bf16)
    rows_f32 = shape_of((row_count, model_width), f32)

    cot_rows = cotangent.reshape(row_count, model_width)
    token_rows = tokens.reshape(row_count, model_width)
    cot_plane = plane_gather(cot_rows, core)

    frequency = theta_base ** (-(jnp.arange(half_dim, dtype=f32) * 2.0) / head_dim)
    repeat = lanes // half_dim
    angles = positions.reshape(row_count, 1).astype(f32) * jnp.tile(frequency, repeat)[None, :]
    cosine = jnp.cos(angles)
    sign = jnp.where(jnp.arange(lanes) % head_dim < half_dim, -1.0, 1.0)
    sine = jnp.sin(angles) * sign[None, :]
    pack_width = 2 * lanes
    pos_row = jnp.concatenate([positions // pos_base, positions % pos_base], axis=1)
    pos_row = jnp.broadcast_to(
        pos_row.astype(bf16)[:, None, :], (seq_count, pos_rows, pack_width)
    )
    q_gain_row = jnp.tile(q_gain, lanes // head_dim)[None, :]
    k_gain_row = jnp.tile(k_gain, lanes // head_dim)[None, :]
    attn_gain_row = attn_gain[None, :]
    ffn_gain_row = ffn_gain[None, :]

    packed, normed_one, query_raw, key_raw = whole_call(
        functools.partial(front_kernel, head_dim),
        "front",
        [
            shape_of((count, block_len + pos_rows, pack_width), bf16),
            rows_bf,
            shape_of((row_count, query_width), f32),
            shape_of((row_count, key_width), f32),
        ],
        [
            token_rows,
            attn_gain_row,
            w_query,
            w_key,
            w_value,
            q_gain_row,
            k_gain_row,
            cosine,
            sine,
            pos_row,
        ],
        flops=2 * row_count * model_width * (query_width + 2 * key_width),
    )

    if by_head:
        blocks = ctx_exchange(packed)
        out_heads, log_sum = head_forward(order, blocks, head_dim, group_size)
        out_blocks = ctx_exchange(out_heads)
    else:
        flat = packed[:, :block_len].reshape(seq_count, kv_heads, block_len, pack_width)
        flat = jnp.transpose(flat, (0, 2, 1, 3))
        query_grouped = flat[..., :lanes].reshape(
            seq_count, block_len, kv_heads, group_size, head_dim
        )
        query_index = here_index * block_len + jnp.arange(block_len, dtype=jnp.int32)
        lowest_key = query_index[None, :] - positions
        attended_grouped, log_sum, key_all, value_all = gathered_forward(
            query_grouped,
            flat[..., lanes : lanes + head_dim].reshape(seq_count, block_len, key_width),
            flat[..., lanes + head_dim :].reshape(seq_count, block_len, key_width),
            query_index,
            lowest_key,
        )
        out_blocks = list(
            jnp.transpose(attended_grouped, (0, 2, 1, 3, 4)).reshape(count, block_len, lanes)
        )

    heads, attn_part = whole_call(
        functools.partial(project_kernel, seq_count),
        "project",
        [shape_of((kv_heads, row_count, lanes), bf16), rows_bf],
        [*out_blocks, w_out],
        scalars=(order,),
        flops=2 * row_count * model_width * query_width,
    )
    one_plane = plane_gather(normed_one, core)
    mixed, normed_two, hidden, both_pre, ffn_part, back_part = ffn_call(
        token_rows,
        attn_part,
        xor_swap(attn_part, "tp", 1),
        ffn_gain_row,
        cot_rows,
        w_gate,
        w_up,
        w_down,
    )
    two_plane = plane_gather(normed_two, core)
    half, width = window(hidden_width)

    def take_hidden(member):
        start = (member % 2) * half + (member // 2) * (half - width)
        return lax.dynamic_slice_in_dim(hidden, start, width, 1)

    hidden_plane = plane_exchange(take_hidden, place)
    both_flat = both_pre.reshape(plane, row_count, half)
    both_plane = plane_exchange(lambda member: pick(both_flat, member), place)

    layer_output, grad_mixed, grad_mixed_bf, grad_blocks, ffn_row = whole_call(
        functools.partial(middle_kernel, seq_count),
        "middle",
        [
            rows_f32,
            rows_f32,
            rows_bf,
            shape_of((count, block_len, lanes), bf16),
            shape_of((8, model_width), f32),
        ],
        [
            mixed,
            ffn_part,
            xor_swap(ffn_part, "tp", 1),
            back_part,
            xor_swap(back_part, "tp", 1),
            ffn_gain_row,
            cot_rows,
            w_out,
        ],
        flops=2 * row_count * model_width * query_width,
    )

    if by_head:
        grads = ctx_exchange(grad_blocks)
        packed_grads = head_backward(
            order, blocks, grads, out_heads, log_sum, head_dim, group_size
        )
        returned = ctx_exchange(packed_grads)
    else:
        grad_grouped = jnp.transpose(
            grad_blocks.reshape(seq_count, kv_heads, block_len, group_size, head_dim),
            (0, 2, 1, 3, 4),
        )
        query_grad, key_grad_own, value_grad_own = gathered_backward(
            query_grouped,
            grad_grouped,
            attended_grouped,
            log_sum,
            key_all,
            value_all,
            query_index,
            lowest_key,
        )
        shaped = lambda grad: grad.reshape(seq_count, block_len, kv_heads, -1)
        returned = jnp.concatenate(
            [shaped(query_grad), shaped(key_grad_own), shaped(value_grad_own)], axis=-1
        ).astype(bf16)
        returned = list(
            jnp.transpose(returned, (0, 2, 1, 3)).reshape(count, block_len, pack_width)
        )

    raw_width = (query_width + 2 * key_width) // plane
    grad_raw, one_part, head_rows = whole_call(
        functools.partial(turn_back_kernel, seq_count, head_dim),
        "turn_back",
        [
            shape_of((plane, row_count, raw_width), bf16),
            rows_bf,
            shape_of((8, lanes), f32),
        ],
        [
            *returned,
            query_raw,
            key_raw,
            q_gain_row,
            k_gain_row,
            cosine,
            sine,
            w_query,
            w_key,
            w_value,
        ],
        scalars=(order,),
        scratch=[
            pltpu.VMEM((kv_heads, row_count, lanes), bf16),
            pltpu.VMEM((kv_heads, row_count, lanes), bf16),
            pltpu.VMEM((8, lanes), f32),
        ],
        flops=2 * row_count * model_width * (query_width + 2 * key_width),
    )
    raw_plane = plane_exchange(lambda member: pick(grad_raw, member), place)
    input_grad, attn_row = whole_call(
        last_kernel,
        "last",
        [rows_f32, shape_of((8, model_width), f32)],
        [token_rows, grad_mixed, one_part, xor_swap(one_part, "tp", 1), attn_gain_row],
    )

    down_sum = halve_rows(cot_plane, hidden_plane, index, core, total)
    down_parts = return_rows(down_sum, place)
    skip = 2 * width - half
    (wdown_grad,) = assemble(
        down_parts,
        plane_order,
        [
            [(0, half * (member % 2), 0, width)]
            if member < 2
            else [(0, half * (member % 2) + width, skip, width - skip)]
            for member in range(plane)
        ],
        [hidden_width],
    )
    both_sum = halve_rows(two_plane, both_plane, index, core, total)
    both_parts = return_rows(both_sum, place)
    wgate_grad, wup_grad = assemble(
        both_parts,
        plane_order,
        [[(member % 2, half * (member // 2), 0, half)] for member in range(plane)],
        [hidden_width, hidden_width],
    )

    mixed_plane = plane_gather(grad_mixed_bf, core)
    attended_plane = plane_exchange(lambda member: pick(heads, member), place)
    out_sum = halve_rows(mixed_plane, attended_plane, index, core, total)
    out_width = lanes
    out_parts = return_rows(out_sum, place)
    (wo_grad,) = assemble(
        out_parts,
        plane_order,
        [[(0, member * out_width, 0, out_width)] for member in range(plane)],
        [query_width],
    )

    tiles = model_width // head_dim
    folded = head_rows[:2].reshape(2, lanes // head_dim, head_dim).sum(axis=1)
    gain_rows = jnp.concatenate([ffn_row[:1], attn_row[:1], jnp.tile(folded, (1, tiles))], axis=0)
    gain_cols = jnp.pad(gain_rows.T, ((0, 0), (0, lanes - 4)))
    raw_sum = halve_rows(one_plane, raw_plane, index, core, total, gain_cols)
    raw_parts = return_rows(raw_sum, place)
    raw_moves = []
    for member in range(plane):
        moves = []
        for out, begin, size in (
            (0, 0, query_width),
            (1, query_width, key_width),
            (2, query_width + key_width, key_width),
        ):
            low = max(begin, member * raw_width)
            high = min(begin + size, (member + 1) * raw_width)
            if low < high:
                moves.append((out, low - begin, low - member * raw_width, high - low))
        raw_moves.append(moves)
    wq_grad, wk_grad, wv_grad = assemble(
        raw_parts, plane_order, raw_moves, [query_width, key_width, key_width]
    )
    gain_sums = sum(part[:, raw_width : raw_width + 4].astype(f32) for part in raw_parts)
    ffngain_grad = gain_sums[:, 0]
    attngain_grad = gain_sums[:, 1]
    head_gains = lax.reduce_precision(gain_sums[:, 2:4], 8, 23)
    head_gains = head_gains + xor_swap(head_gains, "tp", 1)
    if gain_sums.shape[0] < head_dim:
        whole_gains = lax.all_gather(head_gains, everywhere, axis=0, tiled=True)[:head_dim]
    else:
        whole_gains = head_gains[:head_dim]
    return (
        layer_output.reshape(seq_count, block_len, model_width),
        input_grad.reshape(seq_count, block_len, model_width),
        wq_grad,
        wk_grad,
        wv_grad,
        wo_grad,
        wgate_grad,
        wup_grad,
        wdown_grad,
        attngain_grad,
        ffngain_grad,
        whole_gains[:, 0],
        whole_gains[:, 1],
    )


def solution(mesh):
    placed = (
        P("seq", "ctx", None),
        P("seq", "ctx"),
        P(),
        P(),
        P(),
        P(),
        P(None, "tp"),
        P(None, "tp"),
        P(None, "tp"),
        P(None, "tp"),
        P(None, "tp"),
        P(None, "tp"),
        P(None, "tp"),
        P("seq", "ctx", None),
    )
    return jax.shard_map(
        shards,
        mesh=mesh,
        in_specs=placed,
        out_specs=(
            P("seq", "ctx", None),
            P("seq", "ctx", None),
            P(("ctx", "seq"), "tp"),
            P(("ctx", "seq"), "tp"),
            P(("ctx", "seq"), "tp"),
            P(("ctx", "seq"), "tp"),
            P(("ctx", "seq"), "tp"),
            P(("ctx", "seq"), "tp"),
            P(("ctx", "seq"), "tp"),
            P(("ctx", "seq")),
            P(("ctx", "seq")),
            P(),
            P(),
        ),
        check_vma=False,
    )
```

```python
import functools
import math

import jax
import jax.numpy as jnp
from jax import lax
from jax.experimental import pallas as pl
from jax.experimental.pallas import tpu as pltpu
from jax.sharding import PartitionSpec as P


eps_norm = 1e-05
theta_base = 1000000.0
negative = -1e30
bf16 = jnp.bfloat16
f32 = jnp.float32
lanes = 128
pos_shift = 7
pos_base = 1 << pos_shift
pos_rows = 16


def dot_f32(lhs, rhs, lhs_dim, rhs_dim):
    return lax.dot_general(
        lhs, rhs, (((lhs_dim,), (rhs_dim,)), ((), ())), preferred_element_type=f32
    )


def rms_back(grad_in, values, stat_val):
    return stat_val * grad_in - values * stat_val**3 * jnp.mean(
        grad_in * values, axis=-1, keepdims=True
    )


def xor_swap(value, axis, flip):
    size = lax.axis_size(axis)
    return lax.ppermute(value, axis, [(index, index ^ flip) for index in range(size)])


def pick(value, index, axis=0):
    return lax.dynamic_index_in_dim(value, index, axis, keepdims=False)


def named_swap(value, axis="tp"):
    return xor_swap(value, axis, 1)


def z_exchange(blocks):
    count = blocks.shape[0]
    here = lax.axis_index("ctx") // 2
    found = [pick(blocks, here)] + [None] * (count - 1)
    for flip in range(count - 1, 0, -1):
        found[flip] = xor_swap(pick(blocks, here ^ flip), "ctx", 2 * flip)
    return found


def fill_heads(ref, place, rows, head_dim):
    tokens_count = rows.shape[0]
    for head in range(rows.shape[1] // head_dim):
        ref[place, head * tokens_count : (head + 1) * tokens_count, :] = rows[
            :, head * head_dim : (head + 1) * head_dim
        ]


def gather_blocks(order_ref, block_refs, pair_refs, query_buf, key_buf, value_buf, low_buf):
    count = len(block_refs)
    seq_count = key_buf.shape[0]
    head_dim = key_buf.shape[2]
    block_len = pair_refs[0].shape[0] // seq_count
    side = order_ref[count]
    for flip in range(count):
        level = order_ref[flip]
        block_ref = block_refs[flip]
        own_start = pl.multiple_of((level * 2 + side) * block_len, block_len)
        other_start = pl.multiple_of((level * 2 + 1 - side) * block_len, block_len)
        tail = block_ref[seq_count * block_len :, :].astype(f32)
        found = tail[:, :block_len] * pos_base + tail[:, block_len : 2 * block_len]
        token = own_start + lax.broadcasted_iota(jnp.int32, (1, block_len), 1)
        for seq in range(seq_count):
            part = slice(seq * block_len, (seq + 1) * block_len)
            fill_heads(query_buf, seq * count + level, block_ref[part, :lanes], head_dim)
            own = pl.ds(own_start, block_len)
            other = pl.ds(other_start, block_len)
            key_buf[seq, own, :] = block_ref[part, lanes : lanes + head_dim]
            value_buf[seq, own, :] = block_ref[part, lanes + head_dim :]
            key_buf[seq, other, :] = pair_refs[flip][part, :head_dim]
            value_buf[seq, other, :] = pair_refs[flip][part, head_dim:]
            low_buf[seq * count + level] = token - found[seq : seq + 1].astype(jnp.int32)


def visible(order_ref, low_row, count, level, key_count, block_len, width):
    low = jnp.concatenate([low_row] * (width // block_len), axis=1)
    shape = (key_count, low.shape[1])
    key_index = lax.broadcasted_iota(jnp.int32, shape, 0)
    lane = lax.broadcasted_iota(jnp.int32, shape, 1) % block_len
    query_index = (level * 2 + order_ref[count]) * block_len + lane
    return (key_index <= query_index) & (key_index >= low)


def unfold(turned, block_len):
    parts = [
        turned[:, start : start + block_len] for start in range(0, turned.shape[1], block_len)
    ]
    return jnp.concatenate(parts, axis=0).T


def attend_kernel(count, *refs):
    order_ref = refs[0]
    block_refs = refs[1 : 1 + count]
    pair_refs = refs[1 + count : 1 + 2 * count]
    out_ref, lse_ref, query_buf, key_buf, value_buf, low_buf = refs[1 + 2 * count :]
    gather_blocks(order_ref, block_refs, pair_refs, query_buf, key_buf, value_buf, low_buf)
    seq_count, _, head_dim = key_buf.shape
    block_len = low_buf.shape[2]
    for seq in range(seq_count):
        for level in range(count):
            place = seq * count + level
            key_count = 2 * block_len * (level + 1)
            query = query_buf[place]
            scores = dot_f32(key_buf[seq, :key_count, :], query, 1, 1) * head_dim ** (-0.5)
            allowed = visible(
                order_ref, low_buf[place], count, level, key_count, block_len, query.shape[0]
            )
            scores = jnp.where(allowed, scores, negative)
            top = jnp.max(scores, axis=0, keepdims=True)
            weights = jnp.exp(scores - top)
            row_sum = jnp.sum(weights, axis=0, keepdims=True)
            lse_ref[place : place + 1, :] = top + jnp.log(row_sum)
            turned = dot_f32(value_buf[seq, :key_count, :], weights.astype(bf16), 0, 0) / row_sum
            out_ref[level, seq * block_len : (seq + 1) * block_len, :] = unfold(
                turned, block_len
            ).astype(bf16)


def attend_back_kernel(count, *refs):
    order_ref = refs[0]
    block_refs = refs[1 : 1 + count]
    pair_refs = refs[1 + count : 1 + 2 * count]
    grad_refs = refs[1 + 2 * count : 1 + 3 * count]
    (
        out_ref,
        lse_ref,
        query_grad_ref,
        own_ref,
        other_ref,
        query_buf,
        key_buf,
        value_buf,
        low_buf,
        grad_buf,
        key_acc,
        value_acc,
    ) = refs[1 + 3 * count :]
    gather_blocks(order_ref, block_refs, pair_refs, query_buf, key_buf, value_buf, low_buf)
    seq_count, _, head_dim = key_buf.shape
    block_len = low_buf.shape[2]
    group = lanes // head_dim
    for flip in range(count):
        for seq in range(seq_count):
            rows = grad_refs[flip][seq * block_len : (seq + 1) * block_len, :]
            fill_heads(grad_buf, seq * count + order_ref[flip], rows, head_dim)
    key_acc[...] = jnp.zeros_like(key_acc)
    value_acc[...] = jnp.zeros_like(value_acc)
    scale = head_dim ** (-0.5)
    ones_row = jnp.ones((8, head_dim), f32)
    for seq in range(seq_count):
        for level in range(count):
            place = seq * count + level
            key_count = 2 * block_len * (level + 1)
            keys = key_buf[seq, :key_count, :]
            query = query_buf[place]
            grad = grad_buf[place]
            rows = out_ref[level, seq * block_len : (seq + 1) * block_len, :]
            out = jnp.concatenate(
                [rows[:, head * head_dim : (head + 1) * head_dim] for head in range(group)], axis=0
            )
            delta = lax.dot_general(
                ones_row,
                grad.astype(f32) * out.astype(f32),
                (((1,), (1,)), ((), ())),
                precision=lax.Precision.HIGHEST,
                preferred_element_type=f32,
            )[:1, :]
            scores = dot_f32(keys, query, 1, 1) * scale
            allowed = visible(
                order_ref, low_buf[place], count, level, key_count, block_len, query.shape[0]
            )
            probs = jnp.where(allowed, jnp.exp(scores - lse_ref[place : place + 1, :]), 0.0)
            grad_probs = dot_f32(value_buf[seq, :key_count, :], grad, 1, 1)
            grad_scores = (probs * (grad_probs - delta)).astype(bf16)
            value_acc[seq, :key_count, :] += dot_f32(probs.astype(bf16), grad, 1, 0)
            key_acc[seq, :key_count, :] += dot_f32(grad_scores, query, 1, 0)
            turned = dot_f32(keys, grad_scores, 0, 0) * scale
            query_grad_ref[level, seq * block_len : (seq + 1) * block_len, :] = unfold(
                turned, block_len
            ).astype(bf16)
    side = order_ref[count]
    for seq in range(seq_count):
        part = slice(seq * block_len, (seq + 1) * block_len)
        for level in range(count):
            for ref, place in ((own_ref, side), (other_ref, 1 - side)):
                start = pl.multiple_of((2 * level + place) * block_len, block_len)
                rows = pl.ds(start, block_len)
                both = [key_acc[seq, rows, :] * scale, value_acc[seq, rows, :]]
                ref[level, part, :] = jnp.concatenate(both, axis=1).astype(ref.dtype)


def merge_kernel(query_ref, own_ref, other_ref, out_ref):
    out_ref[:, :, :lanes] = query_ref[...]
    out_ref[:, :, lanes:] = (own_ref[...] + other_ref[...].astype(f32)).astype(bf16)


def smem_spec():
    return pl.BlockSpec(memory_space=pltpu.SMEM)


def vmem_spec():
    return pl.BlockSpec(memory_space=pltpu.VMEM)


def shape_of(shape, dtype):
    return jax.ShapeDtypeStruct(shape, dtype)


def whole_call(kernel, outs, args, scalars=(), scratch=(), flops=0):
    moved = sum(arg.size * arg.dtype.itemsize for arg in args)
    moved += sum(out.size * jnp.dtype(out.dtype).itemsize for out in outs)
    return pl.pallas_call(
        kernel,
        out_shape=tuple(outs),
        in_specs=[smem_spec()] * len(scalars) + [vmem_spec()] * len(args),
        out_specs=tuple(vmem_spec() for _ in outs),
        scratch_shapes=list(scratch),
        cost_estimate=pl.CostEstimate(flops=flops, bytes_accessed=moved, transcendentals=0),
    )(*scalars, *args)


def head_scratch(seq_count, count, block_len, head_dim):
    total = 2 * count * block_len
    heads_rows = lanes // head_dim * block_len
    return [
        pltpu.VMEM((seq_count * count, heads_rows, head_dim), bf16),
        pltpu.VMEM((seq_count, total, head_dim), bf16),
        pltpu.VMEM((seq_count, total, head_dim), bf16),
        pltpu.VMEM((seq_count * count, 1, block_len), jnp.int32),
    ]


def head_forward(order, blocks, pairs, seq_count, head_dim):
    count = len(blocks)
    row_count = pairs[0].shape[0]
    block_len = row_count // seq_count
    heads_rows = lanes // head_dim * block_len
    return whole_call(
        functools.partial(attend_kernel, count),
        [
            shape_of((count, row_count, lanes), bf16),
            shape_of((seq_count * count, heads_rows), f32),
        ],
        [*blocks, *pairs],
        scalars=(order,),
        scratch=head_scratch(seq_count, count, block_len, head_dim),
        flops=8 * row_count * row_count * count * count * lanes,
    )


def head_backward(order, blocks, pairs, grads, out, log_sum, seq_count, head_dim):
    count = len(blocks)
    row_count = pairs[0].shape[0]
    block_len = row_count // seq_count
    heads_rows = lanes // head_dim * block_len
    total = 2 * count * block_len
    return whole_call(
        functools.partial(attend_back_kernel, count),
        [
            shape_of((count, row_count, lanes), bf16),
            shape_of((count, row_count, lanes), f32),
            shape_of((count, row_count, lanes), bf16),
        ],
        [*blocks, *pairs, *grads, out, log_sum],
        scalars=(order,),
        scratch=head_scratch(seq_count, count, block_len, head_dim)
        + [
            pltpu.VMEM((seq_count * count, heads_rows, head_dim), bf16),
            pltpu.VMEM((seq_count, total, head_dim), f32),
            pltpu.VMEM((seq_count, total, head_dim), f32),
        ],
        flops=20 * row_count * row_count * count * count * lanes,
    )


def gathered_scores(query_grouped, key_piece, query_pos, lowest_pos, key_pos):
    head_dim = query_grouped.shape[-1]
    keys_split = key_piece.reshape(
        key_piece.shape[0], key_piece.shape[1], query_grouped.shape[2], head_dim
    )
    scores = jnp.einsum(
        "sqhgd,skhd->shgqk", query_grouped, keys_split, preferred_element_type=f32
    ) * head_dim ** (-0.5)
    allowed = (key_pos[None, None, :] <= query_pos[None, :, None]) & (
        key_pos[None, None, :] >= lowest_pos[:, :, None]
    )
    allowed = allowed[:, None, None, :, :]
    return (jnp.where(allowed, scores, negative), allowed, keys_split)


def gathered_forward(query_grouped, key_rows, value_rows, query_index, lowest_key):
    key_all = lax.all_gather(key_rows, "ctx", axis=1, tiled=True)
    value_all = lax.all_gather(value_rows, "ctx", axis=1, tiled=True)
    key_pos = jnp.arange(key_all.shape[1], dtype=jnp.int32)
    scores, allowed, keys_split = gathered_scores(
        query_grouped, key_all, query_index, lowest_key, key_pos
    )
    top = jnp.max(scores, axis=-1)
    weights = jnp.where(allowed, jnp.exp(scores - top[..., None]), 0.0)
    row_sum = jnp.sum(weights, axis=-1)
    summed = jnp.einsum(
        "shgqk,skhd->shgqd",
        weights.astype(bf16),
        value_all.reshape(keys_split.shape),
        preferred_element_type=f32,
    )
    attended = (summed / row_sum[..., None]).astype(bf16)
    return (jnp.transpose(attended, (0, 3, 1, 2, 4)), top + jnp.log(row_sum), key_all, value_all)


def gathered_backward(
    query_grouped, grad_grouped, attended, log_sum, key_all, value_all, query_index, lowest_key
):
    scale = query_grouped.shape[-1] ** (-0.5)
    key_pos = jnp.arange(key_all.shape[1], dtype=jnp.int32)
    delta_rows = jnp.sum(grad_grouped.astype(f32) * attended.astype(f32), axis=-1)
    delta_stat = jnp.transpose(delta_rows, (0, 2, 3, 1))
    scores, allowed, keys_split = gathered_scores(
        query_grouped, key_all, query_index, lowest_key, key_pos
    )
    probs = jnp.where(allowed, jnp.exp(scores - log_sum[..., None]), 0.0)
    grad_probs = jnp.einsum(
        "sqhgd,skhd->shgqk",
        grad_grouped,
        value_all.reshape(keys_split.shape),
        preferred_element_type=f32,
    )
    grad_scores = (probs * (grad_probs - delta_stat[..., None])).astype(bf16)
    query_grad = (
        jnp.einsum("shgqk,skhd->sqhgd", grad_scores, keys_split, preferred_element_type=f32) * scale
    )
    key_grad = (
        jnp.einsum("shgqk,sqhgd->skhd", grad_scores, query_grouped, preferred_element_type=f32)
        * scale
    )
    value_grad = jnp.einsum(
        "shgqk,sqhgd->skhd", probs.astype(bf16), grad_grouped, preferred_element_type=f32
    )
    key_own, value_own = (
        lax.psum_scatter(part.reshape(key_all.shape), "ctx", scatter_dimension=1, tiled=True)
        for part in (key_grad, value_grad)
    )
    return (query_grad, key_own, value_own)


def split_dot(value, table):
    high = value.astype(bf16)
    low = (value - high.astype(f32)).astype(bf16)
    return dot_f32(high, table, 1, 0) + dot_f32(low, table, 1, 0)


def head_table(head_dim):
    row = lax.broadcasted_iota(jnp.int32, (lanes, lanes), 0) // head_dim
    col = lax.broadcasted_iota(jnp.int32, (lanes, lanes), 1) // head_dim
    return jnp.where(row == col, 1.0 / head_dim, 0.0).astype(bf16)


def swap_halves(value, head_dim):
    lane = lax.broadcasted_iota(jnp.int32, value.shape, 1)
    ahead = pltpu.roll(value, lanes - head_dim // 2, 1)
    behind = pltpu.roll(value, head_dim // 2, 1)
    return jnp.where(lane % head_dim < head_dim // 2, ahead, behind)


def front_kernel(
    head_dim,
    tokens_ref,
    gain_ref,
    query_w_ref,
    key_w_ref,
    value_w_ref,
    q_gain_ref,
    k_gain_ref,
    pos_ref,
    blocks_ref,
    normed_ref,
    query_ref,
    key_ref,
    cos_ref,
    sin_ref,
):
    seq_count, block_len = pos_ref.shape
    half_dim = head_dim // 2
    places = pos_ref[...]
    spare = jnp.zeros((8 - seq_count, block_len), f32)
    columns = jnp.concatenate([places.astype(f32), spare], axis=0).T
    lane_row = lax.broadcasted_iota(jnp.int32, (1, lanes), 1)
    exponent = (lane_row % half_dim).astype(f32) * (-2.0 / head_dim)
    frequency = jnp.exp(exponent * math.log(theta_base))
    sign = jnp.where(lane_row % head_dim < half_dim, -1.0, 1.0)
    for seq in range(seq_count):
        angles = columns[:, seq : seq + 1] * frequency
        cos_ref[seq * block_len : (seq + 1) * block_len, :] = jnp.cos(angles)
        sin_ref[seq * block_len : (seq + 1) * block_len, :] = jnp.sin(angles) * sign
    packed_pos = jnp.concatenate([places >> pos_shift, places & (pos_base - 1)], axis=1).astype(f32)
    fill = jnp.zeros((pos_rows - seq_count, packed_pos.shape[1]), f32)
    pos_tail = jnp.concatenate([packed_pos, fill], axis=0).astype(bf16)
    q_gain_row = jnp.concatenate([q_gain_ref[...]] * (lanes // head_dim), axis=1)
    k_gain_row = jnp.concatenate([k_gain_ref[...]] * (lanes // head_dim), axis=1)
    rows = tokens_ref[...].astype(f32)
    stat = lax.rsqrt(jnp.mean(rows * rows, axis=1, keepdims=True) + eps_norm)
    normed = (rows * stat * gain_ref[...]).astype(bf16)
    normed_ref[...] = normed
    query = dot_f32(normed, query_w_ref[...], 1, 0)
    key = dot_f32(normed, key_w_ref[...], 1, 0)
    value = dot_f32(normed, value_w_ref[...], 1, 0).astype(bf16).astype(f32)
    query_ref[...] = query
    key_ref[...] = key
    table = head_table(head_dim)
    cosine = cos_ref[...]
    sine = sin_ref[...]
    kv_heads = key.shape[1] // head_dim
    lane = lax.broadcasted_iota(jnp.int32, (rows.shape[0], lanes), 1)

    def turned(tile, gain):
        stat_val = lax.rsqrt(split_dot(tile * tile, table) + eps_norm)
        scaled = tile * stat_val * gain
        return scaled * cosine + swap_halves(scaled, head_dim) * sine

    for head in range(kv_heads):
        query_tile = turned(query[:, head * lanes : (head + 1) * lanes], q_gain_row).astype(bf16)
        pair = slice(head // 2 * lanes, (head // 2 + 1) * lanes)
        key_tile = turned(key[:, pair], k_gain_row)
        value_tile = value[:, pair]
        if head % 2 == 0:
            value_tile = pltpu.roll(value_tile, head_dim, 1)
        else:
            key_tile = pltpu.roll(key_tile, head_dim, 1)
        both = jnp.where(lane < head_dim, key_tile, value_tile).astype(bf16)
        row_count = rows.shape[0]
        blocks_ref[head, :row_count, :lanes] = query_tile
        blocks_ref[head, :row_count, lanes:] = both
        blocks_ref[head, row_count:, :] = pos_tail


def project_kernel(order_ref, *refs):
    count = len(refs) - 3
    block_refs = refs[:count]
    weight_ref, heads_ref, part_ref = refs[count:]
    for flip in range(count):
        heads_ref[order_ref[flip]] = block_refs[flip][...]
    total = None
    for head in range(count):
        found = dot_f32(heads_ref[head], weight_ref[:, head * lanes : (head + 1) * lanes], 1, 1)
        total = found if total is None else total + found
    part_ref[...] = total.astype(bf16)


def ffn_kernel(
    steps,
    tokens_ref,
    own_ref,
    other_ref,
    gain_ref,
    cot_ref,
    gate_ref,
    up_ref,
    down_ref,
    mixed_ref,
    normed_ref,
    hidden_ref,
    both_ref,
    ffn_ref,
    back_ref,
    ffn_acc,
    back_acc,
):
    step = pl.program_id(0)

    @pl.when(step == 0)
    def _():
        mixed = tokens_ref[...].astype(f32) + (own_ref[...].astype(f32) + other_ref[...].astype(f32))
        mixed_ref[...] = mixed
        stat = lax.rsqrt(jnp.mean(mixed * mixed, axis=1, keepdims=True) + eps_norm)
        normed_ref[...] = (mixed * stat * gain_ref[...]).astype(bf16)
        ffn_acc[...] = jnp.zeros_like(ffn_acc)
        back_acc[...] = jnp.zeros_like(back_acc)

    normed = normed_ref[...]
    gate = dot_f32(normed, gate_ref[...], 1, 0)
    up = dot_f32(normed, up_ref[...], 1, 0)
    grad = dot_f32(cot_ref[...], down_ref[...], 1, 0)
    sig = jax.nn.sigmoid(gate)
    silu = gate * sig
    hidden = (silu * up).astype(bf16)
    hidden_ref[...] = hidden
    grad_gate = (grad * up * (sig * (1.0 + gate * (1.0 - sig)))).astype(bf16)
    grad_up = (grad * silu).astype(bf16)
    both_ref[0, 0] = grad_gate
    both_ref[0, 1] = grad_up
    ffn_acc[...] += dot_f32(hidden, down_ref[...], 1, 1)
    back_acc[...] += dot_f32(grad_gate, gate_ref[...], 1, 1) + dot_f32(grad_up, up_ref[...], 1, 1)

    @pl.when(step == steps - 1)
    def _():
        ffn_ref[...] = ffn_acc[...].astype(bf16)
        back_ref[...] = back_acc[...].astype(bf16)


def ffn_call(tokens_in, own, other, gain, cot, w_gate, w_up, w_down):
    row_count, model_width = tokens_in.shape
    cols = w_gate.shape[1]
    half = cols // 2
    tile = half
    while tile > 384 and (tile // lanes) % 3 == 0:
        tile //= 3
    steps = cols // tile
    per_half = half // tile
    fixed = lambda *shape: pl.BlockSpec(shape, lambda step: (0,) * len(shape))
    moving = pl.BlockSpec((model_width, tile), lambda step: (0, step))
    rows_spec = fixed(row_count, model_width)
    return pl.pallas_call(
        functools.partial(ffn_kernel, steps),
        grid=(steps,),
        out_shape=(
            shape_of((row_count, model_width), f32),
            shape_of((row_count, model_width), bf16),
            shape_of((row_count, cols), bf16),
            shape_of((2, 2, row_count, half), bf16),
            shape_of((row_count, model_width), bf16),
            shape_of((row_count, model_width), bf16),
        ),
        in_specs=[rows_spec, rows_spec, rows_spec, fixed(1, model_width), rows_spec]
        + [moving] * 3,
        out_specs=(
            rows_spec,
            rows_spec,
            pl.BlockSpec((row_count, tile), lambda step: (0, step)),
            pl.BlockSpec(
                (1, 2, row_count, tile), lambda step: (step // per_half, 0, 0, step % per_half)
            ),
            rows_spec,
            rows_spec,
        ),
        scratch_shapes=[pltpu.VMEM((row_count, model_width), f32)] * 2,
        cost_estimate=pl.CostEstimate(
            flops=16 * row_count * model_width * cols,
            bytes_accessed=6 * model_width * cols,
            transcendentals=row_count * cols,
        ),
        name="ffn",
    )(tokens_in, own, other, gain, cot, w_gate, w_up, w_down)


def middle_kernel(
    mixed_ref,
    ffn_own_ref,
    ffn_other_ref,
    back_own_ref,
    back_other_ref,
    gain_ref,
    cot_ref,
    weight_ref,
    layer_ref,
    grad_ref,
    rounded_ref,
    blocks_ref,
    row_ref,
):
    mixed = mixed_ref[...]
    layer_ref[...] = mixed + (ffn_own_ref[...].astype(f32) + ffn_other_ref[...].astype(f32))
    found = back_own_ref[...].astype(f32) + back_other_ref[...].astype(f32)
    stat = lax.rsqrt(jnp.mean(mixed * mixed, axis=1, keepdims=True) + eps_norm)
    row_ref[...] = jnp.broadcast_to(
        jnp.sum(found * mixed * stat, axis=0, keepdims=True), row_ref.shape
    )
    grad = cot_ref[...].astype(f32) + rms_back(found * gain_ref[...], mixed, stat)
    grad_ref[...] = grad
    rounded = grad.astype(bf16)
    rounded_ref[...] = rounded
    attended = dot_f32(rounded, weight_ref[...], 1, 0).astype(bf16)
    for head in range(blocks_ref.shape[0]):
        blocks_ref[head] = attended[:, head * lanes : (head + 1) * lanes]


def turn_back_kernel(head_dim, order_ref, *refs):
    count = len(refs) - 14
    block_refs = refs[:count]
    (
        query_ref,
        key_ref,
        q_gain_ref,
        k_gain_ref,
        cos_ref,
        sin_ref,
        query_w_ref,
        key_w_ref,
        value_w_ref,
        raw_ref,
        part_ref,
        gain_row_ref,
        query_buf,
        pair_buf,
    ) = refs[count:]
    kv_heads = count
    for flip in range(count):
        query_buf[order_ref[flip]] = block_refs[flip][:, :lanes]
        pair_buf[order_ref[flip]] = block_refs[flip][:, lanes:]
    table = head_table(head_dim)
    cosine = cos_ref[...]
    sine = sin_ref[...]
    q_gain_row = jnp.concatenate([q_gain_ref[...]] * (lanes // head_dim), axis=1)
    k_gain_row = jnp.concatenate([k_gain_ref[...]] * (lanes // head_dim), axis=1)
    lane = lax.broadcasted_iota(jnp.int32, cosine.shape, 1)

    def back(grad_rot, raw, gain):
        grad_norm = grad_rot * cosine - swap_halves(grad_rot, head_dim) * sine
        stat = lax.rsqrt(split_dot(raw * raw, table) + eps_norm)
        gain_row = jnp.sum(grad_norm * raw * stat, axis=0, keepdims=True)
        grad_in = grad_norm * gain
        grad_raw = stat * grad_in - raw * stat**3 * split_dot(grad_in * raw, table)
        return (grad_raw.astype(bf16), gain_row)

    total = None
    gain_rows = [None, None]
    place = 0
    per_slot = raw_ref.shape[2] // lanes

    def emit(tile, weight, kind, gain_row):
        nonlocal total, place
        slot = place % per_slot
        raw_ref[place // per_slot, :, slot * lanes : (slot + 1) * lanes] = tile
        place += 1
        found = dot_f32(tile, weight, 1, 1)
        total = found if total is None else total + found
        if gain_row is not None:
            gain_rows[kind] = gain_row if gain_rows[kind] is None else gain_rows[kind] + gain_row

    for head in range(kv_heads):
        cols = slice(head * lanes, (head + 1) * lanes)
        tile, gain_row = back(query_buf[head].astype(f32), query_ref[:, cols], q_gain_row)
        emit(tile, query_w_ref[:, cols], 0, gain_row)
    for pair in range(kv_heads // 2):
        cols = slice(pair * lanes, (pair + 1) * lanes)
        first = pair_buf[2 * pair].astype(f32)
        second = pair_buf[2 * pair + 1].astype(f32)
        merged = jnp.where(lane < head_dim, first, pltpu.roll(second, head_dim, 1))
        tile, gain_row = back(merged, key_ref[:, cols], k_gain_row)
        emit(tile, key_w_ref[:, cols], 1, gain_row)
    for pair in range(kv_heads // 2):
        cols = slice(pair * lanes, (pair + 1) * lanes)
        first = pair_buf[2 * pair].astype(f32)
        second = pair_buf[2 * pair + 1].astype(f32)
        merged = jnp.where(lane < head_dim, pltpu.roll(first, head_dim, 1), second).astype(bf16)
        emit(merged, value_w_ref[:, cols], 1, None)
    part_ref[...] = total.astype(bf16)
    gain_row_ref[...] = jnp.concatenate(
        gain_rows + [jnp.zeros((6, lanes), f32)], axis=0
    )


def last_kernel(tokens_ref, grad_ref, own_ref, other_ref, gain_ref, out_ref, row_ref):
    rows = tokens_ref[...].astype(f32)
    stat = lax.rsqrt(jnp.mean(rows * rows, axis=1, keepdims=True) + eps_norm)
    found = own_ref[...].astype(f32) + other_ref[...].astype(f32)
    row_ref[...] = jnp.broadcast_to(
        jnp.sum(found * rows * stat, axis=0, keepdims=True), row_ref.shape
    )
    out_ref[...] = grad_ref[...] + rms_back(found * gain_ref[...], rows, stat)


everywhere = ("ctx", "seq")
plane = 4


def plane_gather(mine):
    near = [xor_swap(mine, everywhere, flip) for flip in range(1, plane)]
    far = [xor_swap(found, "tp", 1) for found in near]
    return (near, far)


def half_of(rows, core):
    half = rows.shape[0] // 2
    return lax.dynamic_slice_in_dim(rows, core * half, half, 0)


def window(cols):
    half = cols // 2
    width = min(half, -(-half // (2 * lanes)) * lanes)
    return (half, width)


def plane_exchange(take, place):
    parts = [take(place)]
    for flip in range(1, plane):
        parts.append(xor_swap(take(place ^ flip), everywhere, flip))
    return parts


def rows_kernel(scalars_ref, own_ref, *refs):
    near_refs = refs[: plane - 1]
    far_refs = refs[plane - 1 : 2 * plane - 2]
    col_refs = refs[2 * plane - 2 : 3 * plane - 2]
    out_ref, row_buf = refs[3 * plane - 2 :]
    step = pl.program_id(0)
    row_count = own_ref.shape[0]
    half = row_count // 2
    height = out_ref.shape[1]
    core = scalars_ref[0]
    start = pl.multiple_of((scalars_ref[1] + step * scalars_ref[2]) * height, height)
    cols = pl.ds(start, height)
    row_buf[:row_count, :] = own_ref[:, cols]
    for n in range(plane - 1):
        base = (n + 1) * row_count
        near_rows = pl.ds(pl.multiple_of(base + core * half, half), half)
        far_rows = pl.ds(pl.multiple_of(base + (1 - core) * half, half), half)
        row_buf[near_rows, :] = near_refs[n][:, cols]
        row_buf[far_rows, :] = far_refs[n][:, cols]
    total = None
    for n in range(plane):
        found = dot_f32(row_buf[n * row_count : (n + 1) * row_count, :], col_refs[n][...], 0, 0)
        total = found if total is None else total + found
    out_ref[0] = total.astype(out_ref.dtype)


def rows_call(row_pieces, col_parts, scalars, steps, height, dtype):
    own, near, far, slot = row_pieces
    row_count, model_width = own.shape
    half = row_count // 2
    width = col_parts[0].shape[1]
    fixed = lambda *shape: pl.BlockSpec(shape, lambda step: (0,) * len(shape))
    return pl.pallas_call(
        rows_kernel,
        grid=(steps,),
        out_shape=shape_of((steps, height, width), dtype),
        in_specs=[smem_spec(), fixed(row_count, model_width)]
        + [pl.BlockSpec((half, model_width), lambda step: (0, slot))] * (2 * plane - 2)
        + [fixed(row_count, width)] * plane,
        out_specs=pl.BlockSpec((1, height, width), lambda step: (step, 0, 0)),
        scratch_shapes=[pltpu.VMEM((plane * row_count, height), bf16)],
        cost_estimate=pl.CostEstimate(
            flops=2 * plane * row_count * steps * height * width,
            bytes_accessed=2 * plane * row_count * (model_width + width)
            + 4 * steps * height * width,
            transcendentals=0,
        ),
        name="rows",
    )(scalars, own, *near, *far, *col_parts)


class Halving:
    def __init__(self, index, core, total, model_width):
        self.blocks = total // plane
        self.bits = self.blocks.bit_length() - 1
        self.block_index = index // plane
        self.core = core
        self.fine = model_width // self.blocks % lanes == 0
        self.order = list(range(self.bits))
        if self.fine:
            self.steps, self.height, self.scale = self.blocks // 2, model_width // self.blocks, 2
        else:
            self.order.reverse()
            self.steps, self.height, self.scale = 1, model_width // 2, 1
        self.first = (self.block_index >> self.order[0]) & 1

    def rows(self, row_pieces, col_parts, mine):
        bit = self.first if mine else 1 - self.first
        scalars = jnp.stack([self.core, bit, jnp.int32(self.scale)]).astype(jnp.int32)
        dtype = f32 if mine else bf16
        return rows_call(row_pieces, col_parts, scalars, self.steps, self.height, dtype)

    def split(self, value):
        shaped = value.reshape(self.steps, 2, self.height, -1)
        return (pick(shaped, 1 - self.first, 1).astype(bf16), pick(shaped, self.first, 1))

    def start(self, sent):
        return xor_swap(sent, everywhere, plane << self.order[0])

    def finish(self, kept, found):
        kept = kept + found.astype(f32)
        width = kept.shape[2]
        for turn, bit in enumerate(self.order[1:]):
            own_bit = (self.block_index >> bit) & 1
            if self.fine:
                shaped = kept.reshape(self.steps >> (turn + 1), 2, self.height, width)
            else:
                shaped = kept.reshape(1, 2, -1, width)
            sent = pick(shaped, 1 - own_bit, 1).astype(bf16)
            kept = pick(shaped, own_bit, 1)
            found = xor_swap(sent, everywhere, plane << bit)
            kept = kept + found.astype(f32)
        return kept.reshape(-1, width)


def return_rows(summed, place):
    width = summed.shape[1]
    shaped = summed.reshape(plane, -1, width)
    found = [pick(shaped, place)]
    for flip in range(1, plane):
        sent = pick(shaped, place ^ flip).astype(bf16)
        found.append(xor_swap(sent, everywhere, flip))
    return found


def assemble_kernel(moves, order_ref, *refs):
    part_refs = refs[:plane]
    out_refs = refs[plane:]
    for flip in range(plane):
        for member in range(plane):

            @pl.when(order_ref[flip] == member)
            def _():
                for out, out_start, start, width in moves[member]:
                    out_refs[out][:, out_start : out_start + width] = part_refs[flip][
                        :, start : start + width
                    ].astype(f32)


def assemble(parts, order, moves, widths):
    height = parts[0].shape[0]
    return whole_call(
        functools.partial(assemble_kernel, moves),
        [shape_of((height, width), f32) for width in widths],
        parts,
        scalars=(order,),
    )


def shards(
    tokens,
    positions,
    attn_gain,
    ffn_gain,
    q_gain,
    k_gain,
    w_query,
    w_key,
    w_value,
    w_out,
    w_gate,
    w_up,
    w_down,
    cotangent,
):
    seq_count, block_len, model_width = tokens.shape
    row_count = seq_count * block_len
    head_dim = q_gain.shape[0]
    q_heads = w_query.shape[1] // head_dim
    kv_heads = w_key.shape[1] // head_dim
    key_width = kv_heads * head_dim
    query_width = q_heads * head_dim
    group_size = q_heads // kv_heads
    hidden_width = w_gate.shape[1]
    ctx_size = lax.axis_size("ctx")
    total = ctx_size * lax.axis_size("seq")
    here_index = lax.axis_index("ctx")
    index = lax.axis_index(everywhere)
    core = lax.axis_index("tp")
    place = index % plane
    by_head = ctx_size == 2 * kv_heads
    natural = jnp.arange(kv_heads, dtype=jnp.int32)
    level_order = (here_index // 2) ^ natural if by_head else natural
    order = jnp.concatenate([level_order, (here_index % 2)[None]]).astype(jnp.int32)
    plane_order = place ^ jnp.arange(plane, dtype=jnp.int32)
    rows_bf = shape_of((row_count, model_width), bf16)
    rows_f32 = shape_of((row_count, model_width), f32)
    halving = Halving(index, core, total, model_width)

    cot_rows = cotangent.reshape(row_count, model_width)
    token_rows = tokens.reshape(row_count, model_width)

    pack_width = 2 * lanes
    q_gain_row = q_gain[None, :]
    k_gain_row = k_gain[None, :]
    attn_gain_row = attn_gain[None, :]
    ffn_gain_row = ffn_gain[None, :]

    packed, normed_one, query_raw, key_raw, cosine, sine = whole_call(
        functools.partial(front_kernel, head_dim),
        [
            shape_of((kv_heads, row_count + pos_rows, pack_width), bf16),
            rows_bf,
            shape_of((row_count, query_width), f32),
            shape_of((row_count, key_width), f32),
            shape_of((row_count, lanes), f32),
            shape_of((row_count, lanes), f32),
        ],
        [
            token_rows,
            attn_gain_row,
            w_query,
            w_key,
            w_value,
            q_gain_row,
            k_gain_row,
            positions,
        ],
        flops=2 * row_count * model_width * (query_width + 2 * key_width),
    )

    if by_head:
        blocks = z_exchange(packed)
        pairs = [xor_swap(block[:row_count, lanes:], "ctx", 1) for block in blocks]
        out_heads, log_sum = head_forward(order, blocks, pairs, seq_count, head_dim)
        out_blocks = z_exchange(out_heads)
    else:
        flat = packed[:, :row_count].reshape(kv_heads, seq_count, block_len, pack_width)
        flat = jnp.transpose(flat, (1, 2, 0, 3))
        query_grouped = flat[..., :lanes].reshape(
            seq_count, block_len, kv_heads, group_size, head_dim
        )
        query_index = here_index * block_len + jnp.arange(block_len, dtype=jnp.int32)
        lowest_key = query_index[None, :] - positions
        attended_grouped, log_sum, key_all, value_all = gathered_forward(
            query_grouped,
            flat[..., lanes : lanes + head_dim].reshape(seq_count, block_len, key_width),
            flat[..., lanes + head_dim :].reshape(seq_count, block_len, key_width),
            query_index,
            lowest_key,
        )
        out_blocks = list(
            jnp.transpose(attended_grouped, (2, 0, 1, 3, 4)).reshape(kv_heads, row_count, lanes)
        )

    early_half = jnp.concatenate([half_of(cot_rows, core), half_of(normed_one, core)], axis=1)
    early_near, early_far = plane_gather(early_half)
    cot_pieces = (cot_rows, early_near, early_far, 0)
    one_pieces = (normed_one, early_near, early_far, 1)

    heads, attn_part = whole_call(
        project_kernel,
        [shape_of((kv_heads, row_count, lanes), bf16), rows_bf],
        [*out_blocks, w_out],
        scalars=(order,),
        flops=2 * row_count * model_width * query_width,
    )
    mixed, normed_two, hidden, both_pre, ffn_part, back_part = ffn_call(
        token_rows,
        attn_part,
        named_swap(attn_part),
        ffn_gain_row,
        cot_rows,
        w_gate,
        w_up,
        w_down,
    )
    ffn_other = named_swap(ffn_part)
    back_other = named_swap(back_part)
    half, width = window(hidden_width)
    both_flat = both_pre.reshape(plane, row_count, half)
    both_plane = plane_exchange(lambda member: pick(both_flat, member), place)
    two_near, two_far = plane_gather(half_of(normed_two, core))
    two_pieces = (normed_two, two_near, two_far, 0)

    def take_hidden(member):
        start = (member % 2) * half + (member // 2) * (half - width)
        return lax.dynamic_slice_in_dim(hidden, start, width, 1)

    hidden_plane = plane_exchange(take_hidden, place)

    layer_output, grad_mixed, grad_mixed_bf, grad_blocks, ffn_row = whole_call(
        middle_kernel,
        [
            rows_f32,
            rows_f32,
            rows_bf,
            shape_of((kv_heads, row_count, lanes), bf16),
            shape_of((8, model_width), f32),
        ],
        [
            mixed,
            ffn_part,
            ffn_other,
            back_part,
            back_other,
            ffn_gain_row,
            cot_rows,
            w_out,
        ],
        flops=2 * row_count * model_width * query_width,
    )

    if by_head:
        grads = z_exchange(grad_blocks)
        query_grads, own_grads, other_grads = head_backward(
            order, blocks, pairs, grads, out_heads, log_sum, seq_count, head_dim
        )
        (packed_grads,) = whole_call(
            merge_kernel,
            [shape_of((kv_heads, row_count, pack_width), bf16)],
            [query_grads, own_grads, named_swap(other_grads, "ctx")],
        )
        returned = z_exchange(packed_grads)
    else:
        grad_grouped = jnp.transpose(
            grad_blocks.reshape(kv_heads, seq_count, block_len, group_size, head_dim),
            (1, 2, 0, 3, 4),
        )
        query_grad, key_grad_own, value_grad_own = gathered_backward(
            query_grouped,
            grad_grouped,
            attended_grouped,
            log_sum,
            key_all,
            value_all,
            query_index,
            lowest_key,
        )
        shaped = lambda grad: grad.reshape(seq_count, block_len, kv_heads, -1)
        returned = jnp.concatenate(
            [shaped(query_grad), shaped(key_grad_own), shaped(value_grad_own)], axis=-1
        ).astype(bf16)
        returned = list(
            jnp.transpose(returned, (2, 0, 1, 3)).reshape(kv_heads, row_count, pack_width)
        )

    both_found = halving.start(halving.rows(two_pieces, both_plane, False))
    both_kept = halving.rows(two_pieces, both_plane, True)
    down_found = halving.start(halving.rows(cot_pieces, hidden_plane, False))
    down_kept = halving.rows(cot_pieces, hidden_plane, True)

    mixed_half = half_of(grad_mixed_bf, core)
    mixed_near, mixed_far = plane_gather(mixed_half)
    mixed_pieces = (grad_mixed_bf, mixed_near, mixed_far, 0)
    attended_plane = plane_exchange(lambda member: pick(heads, member), place)

    raw_width = (query_width + 2 * key_width) // plane
    grad_raw, one_part, head_rows = whole_call(
        functools.partial(turn_back_kernel, head_dim),
        [
            shape_of((plane, row_count, raw_width), bf16),
            rows_bf,
            shape_of((8, lanes), f32),
        ],
        [
            *returned,
            query_raw,
            key_raw,
            q_gain_row,
            k_gain_row,
            cosine,
            sine,
            w_query,
            w_key,
            w_value,
        ],
        scalars=(order,),
        scratch=[
            pltpu.VMEM((kv_heads, row_count, lanes), bf16),
            pltpu.VMEM((kv_heads, row_count, lanes), bf16),
        ],
        flops=2 * row_count * model_width * (query_width + 2 * key_width),
    )
    raw_plane = plane_exchange(lambda member: pick(grad_raw, member), place)
    input_grad, attn_row = whole_call(
        last_kernel,
        [rows_f32, shape_of((8, model_width), f32)],
        [token_rows, grad_mixed, one_part, named_swap(one_part), attn_gain_row],
    )

    tiles = model_width // head_dim
    folded = head_rows[:2].reshape(2, lanes // head_dim, head_dim).sum(axis=1)
    gain_rows = jnp.concatenate([ffn_row[:1], attn_row[:1], jnp.tile(folded, (1, tiles))], axis=0)
    gain_cols = jnp.pad(gain_rows.T, ((0, 0), (0, lanes - 4)))
    gain_sent, gain_kept = halving.split(gain_cols)
    out_width = lanes
    late_sent = jnp.concatenate(
        [
            halving.rows(mixed_pieces, attended_plane, False),
            halving.rows(one_pieces, raw_plane, False),
            gain_sent,
        ],
        axis=2,
    )
    late_found = halving.start(late_sent)
    late_kept = jnp.concatenate(
        [
            halving.rows(mixed_pieces, attended_plane, True),
            halving.rows(one_pieces, raw_plane, True),
            gain_kept,
        ],
        axis=2,
    )

    both_sum = halving.finish(both_kept, both_found)
    down_sum = halving.finish(down_kept, down_found)
    wide_parts = return_rows(jnp.concatenate([both_sum, down_sum], axis=1), place)
    skip = 2 * width - half
    wide_moves = []
    for member in range(plane):
        far_side = member // 2
        down_start = half * (member % 2) + far_side * width
        wide_moves.append(
            [
                (member % 2, half * far_side, 0, half),
                (2, down_start, half + far_side * skip, width - far_side * skip),
            ]
        )
    wgate_grad, wup_grad, wdown_grad = assemble(
        wide_parts, plane_order, wide_moves, [hidden_width] * 3
    )

    late_sum = halving.finish(late_kept, late_found)
    late_parts = return_rows(late_sum, place)
    late_moves = []
    for member in range(plane):
        moves = [(0, member * out_width, 0, out_width)]
        for out, begin, size in (
            (1, 0, query_width),
            (2, query_width, key_width),
            (3, query_width + key_width, key_width),
        ):
            low = max(begin, member * raw_width)
            high = min(begin + size, (member + 1) * raw_width)
            if low < high:
                moves.append((out, low - begin, out_width + low - member * raw_width, high - low))
        late_moves.append(moves)
    wo_grad, wq_grad, wk_grad, wv_grad = assemble(
        late_parts, plane_order, late_moves, [query_width, query_width, key_width, key_width]
    )
    gain_start = out_width + raw_width
    gain_sums = sum(part[:, gain_start : gain_start + 4].astype(f32) for part in late_parts)
    ffngain_grad = gain_sums[:, 0]
    attngain_grad = gain_sums[:, 1]
    head_gains = lax.reduce_precision(gain_sums[:, 2:4], 8, 23)
    head_gains = head_gains + xor_swap(head_gains, "tp", 1)
    if gain_sums.shape[0] < head_dim:
        whole_gains = lax.all_gather(head_gains, everywhere, axis=0, tiled=True)[:head_dim]
    else:
        whole_gains = head_gains[:head_dim]
    return (
        layer_output.reshape(seq_count, block_len, model_width),
        input_grad.reshape(seq_count, block_len, model_width),
        wq_grad,
        wk_grad,
        wv_grad,
        wo_grad,
        wgate_grad,
        wup_grad,
        wdown_grad,
        attngain_grad,
        ffngain_grad,
        whole_gains[:, 0],
        whole_gains[:, 1],
    )


def solution(mesh):
    placed = (
        P("seq", "ctx", None),
        P("seq", "ctx"),
        P(),
        P(),
        P(),
        P(),
        P(None, "tp"),
        P(None, "tp"),
        P(None, "tp"),
        P(None, "tp"),
        P(None, "tp"),
        P(None, "tp"),
        P(None, "tp"),
        P("seq", "ctx", None),
    )
    return jax.shard_map(
        shards,
        mesh=mesh,
        in_specs=placed,
        out_specs=(
            P("seq", "ctx", None),
            P("seq", "ctx", None),
            P(("ctx", "seq"), "tp"),
            P(("ctx", "seq"), "tp"),
            P(("ctx", "seq"), "tp"),
            P(("ctx", "seq"), "tp"),
            P(("ctx", "seq"), "tp"),
            P(("ctx", "seq"), "tp"),
            P(("ctx", "seq"), "tp"),
            P(("ctx", "seq")),
            P(("ctx", "seq")),
            P(),
            P(),
        ),
        check_vma=False,
    )
```

```python
import functools
import math

import jax
import jax.numpy as jnp
from jax import lax
from jax.experimental import pallas as pl
from jax.experimental.pallas import tpu as pltpu
from jax.sharding import PartitionSpec as P


eps_norm = 1e-05
theta_base = 1000000.0
negative = -1e30
bf16 = jnp.bfloat16
f32 = jnp.float32
lanes = 128
pos_shift = 7
pos_base = 1 << pos_shift
pos_rows = 16
ffn_tile = 256
vmem_limit = 28 * 1024 * 1024


def dot_f32(lhs, rhs, lhs_dim, rhs_dim):
    return lax.dot_general(
        lhs, rhs, (((lhs_dim,), (rhs_dim,)), ((), ())), preferred_element_type=f32
    )


def rms_back(grad_in, values, stat_val):
    return stat_val * grad_in - values * stat_val**3 * jnp.mean(
        grad_in * values, axis=-1, keepdims=True
    )


def xor_swap(value, axis, flip):
    size = lax.axis_size(axis)
    return lax.ppermute(value, axis, [(index, index ^ flip) for index in range(size)])


def named_swap(value, axis="tp"):
    return xor_swap(value, axis, 1)


def level_swap(parts):
    count = len(parts)
    found = [parts[0]] + [None] * (count - 1)
    for flip in range(count - 1, 0, -1):
        found[flip] = xor_swap(parts[flip], "ctx", 2 * flip)
    return found


def side_swap(parts):
    return [xor_swap(part, "ctx", 1) for part in parts]


def plane_swap(parts):
    return [parts[0]] + [
        xor_swap(parts[flip], everywhere, flip) for flip in range(1, len(parts))
    ]


everywhere = ("ctx", "seq")
plane = 4
at_level, at_side, at_core, at_place, at_bits = range(5)


def fill_heads(ref, place, rows, head_dim):
    tokens_count = rows.shape[0]
    for head in range(rows.shape[1] // head_dim):
        ref[place, head * tokens_count : (head + 1) * tokens_count, :] = rows[
            :, head * head_dim : (head + 1) * head_dim
        ]


def gather_blocks(
    info_ref, block_refs, own_refs, other_refs, query_buf, key_buf, value_buf, low_buf
):
    count = len(block_refs)
    seq_count = key_buf.shape[0]
    head_dim = key_buf.shape[2]
    block_len = own_refs[0].shape[0] // seq_count
    side = info_ref[at_side]
    for flip in range(count):
        level = info_ref[at_level] ^ flip
        block_ref = block_refs[flip]
        own_start = pl.multiple_of((level * 2 + side) * block_len, block_len)
        other_start = pl.multiple_of((level * 2 + 1 - side) * block_len, block_len)
        tail = block_ref[seq_count * block_len :, :].astype(f32)
        found = tail[:seq_count] * pos_base + tail[seq_count : 2 * seq_count]
        token = own_start + lax.broadcasted_iota(jnp.int32, (1, block_len), 1)
        for seq in range(seq_count):
            part = slice(seq * block_len, (seq + 1) * block_len)
            fill_heads(query_buf, seq * count + level, block_ref[part, :], head_dim)
            for refs, start in ((own_refs, own_start), (other_refs, other_start)):
                rows = pl.ds(start, block_len)
                key_buf[seq, rows, :] = refs[flip][part, :head_dim]
                value_buf[seq, rows, :] = refs[flip][part, head_dim:]
            low_buf[seq * count + level] = token - found[seq : seq + 1].astype(jnp.int32)


def visible(info_ref, low_row, level, key_count, block_len, width):
    low = jnp.concatenate([low_row] * (width // block_len), axis=1)
    shape = (key_count, low.shape[1])
    key_index = lax.broadcasted_iota(jnp.int32, shape, 0)
    lane = lax.broadcasted_iota(jnp.int32, shape, 1) % block_len
    query_index = (level * 2 + info_ref[at_side]) * block_len + lane
    return (key_index <= query_index) & (key_index >= low)


def unfold(turned, block_len):
    parts = [
        turned[:, start : start + block_len] for start in range(0, turned.shape[1], block_len)
    ]
    return jnp.concatenate(parts, axis=0).T


def attend_kernel(count, *refs):
    info_ref = refs[0]
    sources = [refs[1 + n * count : 1 + (n + 1) * count] for n in range(3)]
    out_ref, lse_ref = refs[1 + 3 * count : 3 + 3 * count]
    send_refs = refs[3 + 3 * count : 3 + 4 * count]
    query_buf, key_buf, value_buf, low_buf = refs[3 + 4 * count :]
    gather_blocks(info_ref, *sources, query_buf, key_buf, value_buf, low_buf)
    seq_count, _, head_dim = key_buf.shape
    block_len = low_buf.shape[2]
    for seq in range(seq_count):
        for level in range(count):
            place = seq * count + level
            key_count = 2 * block_len * (level + 1)
            query = query_buf[place]
            scores = dot_f32(key_buf[seq, :key_count, :], query, 1, 1) * head_dim ** (-0.5)
            allowed = visible(info_ref, low_buf[place], level, key_count, block_len, query.shape[0])
            scores = jnp.where(allowed, scores, negative)
            top = jnp.max(scores, axis=0, keepdims=True)
            weights = jnp.exp(scores - top)
            row_sum = jnp.sum(weights, axis=0, keepdims=True)
            lse_ref[place : place + 1, :] = top + jnp.log(row_sum)
            turned = dot_f32(value_buf[seq, :key_count, :], weights.astype(bf16), 0, 0) / row_sum
            out_ref[level, seq * block_len : (seq + 1) * block_len, :] = unfold(
                turned, block_len
            ).astype(bf16)
    for flip in range(count):
        send_refs[flip][...] = out_ref[info_ref[at_level] ^ flip]


def attend_back_kernel(count, *refs):
    info_ref = refs[0]
    sources = [refs[1 + n * count : 1 + (n + 1) * count] for n in range(3)]
    grad_refs = refs[1 + 3 * count : 1 + 4 * count]
    out_ref, lse_ref = refs[1 + 4 * count : 3 + 4 * count]
    query_refs = refs[3 + 4 * count : 3 + 5 * count]
    own_refs = refs[3 + 5 * count : 3 + 6 * count]
    other_refs = refs[3 + 6 * count : 3 + 7 * count]
    (
        query_buf,
        key_buf,
        value_buf,
        low_buf,
        grad_buf,
        key_acc,
        value_acc,
        query_grad,
    ) = refs[3 + 7 * count :]
    gather_blocks(info_ref, *sources, query_buf, key_buf, value_buf, low_buf)
    seq_count, _, head_dim = key_buf.shape
    block_len = low_buf.shape[2]
    group = lanes // head_dim
    for flip in range(count):
        for seq in range(seq_count):
            rows = grad_refs[flip][seq * block_len : (seq + 1) * block_len, :]
            level = info_ref[at_level] ^ flip
            fill_heads(grad_buf, seq * count + level, rows, head_dim)
    key_acc[...] = jnp.zeros_like(key_acc)
    value_acc[...] = jnp.zeros_like(value_acc)
    scale = head_dim ** (-0.5)
    ones_row = jnp.ones((8, head_dim), f32)
    for seq in range(seq_count):
        for level in range(count):
            place = seq * count + level
            key_count = 2 * block_len * (level + 1)
            keys = key_buf[seq, :key_count, :]
            query = query_buf[place]
            grad = grad_buf[place]
            rows = out_ref[level, seq * block_len : (seq + 1) * block_len, :]
            out = jnp.concatenate(
                [rows[:, head * head_dim : (head + 1) * head_dim] for head in range(group)], axis=0
            )
            delta = lax.dot_general(
                ones_row,
                grad.astype(f32) * out.astype(f32),
                (((1,), (1,)), ((), ())),
                precision=lax.Precision.HIGHEST,
                preferred_element_type=f32,
            )[:1, :]
            scores = dot_f32(keys, query, 1, 1) * scale
            allowed = visible(info_ref, low_buf[place], level, key_count, block_len, query.shape[0])
            probs = jnp.where(allowed, jnp.exp(scores - lse_ref[place : place + 1, :]), 0.0)
            grad_probs = dot_f32(value_buf[seq, :key_count, :], grad, 1, 1)
            grad_scores = (probs * (grad_probs - delta)).astype(bf16)
            value_acc[seq, :key_count, :] += dot_f32(probs.astype(bf16), grad, 1, 0)
            key_acc[seq, :key_count, :] += dot_f32(grad_scores, query, 1, 0)
            turned = dot_f32(keys, grad_scores, 0, 0) * scale
            query_grad[level, seq * block_len : (seq + 1) * block_len, :] = unfold(
                turned, block_len
            ).astype(bf16)
    side = info_ref[at_side]
    for flip in range(count):
        level = info_ref[at_level] ^ flip
        query_refs[flip][...] = query_grad[level]
        for seq in range(seq_count):
            part = slice(seq * block_len, (seq + 1) * block_len)
            for place, ref in ((side, own_refs[flip]), (1 - side, other_refs[flip])):
                start = pl.multiple_of((2 * level + place) * block_len, block_len)
                rows = pl.ds(start, block_len)
                both = [key_acc[seq, rows, :] * scale, value_acc[seq, rows, :]]
                ref[part, :] = jnp.concatenate(both, axis=1).astype(ref.dtype)


def merge_kernel(count, *refs):
    for flip in range(count):
        own_ref, other_ref, out_ref = refs[flip::count]
        out_ref[...] = (own_ref[...] + other_ref[...].astype(f32)).astype(bf16)


def smem_spec():
    return pl.BlockSpec(memory_space=pltpu.SMEM)


def vmem_spec():
    return pl.BlockSpec(memory_space=pltpu.VMEM)


def shape_of(shape, dtype):
    return jax.ShapeDtypeStruct(shape, dtype)


def whole_call(kernel, outs, args, scalars=(), scratch=(), flops=0):
    moved = sum(arg.size * arg.dtype.itemsize for arg in args)
    moved += sum(out.size * jnp.dtype(out.dtype).itemsize for out in outs)
    return pl.pallas_call(
        kernel,
        out_shape=tuple(outs),
        in_specs=[smem_spec()] * len(scalars) + [vmem_spec()] * len(args),
        out_specs=tuple(vmem_spec() for _ in outs),
        scratch_shapes=list(scratch),
        cost_estimate=pl.CostEstimate(flops=flops, bytes_accessed=moved, transcendentals=0),
        compiler_params=pltpu.CompilerParams(vmem_limit_bytes=vmem_limit),
    )(*scalars, *args)


def head_scratch(seq_count, count, block_len, head_dim):
    total = 2 * count * block_len
    heads_rows = lanes // head_dim * block_len
    return [
        pltpu.VMEM((seq_count * count, heads_rows, head_dim), bf16),
        pltpu.VMEM((seq_count, total, head_dim), bf16),
        pltpu.VMEM((seq_count, total, head_dim), bf16),
        pltpu.VMEM((seq_count * count, 1, block_len), jnp.int32),
    ]


def head_forward(info, sources, seq_count, head_dim):
    count = len(sources) // 3
    row_count = sources[-1].shape[0]
    block_len = row_count // seq_count
    heads_rows = lanes // head_dim * block_len
    found = whole_call(
        functools.partial(attend_kernel, count),
        [
            shape_of((count, row_count, lanes), bf16),
            shape_of((seq_count * count, heads_rows), f32),
        ]
        + [shape_of((row_count, lanes), bf16)] * count,
        sources,
        scalars=(info,),
        scratch=head_scratch(seq_count, count, block_len, head_dim),
        flops=8 * row_count * row_count * count * count * lanes,
    )
    return (found[0], found[1], found[2:])


def head_backward(info, sources, grads, out, log_sum, seq_count, head_dim):
    count = len(sources) // 3
    row_count = sources[-1].shape[0]
    block_len = row_count // seq_count
    heads_rows = lanes // head_dim * block_len
    total = 2 * count * block_len
    found = whole_call(
        functools.partial(attend_back_kernel, count),
        [shape_of((row_count, lanes), bf16)] * count
        + [shape_of((row_count, lanes), f32)] * count
        + [shape_of((row_count, lanes), bf16)] * count,
        [*sources, *grads, out, log_sum],
        scalars=(info,),
        scratch=head_scratch(seq_count, count, block_len, head_dim)
        + [
            pltpu.VMEM((seq_count * count, heads_rows, head_dim), bf16),
            pltpu.VMEM((seq_count, total, head_dim), f32),
            pltpu.VMEM((seq_count, total, head_dim), f32),
            pltpu.VMEM((count, row_count, lanes), bf16),
        ],
        flops=20 * row_count * row_count * count * count * lanes,
    )
    return (found[:count], found[count : 2 * count], found[2 * count :])


def gathered_scores(query_grouped, key_piece, query_pos, lowest_pos, key_pos):
    head_dim = query_grouped.shape[-1]
    keys_split = key_piece.reshape(
        key_piece.shape[0], key_piece.shape[1], query_grouped.shape[2], head_dim
    )
    scores = jnp.einsum(
        "sqhgd,skhd->shgqk", query_grouped, keys_split, preferred_element_type=f32
    ) * head_dim ** (-0.5)
    allowed = (key_pos[None, None, :] <= query_pos[None, :, None]) & (
        key_pos[None, None, :] >= lowest_pos[:, :, None]
    )
    allowed = allowed[:, None, None, :, :]
    return (jnp.where(allowed, scores, negative), allowed, keys_split)


def gathered_forward(query_grouped, key_rows, value_rows, query_index, lowest_key):
    key_all = lax.all_gather(key_rows, "ctx", axis=1, tiled=True)
    value_all = lax.all_gather(value_rows, "ctx", axis=1, tiled=True)
    key_pos = jnp.arange(key_all.shape[1], dtype=jnp.int32)
    scores, allowed, keys_split = gathered_scores(
        query_grouped, key_all, query_index, lowest_key, key_pos
    )
    top = jnp.max(scores, axis=-1)
    weights = jnp.where(allowed, jnp.exp(scores - top[..., None]), 0.0)
    row_sum = jnp.sum(weights, axis=-1)
    summed = jnp.einsum(
        "shgqk,skhd->shgqd",
        weights.astype(bf16),
        value_all.reshape(keys_split.shape),
        preferred_element_type=f32,
    )
    attended = (summed / row_sum[..., None]).astype(bf16)
    return (jnp.transpose(attended, (0, 3, 1, 2, 4)), top + jnp.log(row_sum), key_all, value_all)


def gathered_backward(
    query_grouped, grad_grouped, attended, log_sum, key_all, value_all, query_index, lowest_key
):
    scale = query_grouped.shape[-1] ** (-0.5)
    key_pos = jnp.arange(key_all.shape[1], dtype=jnp.int32)
    delta_rows = jnp.sum(grad_grouped.astype(f32) * attended.astype(f32), axis=-1)
    delta_stat = jnp.transpose(delta_rows, (0, 2, 3, 1))
    scores, allowed, keys_split = gathered_scores(
        query_grouped, key_all, query_index, lowest_key, key_pos
    )
    probs = jnp.where(allowed, jnp.exp(scores - log_sum[..., None]), 0.0)
    grad_probs = jnp.einsum(
        "sqhgd,skhd->shgqk",
        grad_grouped,
        value_all.reshape(keys_split.shape),
        preferred_element_type=f32,
    )
    grad_scores = (probs * (grad_probs - delta_stat[..., None])).astype(bf16)
    query_grad = (
        jnp.einsum("shgqk,skhd->sqhgd", grad_scores, keys_split, preferred_element_type=f32) * scale
    )
    key_grad = (
        jnp.einsum("shgqk,sqhgd->skhd", grad_scores, query_grouped, preferred_element_type=f32)
        * scale
    )
    value_grad = jnp.einsum(
        "shgqk,sqhgd->skhd", probs.astype(bf16), grad_grouped, preferred_element_type=f32
    )
    key_own, value_own = (
        lax.psum_scatter(part.reshape(key_all.shape), "ctx", scatter_dimension=1, tiled=True)
        for part in (key_grad, value_grad)
    )
    return (query_grad, key_own, value_own)


def split_dot(value, table):
    high = value.astype(bf16)
    low = (value - high.astype(f32)).astype(bf16)
    return dot_f32(high, table, 1, 0) + dot_f32(low, table, 1, 0)


def head_table(head_dim):
    row = lax.broadcasted_iota(jnp.int32, (lanes, lanes), 0) // head_dim
    col = lax.broadcasted_iota(jnp.int32, (lanes, lanes), 1) // head_dim
    return jnp.where(row == col, 1.0 / head_dim, 0.0).astype(bf16)


def swap_halves(value, head_dim):
    lane = lax.broadcasted_iota(jnp.int32, value.shape, 1)
    ahead = pltpu.roll(value, lanes - head_dim // 2, 1)
    behind = pltpu.roll(value, head_dim // 2, 1)
    return jnp.where(lane % head_dim < head_dim // 2, ahead, behind)


def front_kernel(
    head_dim,
    info_ref,
    tokens_ref,
    cot_ref,
    gain_ref,
    query_w_ref,
    key_w_ref,
    value_w_ref,
    q_gain_ref,
    k_gain_ref,
    pos_ref,
    normed_ref,
    early_ref,
    query_ref,
    key_ref,
    cos_ref,
    sin_ref,
    *refs,
):
    count = (len(refs) - 2) // 2
    block_refs = refs[:count]
    pair_refs = refs[count : 2 * count]
    blocks_ref, pairs_ref = refs[2 * count :]
    seq_count, block_len = pos_ref.shape
    half_dim = head_dim // 2
    places = pos_ref[...]
    spare = jnp.zeros((8 - seq_count, block_len), f32)
    columns = jnp.concatenate([places.astype(f32), spare], axis=0).T
    lane_row = lax.broadcasted_iota(jnp.int32, (1, lanes), 1)
    exponent = (lane_row % half_dim).astype(f32) * (-2.0 / head_dim)
    frequency = jnp.exp(exponent * math.log(theta_base))
    sign = jnp.where(lane_row % head_dim < half_dim, -1.0, 1.0)
    for seq in range(seq_count):
        angles = columns[:, seq : seq + 1] * frequency
        cos_ref[seq * block_len : (seq + 1) * block_len, :] = jnp.cos(angles)
        sin_ref[seq * block_len : (seq + 1) * block_len, :] = jnp.sin(angles) * sign
    packed_pos = jnp.concatenate([places >> pos_shift, places & (pos_base - 1)], axis=0).astype(f32)
    fill = jnp.zeros((pos_rows - 2 * seq_count, block_len), f32)
    pos_tail = jnp.concatenate([packed_pos, fill], axis=0).astype(bf16)
    q_gain_row = jnp.concatenate([q_gain_ref[...]] * (lanes // head_dim), axis=1)
    k_gain_row = jnp.concatenate([k_gain_ref[...]] * (lanes // head_dim), axis=1)
    rows = tokens_ref[...].astype(f32)
    stat = lax.rsqrt(jnp.mean(rows * rows, axis=1, keepdims=True) + eps_norm)
    normed = (rows * stat * gain_ref[...]).astype(bf16)
    normed_ref[...] = normed
    half = rows.shape[0] // 2
    model_width = rows.shape[1]
    half_rows = pl.ds(pl.multiple_of(info_ref[at_core] * half, half), half)
    early_ref[:, :model_width] = cot_ref[half_rows, :]
    early_ref[:, model_width:] = normed_ref[half_rows, :]
    query = dot_f32(normed, query_w_ref[...], 1, 0)
    key = dot_f32(normed, key_w_ref[...], 1, 0)
    value = dot_f32(normed, value_w_ref[...], 1, 0).astype(bf16).astype(f32)
    query_ref[...] = query
    key_ref[...] = key
    table = head_table(head_dim)
    cosine = cos_ref[...]
    sine = sin_ref[...]
    kv_heads = key.shape[1] // head_dim
    lane = lax.broadcasted_iota(jnp.int32, (rows.shape[0], lanes), 1)

    def turned(tile, gain):
        stat_val = lax.rsqrt(split_dot(tile * tile, table) + eps_norm)
        scaled = tile * stat_val * gain
        return scaled * cosine + swap_halves(scaled, head_dim) * sine

    for head in range(kv_heads):
        query_tile = turned(query[:, head * lanes : (head + 1) * lanes], q_gain_row).astype(bf16)
        pair = slice(head // 2 * lanes, (head // 2 + 1) * lanes)
        key_tile = turned(key[:, pair], k_gain_row)
        value_tile = value[:, pair]
        if head % 2 == 0:
            value_tile = pltpu.roll(value_tile, head_dim, 1)
        else:
            key_tile = pltpu.roll(key_tile, head_dim, 1)
        both = jnp.where(lane < head_dim, key_tile, value_tile).astype(bf16)
        row_count = rows.shape[0]
        blocks_ref[head, :row_count, :] = query_tile
        blocks_ref[head, row_count:, :] = pos_tail
        pairs_ref[head] = both
    for flip in range(count):
        head = info_ref[at_level] ^ flip
        block_refs[flip][...] = blocks_ref[head]
        pair_refs[flip][...] = pairs_ref[head]


def project_kernel(info_ref, *refs):
    count = (len(refs) - 3) // 2
    block_refs = refs[:count]
    weight_ref, part_ref = refs[count : count + 2]
    send_refs = refs[count + 2 : 2 * count + 2]
    heads_ref = refs[2 * count + 2]
    for flip in range(count):
        heads_ref[info_ref[at_level] ^ flip] = block_refs[flip][...]
    total = None
    for head in range(count):
        found = dot_f32(heads_ref[head], weight_ref[:, head * lanes : (head + 1) * lanes], 1, 1)
        total = found if total is None else total + found
    part_ref[...] = total.astype(bf16)
    for flip in range(plane):
        send_refs[flip][...] = heads_ref[info_ref[at_place] ^ flip]


def ffn_kernel(
    steps,
    info_ref,
    tokens_ref,
    own_ref,
    other_ref,
    gain_ref,
    cot_ref,
    gate_ref,
    up_ref,
    down_ref,
    mixed_ref,
    normed_ref,
    half_ref,
    ffn_ref,
    back_ref,
    *refs,
):
    hidden_refs = refs[:plane]
    both_refs = refs[plane : 2 * plane]
    ffn_acc, back_acc, hidden_buf, gate_buf, up_buf = refs[2 * plane :]
    step = pl.program_id(0)
    tile = gate_ref.shape[1]
    width = hidden_refs[0].shape[1]
    half = steps * tile // 2

    @pl.when(step == 0)
    def _():
        mixed = tokens_ref[...].astype(f32) + (own_ref[...].astype(f32) + other_ref[...].astype(f32))
        mixed_ref[...] = mixed
        stat = lax.rsqrt(jnp.mean(mixed * mixed, axis=1, keepdims=True) + eps_norm)
        normed_ref[...] = (mixed * stat * gain_ref[...]).astype(bf16)
        half_count = half_ref.shape[0]
        start = pl.multiple_of(info_ref[at_core] * half_count, half_count)
        half_ref[...] = normed_ref[pl.ds(start, half_count), :]
        ffn_acc[...] = jnp.zeros_like(ffn_acc)
        back_acc[...] = jnp.zeros_like(back_acc)

    normed = normed_ref[...]
    gate = dot_f32(normed, gate_ref[...], 1, 0)
    up = dot_f32(normed, up_ref[...], 1, 0)
    grad = dot_f32(cot_ref[...], down_ref[...], 1, 0)
    sig = jax.nn.sigmoid(gate)
    silu = gate * sig
    hidden = (silu * up).astype(bf16)
    cols = pl.ds(pl.multiple_of(step * tile, tile), tile)
    hidden_buf[:, cols] = hidden
    grad_gate = (grad * up * (sig * (1.0 + gate * (1.0 - sig)))).astype(bf16)
    grad_up = (grad * silu).astype(bf16)
    gate_buf[:, cols] = grad_gate
    up_buf[:, cols] = grad_up
    ffn_acc[...] += dot_f32(hidden, down_ref[...], 1, 1)
    back_acc[...] += dot_f32(grad_gate, gate_ref[...], 1, 1) + dot_f32(grad_up, up_ref[...], 1, 1)

    @pl.when(step == steps - 1)
    def _():
        ffn_ref[...] = ffn_acc[...].astype(bf16)
        back_ref[...] = back_acc[...].astype(bf16)
        for flip in range(plane):
            member = info_ref[at_place] ^ flip
            start = (member % 2) * half + (member // 2) * (half - width)
            hidden_refs[flip][...] = hidden_buf[:, pl.ds(pl.multiple_of(start, lanes), width)]
            side = pl.ds(pl.multiple_of(member // 2 * half, lanes), half)

            @pl.when(member % 2 == 0)
            def _():
                both_refs[flip][...] = gate_buf[:, side]

            @pl.when(member % 2 == 1)
            def _():
                both_refs[flip][...] = up_buf[:, side]


def ffn_call(info, tokens_in, own, other, gain, cot, w_gate, w_up, w_down):
    row_count, model_width = tokens_in.shape
    cols = w_gate.shape[1]
    half, width = window(cols)
    tile = ffn_tile
    steps = cols // tile
    fixed = lambda *shape: pl.BlockSpec(shape, lambda step, info_ref: (0,) * len(shape))
    moving = pl.BlockSpec((model_width, tile), lambda step, info_ref: (0, step))
    rows_spec = fixed(row_count, model_width)
    wide = (row_count, model_width)
    found = pl.pallas_call(
        functools.partial(ffn_kernel, steps),
        grid_spec=pltpu.PrefetchScalarGridSpec(
            num_scalar_prefetch=1,
            grid=(steps,),
            in_specs=[rows_spec, rows_spec, rows_spec, fixed(1, model_width), rows_spec]
            + [moving] * 3,
            out_specs=[rows_spec, rows_spec, fixed(row_count // 2, model_width)]
            + [rows_spec] * 2
            + [fixed(row_count, width)] * plane
            + [fixed(row_count, half)] * plane,
            scratch_shapes=[pltpu.VMEM(wide, f32), pltpu.VMEM(wide, f32)]
            + [pltpu.VMEM((row_count, cols), bf16)] * 3,
        ),
        out_shape=[
            shape_of(wide, f32),
            shape_of(wide, bf16),
            shape_of((row_count // 2, model_width), bf16),
            shape_of(wide, bf16),
            shape_of(wide, bf16),
        ]
        + [shape_of((row_count, width), bf16)] * plane
        + [shape_of((row_count, half), bf16)] * plane,
        cost_estimate=pl.CostEstimate(
            flops=16 * row_count * model_width * cols,
            bytes_accessed=6 * model_width * cols,
            transcendentals=row_count * cols,
        ),
        compiler_params=pltpu.CompilerParams(vmem_limit_bytes=vmem_limit),
        name="ffn",
    )(info, tokens_in, own, other, gain, cot, w_gate, w_up, w_down)
    return (*found[:5], found[5 : 5 + plane], found[5 + plane :])


def middle_kernel(
    info_ref,
    mixed_ref,
    ffn_own_ref,
    ffn_other_ref,
    back_own_ref,
    back_other_ref,
    gain_ref,
    cot_ref,
    weight_ref,
    *refs,
):
    head_refs = refs[: plane - 1]
    layer_ref, grad_ref, rounded_ref, row_ref = refs[plane - 1 : plane + 3]
    pack_refs = refs[plane + 3 : 2 * plane + 2]
    send_refs = refs[2 * plane + 2 : -1]
    blocks_ref = refs[-1]
    mixed = mixed_ref[...]
    layer_ref[...] = mixed + (ffn_own_ref[...].astype(f32) + ffn_other_ref[...].astype(f32))
    found = back_own_ref[...].astype(f32) + back_other_ref[...].astype(f32)
    stat = lax.rsqrt(jnp.mean(mixed * mixed, axis=1, keepdims=True) + eps_norm)
    row_ref[...] = jnp.broadcast_to(
        jnp.sum(found * mixed * stat, axis=0, keepdims=True), row_ref.shape
    )
    grad = cot_ref[...].astype(f32) + rms_back(found * gain_ref[...], mixed, stat)
    grad_ref[...] = grad
    rounded = grad.astype(bf16)
    rounded_ref[...] = rounded
    attended = dot_f32(rounded, weight_ref[...], 1, 0).astype(bf16)
    for head in range(blocks_ref.shape[0]):
        blocks_ref[head] = attended[:, head * lanes : (head + 1) * lanes]
    for flip, send_ref in enumerate(send_refs):
        send_ref[...] = blocks_ref[info_ref[at_level] ^ flip]
    half, model_width = mixed.shape[0] // 2, mixed.shape[1]
    half_rows = pl.ds(pl.multiple_of(info_ref[at_core] * half, half), half)
    for pack_ref, head_ref in zip(pack_refs, head_refs):
        pack_ref[:, :model_width] = rounded_ref[half_rows, :]
        pack_ref[:, model_width : model_width + lanes] = head_ref[:half, :]
        pack_ref[:, model_width + lanes :] = head_ref[half:, :]


def turn_back_kernel(head_dim, info_ref, *refs):
    count = (len(refs) - 14 - plane) // 2
    block_refs = refs[:count]
    other_refs = refs[count : 2 * count]
    (
        query_ref,
        key_ref,
        q_gain_ref,
        k_gain_ref,
        cos_ref,
        sin_ref,
        query_w_ref,
        key_w_ref,
        value_w_ref,
        part_ref,
        gain_row_ref,
    ) = refs[2 * count : 2 * count + 11]
    send_refs = refs[2 * count + 11 : 2 * count + 11 + plane]
    query_buf, pair_buf, raw_ref = refs[2 * count + 11 + plane :]
    kv_heads = count
    for flip in range(count):
        head = info_ref[at_level] ^ flip
        query_buf[head] = block_refs[flip][...]
        pair_buf[head] = other_refs[flip][...].astype(f32)
    table = head_table(head_dim)
    cosine = cos_ref[...]
    sine = sin_ref[...]
    q_gain_row = jnp.concatenate([q_gain_ref[...]] * (lanes // head_dim), axis=1)
    k_gain_row = jnp.concatenate([k_gain_ref[...]] * (lanes // head_dim), axis=1)
    lane = lax.broadcasted_iota(jnp.int32, cosine.shape, 1)

    def back(grad_rot, raw, gain):
        grad_norm = grad_rot * cosine - swap_halves(grad_rot, head_dim) * sine
        stat = lax.rsqrt(split_dot(raw * raw, table) + eps_norm)
        gain_row = jnp.sum(grad_norm * raw * stat, axis=0, keepdims=True)
        grad_in = grad_norm * gain
        grad_raw = stat * grad_in - raw * stat**3 * split_dot(grad_in * raw, table)
        return (grad_raw.astype(bf16), gain_row)

    total = None
    gain_rows = [None, None]
    place = 0
    per_slot = raw_ref.shape[2] // lanes

    def emit(tile, weight, kind, gain_row):
        nonlocal total, place
        slot = place % per_slot
        raw_ref[place // per_slot, :, slot * lanes : (slot + 1) * lanes] = tile
        place += 1
        found = dot_f32(tile, weight, 1, 1)
        total = found if total is None else total + found
        if gain_row is not None:
            gain_rows[kind] = gain_row if gain_rows[kind] is None else gain_rows[kind] + gain_row

    for head in range(kv_heads):
        cols = slice(head * lanes, (head + 1) * lanes)
        tile, gain_row = back(query_buf[head].astype(f32), query_ref[:, cols], q_gain_row)
        emit(tile, query_w_ref[:, cols], 0, gain_row)
    for pair in range(kv_heads // 2):
        cols = slice(pair * lanes, (pair + 1) * lanes)
        first = pair_buf[2 * pair]
        second = pair_buf[2 * pair + 1]
        merged = jnp.where(lane < head_dim, first, pltpu.roll(second, head_dim, 1))
        tile, gain_row = back(merged, key_ref[:, cols], k_gain_row)
        emit(tile, key_w_ref[:, cols], 1, gain_row)
    for pair in range(kv_heads // 2):
        cols = slice(pair * lanes, (pair + 1) * lanes)
        first = pair_buf[2 * pair]
        second = pair_buf[2 * pair + 1]
        merged = jnp.where(lane < head_dim, pltpu.roll(first, head_dim, 1), second).astype(bf16)
        emit(merged, value_w_ref[:, cols], 1, None)
    part_ref[...] = total.astype(bf16)
    gain_row_ref[...] = jnp.concatenate(gain_rows + [jnp.zeros((6, lanes), f32)], axis=0)
    for flip in range(plane):
        send_refs[flip][...] = raw_ref[info_ref[at_place] ^ flip]


def last_kernel(tokens_ref, grad_ref, own_ref, other_ref, gain_ref, out_ref, row_ref):
    rows = tokens_ref[...].astype(f32)
    stat = lax.rsqrt(jnp.mean(rows * rows, axis=1, keepdims=True) + eps_norm)
    found = own_ref[...].astype(f32) + other_ref[...].astype(f32)
    row_ref[...] = jnp.broadcast_to(
        jnp.sum(found * rows * stat, axis=0, keepdims=True), row_ref.shape
    )
    out_ref[...] = grad_ref[...] + rms_back(found * gain_ref[...], rows, stat)


def plane_gather(mine):
    near = [xor_swap(mine, everywhere, flip) for flip in range(1, plane)]
    far = [xor_swap(found, "tp", 1) for found in near]
    return (near, far)


def window(cols):
    half = cols // 2
    width = min(half, -(-half // (2 * lanes)) * lanes)
    return (half, width)


def rows_kernel(jobs, steps, info_ref, *refs):
    step = pl.program_id(0)
    gain_refs = refs[-5 - 2 * len(jobs) : -2 - 2 * len(jobs)]
    send_ref, keep_ref = refs[-2 - 2 * len(jobs) : -2 * len(jobs)]
    bufs = refs[-2 * len(jobs) :]
    height = keep_ref.shape[1]
    core = info_ref[at_core]
    used = 0
    offset = 0
    pieces = []
    for number, (packed, width) in enumerate(jobs):
        row_buf, col_buf = bufs[2 * number : 2 * number + 2]
        own_ref = refs[used]
        near_refs = refs[used + 1 : used + plane]
        far_refs = refs[used + plane : used + 2 * plane - 1]
        used += 2 * plane - 1
        row_count = own_ref.shape[0]
        half = row_count // 2
        col_count = 2 * plane - 1 if packed else plane
        col_refs = refs[used : used + col_count]
        used += col_count

        @pl.when(step == 0)
        def _():
            if packed:
                col_buf[:row_count, :] = col_refs[0][...]
                for n, col_ref in enumerate(col_refs[1:]):
                    start = row_count + n * half
                    col_buf[start : start + half, :] = col_ref[...]
            else:
                for n, col_ref in enumerate(col_refs):
                    col_buf[n * row_count : (n + 1) * row_count, :] = col_ref[...]

        row_buf[:row_count, :] = own_ref[...]
        for n in range(plane - 1):
            base = (n + 1) * row_count
            near_rows = pl.ds(pl.multiple_of(base + core * half, half), half)
            far_rows = pl.ds(pl.multiple_of(base + (1 - core) * half, half), half)
            row_buf[near_rows, :] = near_refs[n][...]
            row_buf[far_rows, :] = far_refs[n][...]
        pieces.append((offset, width, dot_f32(row_buf[...], col_buf[...], 0, 0)))
        offset += width
    if offset < keep_ref.shape[2]:
        ffn_ref, attn_ref, head_ref = gain_refs
        rows = [ffn_ref[:1, :], attn_ref[:1, :]]
        for n in range(2):
            rows.append(jnp.concatenate([head_ref[n : n + 1, :]] * (height // lanes), axis=1))
        rows.append(jnp.zeros((lanes - 4, height), f32))
        pieces.append((offset, lanes, jnp.concatenate(rows, axis=0).T))

    @pl.when(step < steps)
    def _():
        for offset, width, found in pieces:
            send_ref[0, :, offset : offset + width] = found.astype(bf16)

    @pl.when(step >= steps)
    def _():
        for offset, width, found in pieces:
            keep_ref[0, :, offset : offset + width] = found


def fold_kernel(info_ref, kept_ref, found_ref, send_ref, keep_ref, *, slot):
    bit = info_ref[at_bits + slot]
    send_ref[...] = (kept_ref[1 - bit] + found_ref[1 - bit].astype(f32)).astype(bf16)
    keep_ref[...] = kept_ref[bit] + found_ref[bit].astype(f32)


def finish_kernel(jobs, info_ref, *refs):
    out_refs = refs[2 * jobs :]
    height = out_refs[0].shape[0]
    for flip, out_ref in enumerate(out_refs):
        start = pl.multiple_of((info_ref[at_place] ^ flip) * height, height)
        rows = pl.ds(start, height)
        offset = 0
        for n in range(jobs):
            kept_ref, found_ref = refs[2 * n : 2 * n + 2]
            width = kept_ref.shape[1]
            total = kept_ref[rows, :] + found_ref[rows, :].astype(f32)
            out_ref[:, offset : offset + width] = total.astype(out_ref.dtype)
            offset += width


class Halving:
    def __init__(self, index, total, model_width):
        self.blocks = total // plane
        self.model_width = model_width
        bits = self.blocks.bit_length() - 1
        self.fine = self.blocks == 4 and model_width // self.blocks % lanes == 0
        self.order = list(range(bits)) if self.fine else list(range(bits))[::-1]
        self.steps = 2 if self.fine else 1
        self.height = model_width // self.steps // 2
        block_index = index // plane
        self.bits = [(block_index >> bit) & 1 for bit in self.order]

    def rows(self, info, jobs, gains=None):
        steps, height = self.steps, self.height
        per_piece = self.model_width // height

        def block_of(step, info_ref):
            first = info_ref[at_bits]
            bit = jnp.where(step < steps, 1 - first, first)
            return 2 * (step % steps) + bit if steps > 1 else bit

        fixed = lambda *shape: pl.BlockSpec(shape, lambda step, info_ref: (0,) * len(shape))
        args, specs, scratch, shape_jobs = [], [], [], []
        flops = 0
        for (own, near, far, slot), cols in jobs:
            row_count = own.shape[0]
            half = row_count // 2
            packed = len(cols) == 1
            width = cols[0].shape[1]
            args += [own, *near, *far]
            specs.append(
                pl.BlockSpec((row_count, height), lambda step, ref: (0, block_of(step, ref)))
            )
            specs += [
                pl.BlockSpec(
                    (half, height),
                    lambda step, ref, base=slot * per_piece: (0, base + block_of(step, ref)),
                )
            ] * (2 * plane - 2)
            args.append(cols[0])
            specs.append(fixed(row_count, width))
            if packed:
                for part in near:
                    for n in range(2):
                        args.append(part)
                        spot = self.model_width // width + n
                        specs.append(
                            pl.BlockSpec((half, width), lambda step, ref, spot=spot: (0, spot))
                        )
            else:
                args += cols[1:]
                specs += [fixed(row_count, width)] * (plane - 1)
            scratch += [
                pltpu.VMEM((plane * row_count, height), bf16),
                pltpu.VMEM((plane * row_count, width), bf16),
            ]
            shape_jobs.append((packed, width))
            flops += 2 * plane * row_count * self.model_width * width
        total_width = sum(width for _, width in shape_jobs)
        if gains is not None:
            total_width += lanes
            row_spec = pl.BlockSpec((8, height), lambda step, ref: (0, block_of(step, ref)))
            specs += [row_spec, row_spec, fixed(8, lanes)]
        else:
            gains = [jnp.zeros((8, lanes), f32)] * 3
            specs += [fixed(8, lanes)] * 3
        args += gains
        out = (1, height, total_width)
        return pl.pallas_call(
            functools.partial(rows_kernel, shape_jobs, steps),
            grid_spec=pltpu.PrefetchScalarGridSpec(
                num_scalar_prefetch=1,
                grid=(2 * steps,),
                in_specs=specs,
                out_specs=[
                    pl.BlockSpec(out, lambda step, ref: (jnp.minimum(step, steps - 1), 0, 0)),
                    pl.BlockSpec(out, lambda step, ref: (jnp.maximum(step - steps, 0), 0, 0)),
                ],
                scratch_shapes=scratch,
            ),
            out_shape=[
                shape_of((steps, height, total_width), bf16),
                shape_of((steps, height, total_width), f32),
            ],
            cost_estimate=pl.CostEstimate(
                flops=flops,
                bytes_accessed=sum(arg.size * arg.dtype.itemsize for arg in args)
                + 6 * steps * height * total_width,
                transcendentals=0,
            ),
            compiler_params=pltpu.CompilerParams(vmem_limit_bytes=vmem_limit),
            name="rows",
        )(info, *args)

    def start(self, turn, sent):
        return xor_swap(sent, everywhere, plane << self.order[turn])

    def fold(self, info, turn, kept, found):
        width = kept.shape[-1]
        rows_left = kept.size // width // 2
        send, keep = whole_call(
            functools.partial(fold_kernel, slot=turn),
            [shape_of((rows_left, width), bf16), shape_of((rows_left, width), f32)],
            [kept.reshape(2, rows_left, width), found.reshape(2, rows_left, width)],
            scalars=(info,),
        )
        return (keep, self.start(turn, send))

    def through(self, info, rows):
        sent, kept = rows
        found = self.start(0, sent)
        for turn in range(1, len(self.order)):
            kept, found = self.fold(info, turn, kept, found)
        return (kept.reshape(-1, kept.shape[-1]), found.reshape(-1, kept.shape[-1]))


def return_rows(info, sums):
    height = sums[0][0].shape[0] // plane
    width = sum(kept.shape[1] for kept, _ in sums)
    parts = whole_call(
        functools.partial(finish_kernel, len(sums)),
        [shape_of((height, width), bf16 if flip else f32) for flip in range(plane)],
        [value for pair in sums for value in pair],
        scalars=(info,),
    )
    return plane_swap(parts)


def assemble_kernel(moves, gain_start, info_ref, *refs):
    part_refs = refs[:plane]
    out_refs = refs[plane:]
    for flip in range(plane):
        for member in range(plane):

            @pl.when((info_ref[at_place] ^ flip) == member)
            def _():
                for out, out_start, start, width in moves[member]:
                    out_refs[out][:, out_start : out_start + width] = part_refs[flip][
                        :, start : start + width
                    ].astype(f32)

    if gain_start is not None:
        cols = slice(gain_start, gain_start + lanes)
        total = sum(part_ref[:, cols].astype(f32) for part_ref in part_refs).T
        for n in range(4):
            out_refs[len(out_refs) - 4 + n][...] = total[n : n + 1, :]


def assemble(info, parts, moves, widths, gain_start=None):
    height = parts[0].shape[0]
    outs = [shape_of((height, width), f32) for width in widths]
    if gain_start is not None:
        outs += [shape_of((1, height), f32)] * 4
    return whole_call(
        functools.partial(assemble_kernel, moves, gain_start), outs, parts, scalars=(info,)
    )


def shards(
    tokens,
    positions,
    attn_gain,
    ffn_gain,
    q_gain,
    k_gain,
    w_query,
    w_key,
    w_value,
    w_out,
    w_gate,
    w_up,
    w_down,
    cotangent,
):
    seq_count, block_len, model_width = tokens.shape
    row_count = seq_count * block_len
    head_dim = q_gain.shape[0]
    q_heads = w_query.shape[1] // head_dim
    kv_heads = w_key.shape[1] // head_dim
    key_width = kv_heads * head_dim
    query_width = q_heads * head_dim
    group_size = q_heads // kv_heads
    hidden_width = w_gate.shape[1]
    ctx_size = lax.axis_size("ctx")
    total = ctx_size * lax.axis_size("seq")
    here_index = lax.axis_index("ctx")
    index = lax.axis_index(everywhere)
    by_head = ctx_size == 2 * kv_heads
    rows_bf = shape_of((row_count, model_width), bf16)
    rows_f32 = shape_of((row_count, model_width), f32)
    head_block = shape_of((row_count, lanes), bf16)
    full_block = shape_of((row_count + pos_rows, lanes), bf16)
    halving = Halving(index, total, model_width)
    info = jnp.stack(
        [
            here_index // 2 if by_head else jnp.int32(0),
            here_index % 2,
            lax.axis_index("tp"),
            index % plane,
            *halving.bits,
        ]
    ).astype(jnp.int32)

    cot_rows = cotangent.reshape(row_count, model_width)
    token_rows = tokens.reshape(row_count, model_width)
    pack_width = 2 * lanes
    q_gain_row = q_gain[None, :]
    k_gain_row = k_gain[None, :]
    attn_gain_row = attn_gain[None, :]
    ffn_gain_row = ffn_gain[None, :]

    normed_one, early_half, query_raw, key_raw, cosine, sine, *found = whole_call(
        functools.partial(front_kernel, head_dim),
        [
            rows_bf,
            shape_of((row_count // 2, 2 * model_width), bf16),
            shape_of((row_count, query_width), f32),
            shape_of((row_count, key_width), f32),
            shape_of((row_count, lanes), f32),
            shape_of((row_count, lanes), f32),
        ]
        + [full_block] * kv_heads
        + [head_block] * kv_heads,
        [
            token_rows,
            cot_rows,
            attn_gain_row,
            w_query,
            w_key,
            w_value,
            q_gain_row,
            k_gain_row,
            positions,
        ],
        scalars=(info,),
        scratch=[
            pltpu.VMEM((kv_heads, row_count + pos_rows, lanes), bf16),
            pltpu.VMEM((kv_heads, row_count, lanes), bf16),
        ],
        flops=2 * row_count * model_width * (query_width + 2 * key_width),
    )
    packed, pair_parts = found[:kv_heads], found[kv_heads:]

    if by_head:
        pairs = level_swap(pair_parts)
        blocks = level_swap(packed)
        sources = [*blocks, *pairs, *side_swap(pairs)]
        out_heads, log_sum, out_parts = head_forward(info, sources, seq_count, head_dim)
        out_blocks = level_swap(out_parts)
    else:
        flat = jnp.concatenate(
            [jnp.stack([part[:row_count] for part in packed]), jnp.stack(pair_parts)], axis=2
        )
        flat = flat.reshape(kv_heads, seq_count, block_len, pack_width)
        flat = jnp.transpose(flat, (1, 2, 0, 3))
        query_grouped = flat[..., :lanes].reshape(
            seq_count, block_len, kv_heads, group_size, head_dim
        )
        query_index = here_index * block_len + jnp.arange(block_len, dtype=jnp.int32)
        lowest_key = query_index[None, :] - positions
        attended_grouped, log_sum, key_all, value_all = gathered_forward(
            query_grouped,
            flat[..., lanes : lanes + head_dim].reshape(seq_count, block_len, key_width),
            flat[..., lanes + head_dim :].reshape(seq_count, block_len, key_width),
            query_index,
            lowest_key,
        )
        out_blocks = list(
            jnp.transpose(attended_grouped, (2, 0, 1, 3, 4)).reshape(kv_heads, row_count, lanes)
        )

    early_near, early_far = plane_gather(early_half)
    cot_pieces = (cot_rows, early_near, early_far, 0)
    one_pieces = (normed_one, early_near, early_far, 1)

    attn_part, *head_parts = whole_call(
        project_kernel,
        [rows_bf] + [head_block] * plane,
        [*out_blocks, w_out],
        scalars=(info,),
        scratch=[pltpu.VMEM((kv_heads, row_count, lanes), bf16)],
        flops=2 * row_count * model_width * query_width,
    )
    mixed, normed_two, two_half, ffn_part, back_part, hidden_parts, both_parts = ffn_call(
        info,
        token_rows,
        attn_part,
        named_swap(attn_part),
        ffn_gain_row,
        cot_rows,
        w_gate,
        w_up,
        w_down,
    )
    ffn_other = named_swap(ffn_part)
    back_other = named_swap(back_part)
    hidden_plane = plane_swap(hidden_parts)
    both_plane = plane_swap(both_parts)
    two_near, two_far = plane_gather(two_half)
    two_pieces = (normed_two, two_near, two_far, 0)
    half, width = window(hidden_width)

    pack_block = shape_of((row_count // 2, model_width + 2 * lanes), bf16)
    layer_output, grad_mixed, grad_mixed_bf, ffn_row, *found = whole_call(
        middle_kernel,
        [rows_f32, rows_f32, rows_bf, shape_of((8, model_width), f32)]
        + [pack_block] * (plane - 1)
        + [head_block] * kv_heads,
        [
            mixed,
            ffn_part,
            ffn_other,
            back_part,
            back_other,
            ffn_gain_row,
            cot_rows,
            w_out,
            *head_parts[1:],
        ],
        scalars=(info,),
        scratch=[pltpu.VMEM((kv_heads, row_count, lanes), bf16)],
        flops=2 * row_count * model_width * query_width,
    )
    mixed_packs, grad_parts = found[: plane - 1], found[plane - 1 :]

    if by_head:
        grads = level_swap(grad_parts)
        query_parts, own_parts, other_parts = head_backward(
            info, sources, grads, out_heads, log_sum, seq_count, head_dim
        )
        crossed = side_swap(other_parts)
        returned = level_swap(query_parts)
        pair_sums = whole_call(
            functools.partial(merge_kernel, kv_heads),
            [head_block] * kv_heads,
            [*own_parts, *crossed],
        )
        others = level_swap(pair_sums)
    else:
        grad_grouped = jnp.transpose(
            jnp.stack(grad_parts).reshape(kv_heads, seq_count, block_len, group_size, head_dim),
            (1, 2, 0, 3, 4),
        )
        query_grad, key_grad_own, value_grad_own = gathered_backward(
            query_grouped,
            grad_grouped,
            attended_grouped,
            log_sum,
            key_all,
            value_all,
            query_index,
            lowest_key,
        )
        shaped = lambda grad: grad.reshape(seq_count, block_len, kv_heads, -1)
        returned = jnp.concatenate(
            [shaped(query_grad), shaped(key_grad_own), shaped(value_grad_own)], axis=-1
        ).astype(bf16)
        returned = jnp.transpose(returned, (2, 0, 1, 3)).reshape(kv_heads, row_count, pack_width)
        others = list(returned[..., lanes:])
        returned = list(returned[..., :lanes])

    down_sum = halving.through(info, halving.rows(info, [(cot_pieces, hidden_plane)]))
    both_sum = halving.through(info, halving.rows(info, [(two_pieces, both_plane)]))
    wide_parts = return_rows(info, [both_sum, down_sum])

    mixed_near = [xor_swap(pack, everywhere, flip + 1) for flip, pack in enumerate(mixed_packs)]
    mixed_far = [xor_swap(found, "tp", 1) for found in mixed_near]
    mixed_pieces = (grad_mixed_bf, mixed_near, mixed_far, 0)

    raw_width = (query_width + 2 * key_width) // plane
    one_part, head_rows, *raw_parts = whole_call(
        functools.partial(turn_back_kernel, head_dim),
        [rows_bf, shape_of((8, lanes), f32)] + [shape_of((row_count, raw_width), bf16)] * plane,
        [
            *returned,
            *others,
            query_raw,
            key_raw,
            q_gain_row,
            k_gain_row,
            cosine,
            sine,
            w_query,
            w_key,
            w_value,
        ],
        scalars=(info,),
        scratch=[
            pltpu.VMEM((kv_heads, row_count, lanes), bf16),
            pltpu.VMEM((kv_heads, row_count, lanes), f32),
            pltpu.VMEM((plane, row_count, raw_width), bf16),
        ],
        flops=2 * row_count * model_width * (query_width + 2 * key_width),
    )
    one_other = named_swap(one_part)
    head_sum = head_rows + named_swap(head_rows)
    head_sum = head_sum + jnp.roll(head_sum, head_dim, axis=1)
    raw_plane = plane_swap(raw_parts)
    input_grad, attn_row = whole_call(
        last_kernel,
        [rows_f32, shape_of((8, model_width), f32)],
        [token_rows, grad_mixed, one_part, one_other, attn_gain_row],
    )

    late_sum = halving.through(
        info,
        halving.rows(
            info,
            [(mixed_pieces, head_parts[:1]), (one_pieces, raw_plane)],
            [ffn_row, attn_row, head_sum],
        ),
    )
    late_parts = return_rows(info, [late_sum])

    skip = 2 * width - half
    wide_moves = []
    for member in range(plane):
        far_side = member // 2
        down_start = half * (member % 2) + far_side * width
        wide_moves.append(
            [
                (member % 2, half * far_side, 0, half),
                (2, down_start, half + far_side * skip, width - far_side * skip),
            ]
        )
    wgate_grad, wup_grad, wdown_grad = assemble(info, wide_parts, wide_moves, [hidden_width] * 3)

    out_width = lanes
    late_moves = []
    for member in range(plane):
        moves = [(0, member * out_width, 0, out_width)]
        for out, begin, size in (
            (1, 0, query_width),
            (2, query_width, key_width),
            (3, query_width + key_width, key_width),
        ):
            low = max(begin, member * raw_width)
            high = min(begin + size, (member + 1) * raw_width)
            if low < high:
                moves.append((out, low - begin, out_width + low - member * raw_width, high - low))
        late_moves.append(moves)
    wo_grad, wq_grad, wk_grad, wv_grad, *gain_rows = assemble(
        info,
        late_parts,
        late_moves,
        [query_width, query_width, key_width, key_width],
        out_width + raw_width,
    )
    ffngain_grad, attngain_grad, qgain_grad, kgain_grad = (row.reshape(-1) for row in gain_rows)
    if qgain_grad.shape[0] < head_dim:
        qgain_grad, kgain_grad = (
            lax.all_gather(row, everywhere, axis=0, tiled=True)[:head_dim]
            for row in (qgain_grad, kgain_grad)
        )
    else:
        qgain_grad, kgain_grad = qgain_grad[:head_dim], kgain_grad[:head_dim]
    return (
        layer_output.reshape(seq_count, block_len, model_width),
        input_grad.reshape(seq_count, block_len, model_width),
        wq_grad,
        wk_grad,
        wv_grad,
        wo_grad,
        wgate_grad,
        wup_grad,
        wdown_grad,
        attngain_grad,
        ffngain_grad,
        qgain_grad,
        kgain_grad,
    )


def solution(mesh):
    placed = (
        P("seq", "ctx", None),
        P("seq", "ctx"),
        P(),
        P(),
        P(),
        P(),
        P(None, "tp"),
        P(None, "tp"),
        P(None, "tp"),
        P(None, "tp"),
        P(None, "tp"),
        P(None, "tp"),
        P(None, "tp"),
        P("seq", "ctx", None),
    )
    return jax.shard_map(
        shards,
        mesh=mesh,
        in_specs=placed,
        out_specs=(
            P("seq", "ctx", None),
            P("seq", "ctx", None),
            P(("ctx", "seq"), "tp"),
            P(("ctx", "seq"), "tp"),
            P(("ctx", "seq"), "tp"),
            P(("ctx", "seq"), "tp"),
            P(("ctx", "seq"), "tp"),
            P(("ctx", "seq"), "tp"),
            P(("ctx", "seq"), "tp"),
            P(("ctx", "seq")),
            P(("ctx", "seq")),
            P(),
            P(),
        ),
        check_vma=False,
    )
```

```python
import functools
import math

import jax
import jax.numpy as jnp
from jax import lax
from jax.experimental import pallas as pl
from jax.experimental.pallas import tpu as pltpu
from jax.sharding import PartitionSpec as P


eps_norm = 1e-05
theta_base = 1000000.0
negative = -1e30
bf16 = jnp.bfloat16
f32 = jnp.float32
lanes = 128
pos_shift = 7
pos_base = 1 << pos_shift
pos_rows = 16
ffn_tile = 256
vmem_limit = 28 * 1024 * 1024


def dot_f32(lhs, rhs, lhs_dim, rhs_dim):
    return lax.dot_general(
        lhs, rhs, (((lhs_dim,), (rhs_dim,)), ((), ())), preferred_element_type=f32
    )


def rms_back(grad_in, values, stat_val):
    return stat_val * grad_in - values * stat_val**3 * jnp.mean(
        grad_in * values, axis=-1, keepdims=True
    )


def xor_swap(value, axis, flip):
    size = lax.axis_size(axis)
    return lax.ppermute(value, axis, [(index, index ^ flip) for index in range(size)])


def named_swap(value, axis="tp"):
    return xor_swap(value, axis, 1)


def stay(value):
    return pltpu.with_memory_space_constraint(value, pltpu.HBM)


def level_swap(parts):
    count = len(parts)
    found = [parts[0]] + [None] * (count - 1)
    for flip in range(count - 1, 0, -1):
        found[flip] = xor_swap(parts[flip], "ctx", 2 * flip)
    return found


def side_swap(parts):
    return [xor_swap(part, "ctx", 1) for part in parts]


def plane_swap(parts):
    return [parts[0]] + [
        xor_swap(parts[flip], everywhere, flip) for flip in range(1, len(parts))
    ]


everywhere = ("ctx", "seq")
plane = 4
at_level, at_side, at_core, at_place, at_bits = range(5)


def fill_heads(ref, place, rows, head_dim):
    tokens_count = rows.shape[0]
    for head in range(rows.shape[1] // head_dim):
        ref[place, head * tokens_count : (head + 1) * tokens_count, :] = rows[
            :, head * head_dim : (head + 1) * head_dim
        ]


def gather_blocks(
    info_ref, block_refs, own_refs, other_refs, query_buf, key_buf, value_buf, low_buf
):
    count = len(block_refs)
    seq_count = key_buf.shape[0]
    head_dim = key_buf.shape[2]
    block_len = own_refs[0].shape[0] // seq_count
    side = info_ref[at_side]
    for flip in range(count):
        level = info_ref[at_level] ^ flip
        block_ref = block_refs[flip]
        own_start = pl.multiple_of((level * 2 + side) * block_len, block_len)
        other_start = pl.multiple_of((level * 2 + 1 - side) * block_len, block_len)
        tail = block_ref[seq_count * block_len :, :].astype(f32)
        found = tail[:seq_count] * pos_base + tail[seq_count : 2 * seq_count]
        token = own_start + lax.broadcasted_iota(jnp.int32, (1, block_len), 1)
        for seq in range(seq_count):
            part = slice(seq * block_len, (seq + 1) * block_len)
            fill_heads(query_buf, seq * count + level, block_ref[part, :], head_dim)
            for refs, start in ((own_refs, own_start), (other_refs, other_start)):
                rows = pl.ds(start, block_len)
                key_buf[seq, rows, :] = refs[flip][part, :head_dim]
                value_buf[seq, rows, :] = refs[flip][part, head_dim:]
            low_buf[seq * count + level] = token - found[seq : seq + 1].astype(jnp.int32)


def visible(info_ref, low_row, level, key_count, block_len, width):
    low = jnp.concatenate([low_row] * (width // block_len), axis=1)
    shape = (key_count, low.shape[1])
    key_index = lax.broadcasted_iota(jnp.int32, shape, 0)
    lane = lax.broadcasted_iota(jnp.int32, shape, 1) % block_len
    query_index = (level * 2 + info_ref[at_side]) * block_len + lane
    return (key_index <= query_index) & (key_index >= low)


def unfold(turned, block_len):
    parts = [
        turned[:, start : start + block_len] for start in range(0, turned.shape[1], block_len)
    ]
    return jnp.concatenate(parts, axis=0).T


def attend_kernel(count, *refs):
    info_ref = refs[0]
    sources = [refs[1 + n * count : 1 + (n + 1) * count] for n in range(3)]
    out_ref, lse_ref = refs[1 + 3 * count : 3 + 3 * count]
    send_refs = refs[3 + 3 * count : 3 + 4 * count]
    query_buf, key_buf, value_buf, low_buf = refs[3 + 4 * count :]
    gather_blocks(info_ref, *sources, query_buf, key_buf, value_buf, low_buf)
    seq_count, _, head_dim = key_buf.shape
    block_len = low_buf.shape[2]
    for seq in range(seq_count):
        for level in range(count):
            place = seq * count + level
            key_count = 2 * block_len * (level + 1)
            query = query_buf[place]
            scores = dot_f32(key_buf[seq, :key_count, :], query, 1, 1) * head_dim ** (-0.5)
            allowed = visible(info_ref, low_buf[place], level, key_count, block_len, query.shape[0])
            scores = jnp.where(allowed, scores, negative)
            top = jnp.max(scores, axis=0, keepdims=True)
            weights = jnp.exp(scores - top)
            row_sum = jnp.sum(weights, axis=0, keepdims=True)
            lse_ref[place : place + 1, :] = top + jnp.log(row_sum)
            turned = dot_f32(value_buf[seq, :key_count, :], weights.astype(bf16), 0, 0) / row_sum
            out_ref[level, seq * block_len : (seq + 1) * block_len, :] = unfold(
                turned, block_len
            ).astype(bf16)
    for flip in range(count):
        send_refs[flip][...] = out_ref[info_ref[at_level] ^ flip]


def attend_back_kernel(count, *refs):
    info_ref = refs[0]
    sources = [refs[1 + n * count : 1 + (n + 1) * count] for n in range(3)]
    grad_refs = refs[1 + 3 * count : 1 + 4 * count]
    out_ref, lse_ref = refs[1 + 4 * count : 3 + 4 * count]
    query_refs = refs[3 + 4 * count : 3 + 5 * count]
    own_refs = refs[3 + 5 * count : 3 + 6 * count]
    other_refs = refs[3 + 6 * count : 3 + 7 * count]
    (
        query_buf,
        key_buf,
        value_buf,
        low_buf,
        grad_buf,
        key_acc,
        value_acc,
        query_grad,
    ) = refs[3 + 7 * count :]
    gather_blocks(info_ref, *sources, query_buf, key_buf, value_buf, low_buf)
    seq_count, _, head_dim = key_buf.shape
    block_len = low_buf.shape[2]
    group = lanes // head_dim
    for flip in range(count):
        for seq in range(seq_count):
            rows = grad_refs[flip][seq * block_len : (seq + 1) * block_len, :]
            level = info_ref[at_level] ^ flip
            fill_heads(grad_buf, seq * count + level, rows, head_dim)
    key_acc[...] = jnp.zeros_like(key_acc)
    value_acc[...] = jnp.zeros_like(value_acc)
    scale = head_dim ** (-0.5)
    ones_row = jnp.ones((8, head_dim), f32)
    for seq in range(seq_count):
        for level in range(count):
            place = seq * count + level
            key_count = 2 * block_len * (level + 1)
            keys = key_buf[seq, :key_count, :]
            query = query_buf[place]
            grad = grad_buf[place]
            rows = out_ref[level, seq * block_len : (seq + 1) * block_len, :]
            out = jnp.concatenate(
                [rows[:, head * head_dim : (head + 1) * head_dim] for head in range(group)], axis=0
            )
            delta = lax.dot_general(
                ones_row,
                grad.astype(f32) * out.astype(f32),
                (((1,), (1,)), ((), ())),
                precision=lax.Precision.HIGHEST,
                preferred_element_type=f32,
            )[:1, :]
            scores = dot_f32(keys, query, 1, 1) * scale
            allowed = visible(info_ref, low_buf[place], level, key_count, block_len, query.shape[0])
            probs = jnp.where(allowed, jnp.exp(scores - lse_ref[place : place + 1, :]), 0.0)
            grad_probs = dot_f32(value_buf[seq, :key_count, :], grad, 1, 1)
            grad_scores = (probs * (grad_probs - delta)).astype(bf16)
            value_acc[seq, :key_count, :] += dot_f32(probs.astype(bf16), grad, 1, 0)
            key_acc[seq, :key_count, :] += dot_f32(grad_scores, query, 1, 0)
            turned = dot_f32(keys, grad_scores, 0, 0) * scale
            query_grad[level, seq * block_len : (seq + 1) * block_len, :] = unfold(
                turned, block_len
            ).astype(bf16)
    side = info_ref[at_side]
    for flip in range(count):
        level = info_ref[at_level] ^ flip
        query_refs[flip][...] = query_grad[level]
        for seq in range(seq_count):
            part = slice(seq * block_len, (seq + 1) * block_len)
            for place, ref in ((side, own_refs[flip]), (1 - side, other_refs[flip])):
                start = pl.multiple_of((2 * level + place) * block_len, block_len)
                rows = pl.ds(start, block_len)
                both = [key_acc[seq, rows, :] * scale, value_acc[seq, rows, :]]
                ref[part, :] = jnp.concatenate(both, axis=1).astype(ref.dtype)


def merge_kernel(count, *refs):
    for flip in range(count):
        own_ref, other_ref, out_ref = refs[flip::count]
        out_ref[...] = (own_ref[...] + other_ref[...].astype(f32)).astype(bf16)


def smem_spec():
    return pl.BlockSpec(memory_space=pltpu.SMEM)


def vmem_spec():
    return pl.BlockSpec(memory_space=pltpu.VMEM)


def shape_of(shape, dtype):
    return jax.ShapeDtypeStruct(shape, dtype)


def whole_call(kernel, outs, args, scalars=(), scratch=(), flops=0):
    moved = sum(arg.size * arg.dtype.itemsize for arg in args)
    moved += sum(out.size * jnp.dtype(out.dtype).itemsize for out in outs)
    return pl.pallas_call(
        kernel,
        out_shape=tuple(outs),
        in_specs=[smem_spec()] * len(scalars) + [vmem_spec()] * len(args),
        out_specs=tuple(vmem_spec() for _ in outs),
        scratch_shapes=list(scratch),
        cost_estimate=pl.CostEstimate(flops=flops, bytes_accessed=moved, transcendentals=0),
        compiler_params=pltpu.CompilerParams(vmem_limit_bytes=vmem_limit),
    )(*scalars, *args)


def head_scratch(seq_count, count, block_len, head_dim):
    total = 2 * count * block_len
    heads_rows = lanes // head_dim * block_len
    return [
        pltpu.VMEM((seq_count * count, heads_rows, head_dim), bf16),
        pltpu.VMEM((seq_count, total, head_dim), bf16),
        pltpu.VMEM((seq_count, total, head_dim), bf16),
        pltpu.VMEM((seq_count * count, 1, block_len), jnp.int32),
    ]


def head_forward(info, sources, seq_count, head_dim):
    count = len(sources) // 3
    row_count = sources[-1].shape[0]
    block_len = row_count // seq_count
    heads_rows = lanes // head_dim * block_len
    found = whole_call(
        functools.partial(attend_kernel, count),
        [
            shape_of((count, row_count, lanes), bf16),
            shape_of((seq_count * count, heads_rows), f32),
        ]
        + [shape_of((row_count, lanes), bf16)] * count,
        sources,
        scalars=(info,),
        scratch=head_scratch(seq_count, count, block_len, head_dim),
        flops=8 * row_count * row_count * count * count * lanes,
    )
    return (found[0], found[1], found[2:])


def head_backward(info, sources, grads, out, log_sum, seq_count, head_dim):
    count = len(sources) // 3
    row_count = sources[-1].shape[0]
    block_len = row_count // seq_count
    heads_rows = lanes // head_dim * block_len
    total = 2 * count * block_len
    found = whole_call(
        functools.partial(attend_back_kernel, count),
        [shape_of((row_count, lanes), bf16)] * count
        + [shape_of((row_count, lanes), f32)] * count
        + [shape_of((row_count, lanes), bf16)] * count,
        [*sources, *grads, out, log_sum],
        scalars=(info,),
        scratch=head_scratch(seq_count, count, block_len, head_dim)
        + [
            pltpu.VMEM((seq_count * count, heads_rows, head_dim), bf16),
            pltpu.VMEM((seq_count, total, head_dim), f32),
            pltpu.VMEM((seq_count, total, head_dim), f32),
            pltpu.VMEM((count, row_count, lanes), bf16),
        ],
        flops=20 * row_count * row_count * count * count * lanes,
    )
    return (found[:count], found[count : 2 * count], found[2 * count :])


def gathered_scores(query_grouped, key_piece, query_pos, lowest_pos, key_pos):
    head_dim = query_grouped.shape[-1]
    keys_split = key_piece.reshape(
        key_piece.shape[0], key_piece.shape[1], query_grouped.shape[2], head_dim
    )
    scores = jnp.einsum(
        "sqhgd,skhd->shgqk", query_grouped, keys_split, preferred_element_type=f32
    ) * head_dim ** (-0.5)
    allowed = (key_pos[None, None, :] <= query_pos[None, :, None]) & (
        key_pos[None, None, :] >= lowest_pos[:, :, None]
    )
    allowed = allowed[:, None, None, :, :]
    return (jnp.where(allowed, scores, negative), allowed, keys_split)


def gathered_forward(query_grouped, key_rows, value_rows, query_index, lowest_key):
    key_all = lax.all_gather(key_rows, "ctx", axis=1, tiled=True)
    value_all = lax.all_gather(value_rows, "ctx", axis=1, tiled=True)
    key_pos = jnp.arange(key_all.shape[1], dtype=jnp.int32)
    scores, allowed, keys_split = gathered_scores(
        query_grouped, key_all, query_index, lowest_key, key_pos
    )
    top = jnp.max(scores, axis=-1)
    weights = jnp.where(allowed, jnp.exp(scores - top[..., None]), 0.0)
    row_sum = jnp.sum(weights, axis=-1)
    summed = jnp.einsum(
        "shgqk,skhd->shgqd",
        weights.astype(bf16),
        value_all.reshape(keys_split.shape),
        preferred_element_type=f32,
    )
    attended = (summed / row_sum[..., None]).astype(bf16)
    return (jnp.transpose(attended, (0, 3, 1, 2, 4)), top + jnp.log(row_sum), key_all, value_all)


def gathered_backward(
    query_grouped, grad_grouped, attended, log_sum, key_all, value_all, query_index, lowest_key
):
    scale = query_grouped.shape[-1] ** (-0.5)
    key_pos = jnp.arange(key_all.shape[1], dtype=jnp.int32)
    delta_rows = jnp.sum(grad_grouped.astype(f32) * attended.astype(f32), axis=-1)
    delta_stat = jnp.transpose(delta_rows, (0, 2, 3, 1))
    scores, allowed, keys_split = gathered_scores(
        query_grouped, key_all, query_index, lowest_key, key_pos
    )
    probs = jnp.where(allowed, jnp.exp(scores - log_sum[..., None]), 0.0)
    grad_probs = jnp.einsum(
        "sqhgd,skhd->shgqk",
        grad_grouped,
        value_all.reshape(keys_split.shape),
        preferred_element_type=f32,
    )
    grad_scores = (probs * (grad_probs - delta_stat[..., None])).astype(bf16)
    query_grad = (
        jnp.einsum("shgqk,skhd->sqhgd", grad_scores, keys_split, preferred_element_type=f32) * scale
    )
    key_grad = (
        jnp.einsum("shgqk,sqhgd->skhd", grad_scores, query_grouped, preferred_element_type=f32)
        * scale
    )
    value_grad = jnp.einsum(
        "shgqk,sqhgd->skhd", probs.astype(bf16), grad_grouped, preferred_element_type=f32
    )
    key_own, value_own = (
        lax.psum_scatter(part.reshape(key_all.shape), "ctx", scatter_dimension=1, tiled=True)
        for part in (key_grad, value_grad)
    )
    return (query_grad, key_own, value_own)


def split_dot(value, table):
    high = value.astype(bf16)
    low = (value - high.astype(f32)).astype(bf16)
    return dot_f32(high, table, 1, 0) + dot_f32(low, table, 1, 0)


def head_table(head_dim):
    row = lax.broadcasted_iota(jnp.int32, (lanes, lanes), 0) // head_dim
    col = lax.broadcasted_iota(jnp.int32, (lanes, lanes), 1) // head_dim
    return jnp.where(row == col, 1.0 / head_dim, 0.0).astype(bf16)


def swap_halves(value, head_dim):
    lane = lax.broadcasted_iota(jnp.int32, value.shape, 1)
    ahead = pltpu.roll(value, lanes - head_dim // 2, 1)
    behind = pltpu.roll(value, head_dim // 2, 1)
    return jnp.where(lane % head_dim < head_dim // 2, ahead, behind)


def front_kernel(
    head_dim,
    info_ref,
    tokens_ref,
    cot_ref,
    gain_ref,
    query_w_ref,
    key_w_ref,
    value_w_ref,
    q_gain_ref,
    k_gain_ref,
    pos_ref,
    normed_ref,
    early_ref,
    query_ref,
    key_ref,
    cos_ref,
    sin_ref,
    *refs,
):
    count = (len(refs) - 2) // 2
    block_refs = refs[:count]
    pair_refs = refs[count : 2 * count]
    blocks_ref, pairs_ref = refs[2 * count :]
    seq_count, block_len = pos_ref.shape
    half_dim = head_dim // 2
    places = pos_ref[...]
    spare = jnp.zeros((8 - seq_count, block_len), f32)
    columns = jnp.concatenate([places.astype(f32), spare], axis=0).T
    lane_row = lax.broadcasted_iota(jnp.int32, (1, lanes), 1)
    exponent = (lane_row % half_dim).astype(f32) * (-2.0 / head_dim)
    frequency = jnp.exp(exponent * math.log(theta_base))
    sign = jnp.where(lane_row % head_dim < half_dim, -1.0, 1.0)
    for seq in range(seq_count):
        angles = columns[:, seq : seq + 1] * frequency
        cos_ref[seq * block_len : (seq + 1) * block_len, :] = jnp.cos(angles)
        sin_ref[seq * block_len : (seq + 1) * block_len, :] = jnp.sin(angles) * sign
    packed_pos = jnp.concatenate([places >> pos_shift, places & (pos_base - 1)], axis=0).astype(f32)
    fill = jnp.zeros((pos_rows - 2 * seq_count, block_len), f32)
    pos_tail = jnp.concatenate([packed_pos, fill], axis=0).astype(bf16)
    q_gain_row = jnp.concatenate([q_gain_ref[...]] * (lanes // head_dim), axis=1)
    k_gain_row = jnp.concatenate([k_gain_ref[...]] * (lanes // head_dim), axis=1)
    rows = tokens_ref[...].astype(f32)
    stat = lax.rsqrt(jnp.mean(rows * rows, axis=1, keepdims=True) + eps_norm)
    normed = (rows * stat * gain_ref[...]).astype(bf16)
    normed_ref[...] = normed
    half = rows.shape[0] // 2
    model_width = rows.shape[1]
    half_rows = pl.ds(pl.multiple_of(info_ref[at_core] * half, half), half)
    early_ref[:, :model_width] = cot_ref[half_rows, :]
    early_ref[:, model_width:] = normed_ref[half_rows, :]
    query = dot_f32(normed, query_w_ref[...], 1, 0)
    key = dot_f32(normed, key_w_ref[...], 1, 0)
    value = dot_f32(normed, value_w_ref[...], 1, 0).astype(bf16).astype(f32)
    query_ref[...] = query
    key_ref[...] = key
    table = head_table(head_dim)
    cosine = cos_ref[...]
    sine = sin_ref[...]
    kv_heads = key.shape[1] // head_dim
    lane = lax.broadcasted_iota(jnp.int32, (rows.shape[0], lanes), 1)

    def turned(tile, gain):
        stat_val = lax.rsqrt(split_dot(tile * tile, table) + eps_norm)
        scaled = tile * stat_val * gain
        return scaled * cosine + swap_halves(scaled, head_dim) * sine

    for head in range(kv_heads):
        query_tile = turned(query[:, head * lanes : (head + 1) * lanes], q_gain_row).astype(bf16)
        pair = slice(head // 2 * lanes, (head // 2 + 1) * lanes)
        key_tile = turned(key[:, pair], k_gain_row)
        value_tile = value[:, pair]
        if head % 2 == 0:
            value_tile = pltpu.roll(value_tile, head_dim, 1)
        else:
            key_tile = pltpu.roll(key_tile, head_dim, 1)
        both = jnp.where(lane < head_dim, key_tile, value_tile).astype(bf16)
        row_count = rows.shape[0]
        blocks_ref[head, :row_count, :] = query_tile
        blocks_ref[head, row_count:, :] = pos_tail
        pairs_ref[head] = both
    for flip in range(count):
        head = info_ref[at_level] ^ flip
        block_refs[flip][...] = blocks_ref[head]
        pair_refs[flip][...] = pairs_ref[head]


def project_kernel(info_ref, *refs):
    count = (len(refs) - 3) // 2
    block_refs = refs[:count]
    weight_ref, part_ref = refs[count : count + 2]
    send_refs = refs[count + 2 : 2 * count + 2]
    heads_ref = refs[2 * count + 2]
    for flip in range(count):
        heads_ref[info_ref[at_level] ^ flip] = block_refs[flip][...]
    total = None
    for head in range(count):
        found = dot_f32(heads_ref[head], weight_ref[:, head * lanes : (head + 1) * lanes], 1, 1)
        total = found if total is None else total + found
    part_ref[...] = total.astype(bf16)
    for flip in range(plane):
        send_refs[flip][...] = heads_ref[info_ref[at_place] ^ flip]


def ffn_kernel(
    steps,
    info_ref,
    tokens_ref,
    own_ref,
    other_ref,
    gain_ref,
    cot_ref,
    gate_ref,
    up_ref,
    down_ref,
    mixed_ref,
    normed_ref,
    half_ref,
    ffn_ref,
    back_ref,
    *refs,
):
    hidden_refs = refs[:plane]
    both_refs = refs[plane : 2 * plane]
    ffn_acc, back_acc, hidden_buf, gate_buf, up_buf = refs[2 * plane :]
    step = pl.program_id(0)
    tile = gate_ref.shape[1]
    width = hidden_refs[0].shape[1]
    half = steps * tile // 2

    @pl.when(step == 0)
    def _():
        mixed = tokens_ref[...].astype(f32) + (own_ref[...].astype(f32) + other_ref[...].astype(f32))
        mixed_ref[...] = mixed
        stat = lax.rsqrt(jnp.mean(mixed * mixed, axis=1, keepdims=True) + eps_norm)
        normed_ref[...] = (mixed * stat * gain_ref[...]).astype(bf16)
        half_count = half_ref.shape[0]
        start = pl.multiple_of(info_ref[at_core] * half_count, half_count)
        half_ref[...] = normed_ref[pl.ds(start, half_count), :]
        ffn_acc[...] = jnp.zeros_like(ffn_acc)
        back_acc[...] = jnp.zeros_like(back_acc)

    normed = normed_ref[...]
    gate = dot_f32(normed, gate_ref[...], 1, 0)
    up = dot_f32(normed, up_ref[...], 1, 0)
    grad = dot_f32(cot_ref[...], down_ref[...], 1, 0)
    sig = jax.nn.sigmoid(gate)
    silu = gate * sig
    hidden = (silu * up).astype(bf16)
    cols = pl.ds(pl.multiple_of(step * tile, tile), tile)
    hidden_buf[:, cols] = hidden
    grad_gate = (grad * up * (sig * (1.0 + gate * (1.0 - sig)))).astype(bf16)
    grad_up = (grad * silu).astype(bf16)
    gate_buf[:, cols] = grad_gate
    up_buf[:, cols] = grad_up
    ffn_acc[...] += dot_f32(hidden, down_ref[...], 1, 1)
    back_acc[...] += dot_f32(grad_gate, gate_ref[...], 1, 1) + dot_f32(grad_up, up_ref[...], 1, 1)

    @pl.when(step == steps - 1)
    def _():
        ffn_ref[...] = ffn_acc[...].astype(bf16)
        back_ref[...] = back_acc[...].astype(bf16)
        for flip in range(plane):
            member = info_ref[at_place] ^ flip
            start = (member % 2) * half + (member // 2) * (half - width)
            hidden_refs[flip][...] = hidden_buf[:, pl.ds(pl.multiple_of(start, lanes), width)]
            side = pl.ds(pl.multiple_of(member // 2 * half, lanes), half)

            @pl.when(member % 2 == 0)
            def _():
                both_refs[flip][...] = gate_buf[:, side]

            @pl.when(member % 2 == 1)
            def _():
                both_refs[flip][...] = up_buf[:, side]


def ffn_call(info, tokens_in, own, other, gain, cot, w_gate, w_up, w_down):
    row_count, model_width = tokens_in.shape
    cols = w_gate.shape[1]
    half, width = window(cols)
    tile = ffn_tile
    steps = cols // tile
    fixed = lambda *shape: pl.BlockSpec(shape, lambda step, info_ref: (0,) * len(shape))
    moving = pl.BlockSpec((model_width, tile), lambda step, info_ref: (0, step))
    rows_spec = fixed(row_count, model_width)
    wide = (row_count, model_width)
    found = pl.pallas_call(
        functools.partial(ffn_kernel, steps),
        grid_spec=pltpu.PrefetchScalarGridSpec(
            num_scalar_prefetch=1,
            grid=(steps,),
            in_specs=[rows_spec, rows_spec, rows_spec, fixed(1, model_width), rows_spec]
            + [moving] * 3,
            out_specs=[rows_spec, rows_spec, fixed(row_count // 2, model_width)]
            + [rows_spec] * 2
            + [fixed(row_count, width)] * plane
            + [fixed(row_count, half)] * plane,
            scratch_shapes=[pltpu.VMEM(wide, f32), pltpu.VMEM(wide, f32)]
            + [pltpu.VMEM((row_count, cols), bf16)] * 3,
        ),
        out_shape=[
            shape_of(wide, f32),
            shape_of(wide, bf16),
            shape_of((row_count // 2, model_width), bf16),
            shape_of(wide, bf16),
            shape_of(wide, bf16),
        ]
        + [shape_of((row_count, width), bf16)] * plane
        + [shape_of((row_count, half), bf16)] * plane,
        cost_estimate=pl.CostEstimate(
            flops=16 * row_count * model_width * cols,
            bytes_accessed=6 * model_width * cols,
            transcendentals=row_count * cols,
        ),
        compiler_params=pltpu.CompilerParams(vmem_limit_bytes=vmem_limit),
        name="ffn",
    )(info, tokens_in, own, other, gain, cot, w_gate, w_up, w_down)
    return (*found[:5], found[5 : 5 + plane], found[5 + plane :])


def middle_kernel(
    info_ref,
    mixed_ref,
    ffn_own_ref,
    ffn_other_ref,
    back_own_ref,
    back_other_ref,
    gain_ref,
    cot_ref,
    weight_ref,
    *refs,
):
    head_refs = refs[: plane - 1]
    layer_ref, grad_ref, rounded_ref, row_ref = refs[plane - 1 : plane + 3]
    pack_refs = refs[plane + 3 : 2 * plane + 2]
    send_refs = refs[2 * plane + 2 : -1]
    blocks_ref = refs[-1]
    mixed = mixed_ref[...]
    layer_ref[...] = mixed + (ffn_own_ref[...].astype(f32) + ffn_other_ref[...].astype(f32))
    found = back_own_ref[...].astype(f32) + back_other_ref[...].astype(f32)
    stat = lax.rsqrt(jnp.mean(mixed * mixed, axis=1, keepdims=True) + eps_norm)
    row_ref[...] = jnp.broadcast_to(
        jnp.sum(found * mixed * stat, axis=0, keepdims=True), row_ref.shape
    )
    grad = cot_ref[...].astype(f32) + rms_back(found * gain_ref[...], mixed, stat)
    grad_ref[...] = grad
    rounded = grad.astype(bf16)
    rounded_ref[...] = rounded
    attended = dot_f32(rounded, weight_ref[...], 1, 0).astype(bf16)
    for head in range(blocks_ref.shape[0]):
        blocks_ref[head] = attended[:, head * lanes : (head + 1) * lanes]
    for flip, send_ref in enumerate(send_refs):
        send_ref[...] = blocks_ref[info_ref[at_level] ^ flip]
    half, model_width = mixed.shape[0] // 2, mixed.shape[1]
    half_rows = pl.ds(pl.multiple_of(info_ref[at_core] * half, half), half)
    for pack_ref, head_ref in zip(pack_refs, head_refs):
        pack_ref[:, :model_width] = rounded_ref[half_rows, :]
        pack_ref[:, model_width : model_width + lanes] = head_ref[:half, :]
        pack_ref[:, model_width + lanes :] = head_ref[half:, :]


def turn_back_kernel(head_dim, info_ref, *refs):
    count = (len(refs) - 14 - plane) // 2
    block_refs = refs[:count]
    other_refs = refs[count : 2 * count]
    (
        query_ref,
        key_ref,
        q_gain_ref,
        k_gain_ref,
        cos_ref,
        sin_ref,
        query_w_ref,
        key_w_ref,
        value_w_ref,
        part_ref,
        gain_row_ref,
    ) = refs[2 * count : 2 * count + 11]
    send_refs = refs[2 * count + 11 : 2 * count + 11 + plane]
    query_buf, pair_buf, raw_ref = refs[2 * count + 11 + plane :]
    kv_heads = count
    for flip in range(count):
        head = info_ref[at_level] ^ flip
        query_buf[head] = block_refs[flip][...]
        pair_buf[head] = other_refs[flip][...].astype(f32)
    table = head_table(head_dim)
    cosine = cos_ref[...]
    sine = sin_ref[...]
    q_gain_row = jnp.concatenate([q_gain_ref[...]] * (lanes // head_dim), axis=1)
    k_gain_row = jnp.concatenate([k_gain_ref[...]] * (lanes // head_dim), axis=1)
    lane = lax.broadcasted_iota(jnp.int32, cosine.shape, 1)

    def back(grad_rot, raw, gain):
        grad_norm = grad_rot * cosine - swap_halves(grad_rot, head_dim) * sine
        stat = lax.rsqrt(split_dot(raw * raw, table) + eps_norm)
        gain_row = jnp.sum(grad_norm * raw * stat, axis=0, keepdims=True)
        grad_in = grad_norm * gain
        grad_raw = stat * grad_in - raw * stat**3 * split_dot(grad_in * raw, table)
        return (grad_raw.astype(bf16), gain_row)

    total = None
    gain_rows = [None, None]
    place = 0
    per_slot = raw_ref.shape[2] // lanes

    def emit(tile, weight, kind, gain_row):
        nonlocal total, place
        slot = place % per_slot
        raw_ref[place // per_slot, :, slot * lanes : (slot + 1) * lanes] = tile
        place += 1
        found = dot_f32(tile, weight, 1, 1)
        total = found if total is None else total + found
        if gain_row is not None:
            gain_rows[kind] = gain_row if gain_rows[kind] is None else gain_rows[kind] + gain_row

    for head in range(kv_heads):
        cols = slice(head * lanes, (head + 1) * lanes)
        tile, gain_row = back(query_buf[head].astype(f32), query_ref[:, cols], q_gain_row)
        emit(tile, query_w_ref[:, cols], 0, gain_row)
    for pair in range(kv_heads // 2):
        cols = slice(pair * lanes, (pair + 1) * lanes)
        first = pair_buf[2 * pair]
        second = pair_buf[2 * pair + 1]
        merged = jnp.where(lane < head_dim, first, pltpu.roll(second, head_dim, 1))
        tile, gain_row = back(merged, key_ref[:, cols], k_gain_row)
        emit(tile, key_w_ref[:, cols], 1, gain_row)
    for pair in range(kv_heads // 2):
        cols = slice(pair * lanes, (pair + 1) * lanes)
        first = pair_buf[2 * pair]
        second = pair_buf[2 * pair + 1]
        merged = jnp.where(lane < head_dim, pltpu.roll(first, head_dim, 1), second).astype(bf16)
        emit(merged, value_w_ref[:, cols], 1, None)
    part_ref[...] = total.astype(bf16)
    gain_row_ref[...] = jnp.concatenate(gain_rows + [jnp.zeros((6, lanes), f32)], axis=0)
    for flip in range(plane):
        send_refs[flip][...] = raw_ref[info_ref[at_place] ^ flip]


def last_kernel(tokens_ref, grad_ref, own_ref, other_ref, gain_ref, out_ref, row_ref):
    rows = tokens_ref[...].astype(f32)
    stat = lax.rsqrt(jnp.mean(rows * rows, axis=1, keepdims=True) + eps_norm)
    found = own_ref[...].astype(f32) + other_ref[...].astype(f32)
    row_ref[...] = jnp.broadcast_to(
        jnp.sum(found * rows * stat, axis=0, keepdims=True), row_ref.shape
    )
    out_ref[...] = grad_ref[...] + rms_back(found * gain_ref[...], rows, stat)


def plane_gather(mine):
    near = [xor_swap(mine, everywhere, flip) for flip in range(1, plane)]
    far = [xor_swap(found, "tp", 1) for found in near]
    return (near, far)


def window(cols):
    half = cols // 2
    width = min(half, -(-half // (2 * lanes)) * lanes)
    return (half, width)


def rows_kernel(jobs, steps, info_ref, *refs):
    step = pl.program_id(0)
    gain_refs = refs[-5 - 2 * len(jobs) : -2 - 2 * len(jobs)]
    send_ref, keep_ref = refs[-2 - 2 * len(jobs) : -2 * len(jobs)]
    bufs = refs[-2 * len(jobs) :]
    height = keep_ref.shape[1]
    core = info_ref[at_core]
    used = 0
    offset = 0
    pieces = []
    for number, (packed, width) in enumerate(jobs):
        row_buf, col_buf = bufs[2 * number : 2 * number + 2]
        own_ref = refs[used]
        near_refs = refs[used + 1 : used + plane]
        far_refs = refs[used + plane : used + 2 * plane - 1]
        used += 2 * plane - 1
        row_count = own_ref.shape[0]
        half = row_count // 2
        col_count = 2 * plane - 1 if packed else plane
        col_refs = refs[used : used + col_count]
        used += col_count

        @pl.when(step == 0)
        def _():
            if packed:
                col_buf[:row_count, :] = col_refs[0][...]
                for n, col_ref in enumerate(col_refs[1:]):
                    start = row_count + n * half
                    col_buf[start : start + half, :] = col_ref[...]
            else:
                for n, col_ref in enumerate(col_refs):
                    col_buf[n * row_count : (n + 1) * row_count, :] = col_ref[...]

        row_buf[:row_count, :] = own_ref[...]
        for n in range(plane - 1):
            base = (n + 1) * row_count
            near_rows = pl.ds(pl.multiple_of(base + core * half, half), half)
            far_rows = pl.ds(pl.multiple_of(base + (1 - core) * half, half), half)
            row_buf[near_rows, :] = near_refs[n][...]
            row_buf[far_rows, :] = far_refs[n][...]
        pieces.append((offset, width, dot_f32(row_buf[...], col_buf[...], 0, 0)))
        offset += width
    if offset < keep_ref.shape[2]:
        ffn_ref, attn_ref, head_ref = gain_refs
        rows = [ffn_ref[:1, :], attn_ref[:1, :]]
        for n in range(2):
            rows.append(jnp.concatenate([head_ref[n : n + 1, :]] * (height // lanes), axis=1))
        rows.append(jnp.zeros((lanes - 4, height), f32))
        pieces.append((offset, lanes, jnp.concatenate(rows, axis=0).T))

    @pl.when(step < steps)
    def _():
        for offset, width, found in pieces:
            send_ref[0, :, offset : offset + width] = found.astype(bf16)

    @pl.when(step >= steps)
    def _():
        for offset, width, found in pieces:
            keep_ref[0, :, offset : offset + width] = found


def fold_kernel(info_ref, kept_ref, found_ref, send_ref, keep_ref, *, slot):
    bit = info_ref[at_bits + slot]
    send_ref[...] = (kept_ref[1 - bit] + found_ref[1 - bit].astype(f32)).astype(bf16)
    keep_ref[...] = kept_ref[bit] + found_ref[bit].astype(f32)


def finish_kernel(jobs, info_ref, *refs):
    out_refs = refs[2 * jobs :]
    height = out_refs[0].shape[0]
    for flip, out_ref in enumerate(out_refs):
        start = pl.multiple_of((info_ref[at_place] ^ flip) * height, height)
        rows = pl.ds(start, height)
        offset = 0
        for n in range(jobs):
            kept_ref, found_ref = refs[2 * n : 2 * n + 2]
            width = kept_ref.shape[1]
            total = kept_ref[rows, :] + found_ref[rows, :].astype(f32)
            out_ref[:, offset : offset + width] = total.astype(out_ref.dtype)
            offset += width


class Halving:
    def __init__(self, index, total, model_width):
        self.blocks = total // plane
        self.model_width = model_width
        bits = self.blocks.bit_length() - 1
        self.fine = self.blocks == 4 and model_width // self.blocks % lanes == 0
        self.order = list(range(bits)) if self.fine else list(range(bits))[::-1]
        self.steps = 2 if self.fine else 1
        self.height = model_width // self.steps // 2
        block_index = index // plane
        self.bits = [(block_index >> bit) & 1 for bit in self.order]

    def rows(self, info, jobs, gains=None):
        steps, height = self.steps, self.height
        per_piece = self.model_width // height

        def block_of(step, info_ref):
            first = info_ref[at_bits]
            bit = jnp.where(step < steps, 1 - first, first)
            return 2 * (step % steps) + bit if steps > 1 else bit

        fixed = lambda *shape: pl.BlockSpec(shape, lambda step, info_ref: (0,) * len(shape))
        args, specs, scratch, shape_jobs = [], [], [], []
        flops = 0
        for (own, near, far, slot), cols in jobs:
            row_count = own.shape[0]
            half = row_count // 2
            packed = len(cols) == 1
            width = cols[0].shape[1]
            args += [own, *near, *far]
            specs.append(
                pl.BlockSpec((row_count, height), lambda step, ref: (0, block_of(step, ref)))
            )
            specs += [
                pl.BlockSpec(
                    (half, height),
                    lambda step, ref, base=slot * per_piece: (0, base + block_of(step, ref)),
                )
            ] * (2 * plane - 2)
            args.append(cols[0])
            specs.append(fixed(row_count, width))
            if packed:
                for part in near:
                    for n in range(2):
                        args.append(part)
                        spot = self.model_width // width + n
                        specs.append(
                            pl.BlockSpec((half, width), lambda step, ref, spot=spot: (0, spot))
                        )
            else:
                args += cols[1:]
                specs += [fixed(row_count, width)] * (plane - 1)
            scratch += [
                pltpu.VMEM((plane * row_count, height), bf16),
                pltpu.VMEM((plane * row_count, width), bf16),
            ]
            shape_jobs.append((packed, width))
            flops += 2 * plane * row_count * self.model_width * width
        total_width = sum(width for _, width in shape_jobs)
        if gains is not None:
            total_width += lanes
            row_spec = pl.BlockSpec((8, height), lambda step, ref: (0, block_of(step, ref)))
            specs += [row_spec, row_spec, fixed(8, lanes)]
        else:
            gains = [jnp.zeros((8, lanes), f32)] * 3
            specs += [fixed(8, lanes)] * 3
        args += gains
        out = (1, height, total_width)
        return pl.pallas_call(
            functools.partial(rows_kernel, shape_jobs, steps),
            grid_spec=pltpu.PrefetchScalarGridSpec(
                num_scalar_prefetch=1,
                grid=(2 * steps,),
                in_specs=specs,
                out_specs=[
                    pl.BlockSpec(out, lambda step, ref: (jnp.minimum(step, steps - 1), 0, 0)),
                    pl.BlockSpec(out, lambda step, ref: (jnp.maximum(step - steps, 0), 0, 0)),
                ],
                scratch_shapes=scratch,
            ),
            out_shape=[
                shape_of((steps, height, total_width), bf16),
                shape_of((steps, height, total_width), f32),
            ],
            cost_estimate=pl.CostEstimate(
                flops=flops,
                bytes_accessed=sum(arg.size * arg.dtype.itemsize for arg in args)
                + 6 * steps * height * total_width,
                transcendentals=0,
            ),
            compiler_params=pltpu.CompilerParams(vmem_limit_bytes=vmem_limit),
            name="rows",
        )(info, *args)

    def start(self, turn, sent):
        return xor_swap(sent, everywhere, plane << self.order[turn])

    def fold(self, info, turn, kept, found):
        width = kept.shape[-1]
        rows_left = kept.size // width // 2
        send, keep = whole_call(
            functools.partial(fold_kernel, slot=turn),
            [shape_of((rows_left, width), bf16), shape_of((rows_left, width), f32)],
            [kept.reshape(2, rows_left, width), found.reshape(2, rows_left, width)],
            scalars=(info,),
        )
        return (keep, self.start(turn, send))

    def through(self, info, rows):
        sent, kept = rows
        found = self.start(0, sent)
        for turn in range(1, len(self.order)):
            kept, found = self.fold(info, turn, kept, found)
        return (kept.reshape(-1, kept.shape[-1]), found.reshape(-1, kept.shape[-1]))


def return_rows(info, sums):
    height = sums[0][0].shape[0] // plane
    width = sum(kept.shape[1] for kept, _ in sums)
    parts = whole_call(
        functools.partial(finish_kernel, len(sums)),
        [shape_of((height, width), bf16 if flip else f32) for flip in range(plane)],
        [value for pair in sums for value in pair],
        scalars=(info,),
    )
    return plane_swap(parts)


def assemble_kernel(moves, gain_start, info_ref, *refs):
    part_refs = refs[:plane]
    out_refs = refs[plane:]
    for flip in range(plane):
        for member in range(plane):

            @pl.when((info_ref[at_place] ^ flip) == member)
            def _():
                for out, out_start, start, width in moves[member]:
                    out_refs[out][:, out_start : out_start + width] = part_refs[flip][
                        :, start : start + width
                    ].astype(f32)

    if gain_start is not None:
        cols = slice(gain_start, gain_start + lanes)
        total = sum(part_ref[:, cols].astype(f32) for part_ref in part_refs).T
        for n in range(4):
            out_refs[len(out_refs) - 4 + n][...] = total[n : n + 1, :]


def assemble(info, parts, moves, widths, gain_start=None):
    height = parts[0].shape[0]
    outs = [shape_of((height, width), f32) for width in widths]
    if gain_start is not None:
        outs += [shape_of((1, height), f32)] * 4
    return whole_call(
        functools.partial(assemble_kernel, moves, gain_start), outs, parts, scalars=(info,)
    )


def shards(
    tokens,
    positions,
    attn_gain,
    ffn_gain,
    q_gain,
    k_gain,
    w_query,
    w_key,
    w_value,
    w_out,
    w_gate,
    w_up,
    w_down,
    cotangent,
):
    seq_count, block_len, model_width = tokens.shape
    row_count = seq_count * block_len
    head_dim = q_gain.shape[0]
    q_heads = w_query.shape[1] // head_dim
    kv_heads = w_key.shape[1] // head_dim
    key_width = kv_heads * head_dim
    query_width = q_heads * head_dim
    group_size = q_heads // kv_heads
    hidden_width = w_gate.shape[1]
    ctx_size = lax.axis_size("ctx")
    total = ctx_size * lax.axis_size("seq")
    here_index = lax.axis_index("ctx")
    index = lax.axis_index(everywhere)
    by_head = ctx_size == 2 * kv_heads
    rows_bf = shape_of((row_count, model_width), bf16)
    rows_f32 = shape_of((row_count, model_width), f32)
    head_block = shape_of((row_count, lanes), bf16)
    full_block = shape_of((row_count + pos_rows, lanes), bf16)
    halving = Halving(index, total, model_width)
    info = jnp.stack(
        [
            here_index // 2 if by_head else jnp.int32(0),
            here_index % 2,
            lax.axis_index("tp"),
            index % plane,
            *halving.bits,
        ]
    ).astype(jnp.int32)

    cot_rows = cotangent.reshape(row_count, model_width)
    token_rows = tokens.reshape(row_count, model_width)
    pack_width = 2 * lanes
    q_gain_row = q_gain[None, :]
    k_gain_row = k_gain[None, :]
    attn_gain_row = attn_gain[None, :]
    ffn_gain_row = ffn_gain[None, :]

    normed_one, early_half, query_raw, key_raw, cosine, sine, *found = whole_call(
        functools.partial(front_kernel, head_dim),
        [
            rows_bf,
            shape_of((row_count // 2, 2 * model_width), bf16),
            shape_of((row_count, query_width), f32),
            shape_of((row_count, key_width), f32),
            shape_of((row_count, lanes), f32),
            shape_of((row_count, lanes), f32),
        ]
        + [full_block] * kv_heads
        + [head_block] * kv_heads,
        [
            stay(token_rows),
            stay(cot_rows),
            stay(attn_gain_row),
            stay(w_query),
            stay(w_key),
            stay(w_value),
            stay(q_gain_row),
            stay(k_gain_row),
            stay(positions),
        ],
        scalars=(info,),
        scratch=[
            pltpu.VMEM((kv_heads, row_count + pos_rows, lanes), bf16),
            pltpu.VMEM((kv_heads, row_count, lanes), bf16),
        ],
        flops=2 * row_count * model_width * (query_width + 2 * key_width),
    )
    packed, pair_parts = found[:kv_heads], found[kv_heads:]

    if by_head:
        pairs = level_swap(pair_parts)
        blocks = level_swap(packed)
        sources = [*blocks, *pairs, *side_swap(pairs)]
        out_heads, log_sum, out_parts = head_forward(info, sources, seq_count, head_dim)
        out_blocks = level_swap(out_parts)
    else:
        flat = jnp.concatenate(
            [jnp.stack([part[:row_count] for part in packed]), jnp.stack(pair_parts)], axis=2
        )
        flat = flat.reshape(kv_heads, seq_count, block_len, pack_width)
        flat = jnp.transpose(flat, (1, 2, 0, 3))
        query_grouped = flat[..., :lanes].reshape(
            seq_count, block_len, kv_heads, group_size, head_dim
        )
        query_index = here_index * block_len + jnp.arange(block_len, dtype=jnp.int32)
        lowest_key = query_index[None, :] - positions
        attended_grouped, log_sum, key_all, value_all = gathered_forward(
            query_grouped,
            flat[..., lanes : lanes + head_dim].reshape(seq_count, block_len, key_width),
            flat[..., lanes + head_dim :].reshape(seq_count, block_len, key_width),
            query_index,
            lowest_key,
        )
        out_blocks = list(
            jnp.transpose(attended_grouped, (2, 0, 1, 3, 4)).reshape(kv_heads, row_count, lanes)
        )

    early_near, early_far = plane_gather(early_half)
    cot_pieces = (cot_rows, early_near, early_far, 0)
    one_pieces = (normed_one, early_near, early_far, 1)

    attn_part, *head_parts = whole_call(
        project_kernel,
        [rows_bf] + [head_block] * plane,
        [*out_blocks, w_out],
        scalars=(info,),
        scratch=[pltpu.VMEM((kv_heads, row_count, lanes), bf16)],
        flops=2 * row_count * model_width * query_width,
    )
    mixed, normed_two, two_half, ffn_part, back_part, hidden_parts, both_parts = ffn_call(
        info,
        token_rows,
        attn_part,
        named_swap(attn_part),
        ffn_gain_row,
        cot_rows,
        stay(w_gate),
        stay(w_up),
        stay(w_down),
    )
    ffn_other = named_swap(ffn_part)
    back_other = named_swap(back_part)
    hidden_plane = plane_swap(hidden_parts)
    both_near = [xor_swap(both_parts[1], everywhere, 1)]
    both_near += [xor_swap(both_parts[flip], everywhere, flip) for flip in (2, 3)]
    both_plane = [both_parts[0], *both_near]
    two_near, two_far = plane_gather(two_half)
    two_pieces = (normed_two, two_near, two_far, 0)
    half, width = window(hidden_width)

    pack_block = shape_of((row_count // 2, model_width + 2 * lanes), bf16)
    layer_output, grad_mixed, grad_mixed_bf, ffn_row, *found = whole_call(
        middle_kernel,
        [rows_f32, rows_f32, rows_bf, shape_of((8, model_width), f32)]
        + [pack_block] * (plane - 1)
        + [head_block] * kv_heads,
        [
            mixed,
            ffn_part,
            ffn_other,
            back_part,
            back_other,
            ffn_gain_row,
            cot_rows,
            w_out,
            *head_parts[1:],
        ],
        scalars=(info,),
        scratch=[pltpu.VMEM((kv_heads, row_count, lanes), bf16)],
        flops=2 * row_count * model_width * query_width,
    )
    mixed_packs, grad_parts = found[: plane - 1], found[plane - 1 :]

    if by_head:
        grads = level_swap(grad_parts)
        query_parts, own_parts, other_parts = head_backward(
            info, sources, grads, out_heads, log_sum, seq_count, head_dim
        )
        crossed = side_swap(other_parts)
        returned = level_swap(query_parts)
        pair_sums = whole_call(
            functools.partial(merge_kernel, kv_heads),
            [head_block] * kv_heads,
            [*own_parts, *crossed],
        )
        others = level_swap(pair_sums)
    else:
        grad_grouped = jnp.transpose(
            jnp.stack(grad_parts).reshape(kv_heads, seq_count, block_len, group_size, head_dim),
            (1, 2, 0, 3, 4),
        )
        query_grad, key_grad_own, value_grad_own = gathered_backward(
            query_grouped,
            grad_grouped,
            attended_grouped,
            log_sum,
            key_all,
            value_all,
            query_index,
            lowest_key,
        )
        shaped = lambda grad: grad.reshape(seq_count, block_len, kv_heads, -1)
        returned = jnp.concatenate(
            [shaped(query_grad), shaped(key_grad_own), shaped(value_grad_own)], axis=-1
        ).astype(bf16)
        returned = jnp.transpose(returned, (2, 0, 1, 3)).reshape(kv_heads, row_count, pack_width)
        others = list(returned[..., lanes:])
        returned = list(returned[..., :lanes])

    down_sum = halving.through(info, halving.rows(info, [(cot_pieces, hidden_plane)]))
    both_sum = halving.through(info, halving.rows(info, [(two_pieces, both_plane)]))
    wide_parts = return_rows(info, [both_sum, down_sum])

    mixed_near = [xor_swap(pack, everywhere, flip + 1) for flip, pack in enumerate(mixed_packs)]
    mixed_far = [xor_swap(found, "tp", 1) for found in mixed_near]
    mixed_pieces = (grad_mixed_bf, mixed_near, mixed_far, 0)

    raw_width = (query_width + 2 * key_width) // plane
    one_part, head_rows, *raw_parts = whole_call(
        functools.partial(turn_back_kernel, head_dim),
        [rows_bf, shape_of((8, lanes), f32)] + [shape_of((row_count, raw_width), bf16)] * plane,
        [
            *returned,
            *others,
            query_raw,
            key_raw,
            q_gain_row,
            k_gain_row,
            cosine,
            sine,
            w_query,
            w_key,
            w_value,
        ],
        scalars=(info,),
        scratch=[
            pltpu.VMEM((kv_heads, row_count, lanes), bf16),
            pltpu.VMEM((kv_heads, row_count, lanes), f32),
            pltpu.VMEM((plane, row_count, raw_width), bf16),
        ],
        flops=2 * row_count * model_width * (query_width + 2 * key_width),
    )
    one_other = named_swap(one_part)
    head_sum = head_rows + named_swap(head_rows)
    head_sum = head_sum + jnp.roll(head_sum, head_dim, axis=1)
    raw_plane = plane_swap(raw_parts)
    input_grad, attn_row = whole_call(
        last_kernel,
        [rows_f32, shape_of((8, model_width), f32)],
        [token_rows, grad_mixed, one_part, one_other, attn_gain_row],
    )

    late_sum = halving.through(
        info,
        halving.rows(
            info,
            [(mixed_pieces, head_parts[:1]), (one_pieces, raw_plane)],
            [ffn_row, attn_row, head_sum],
        ),
    )
    late_parts = return_rows(info, [late_sum])

    skip = 2 * width - half
    wide_moves = []
    for member in range(plane):
        far_side = member // 2
        down_start = half * (member % 2) + far_side * width
        wide_moves.append(
            [
                (member % 2, half * far_side, 0, half),
                (2, down_start, half + far_side * skip, width - far_side * skip),
            ]
        )
    wgate_grad, wup_grad, wdown_grad = assemble(info, wide_parts, wide_moves, [hidden_width] * 3)

    out_width = lanes
    late_moves = []
    for member in range(plane):
        moves = [(0, member * out_width, 0, out_width)]
        for out, begin, size in (
            (1, 0, query_width),
            (2, query_width, key_width),
            (3, query_width + key_width, key_width),
        ):
            low = max(begin, member * raw_width)
            high = min(begin + size, (member + 1) * raw_width)
            if low < high:
                moves.append((out, low - begin, out_width + low - member * raw_width, high - low))
        late_moves.append(moves)
    wo_grad, wq_grad, wk_grad, wv_grad, *gain_rows = assemble(
        info,
        late_parts,
        late_moves,
        [query_width, query_width, key_width, key_width],
        out_width + raw_width,
    )
    ffngain_grad, attngain_grad, qgain_grad, kgain_grad = (row.reshape(-1) for row in gain_rows)
    if qgain_grad.shape[0] < head_dim:
        qgain_grad, kgain_grad = (
            lax.all_gather(row, everywhere, axis=0, tiled=True)[:head_dim]
            for row in (qgain_grad, kgain_grad)
        )
    else:
        qgain_grad, kgain_grad = qgain_grad[:head_dim], kgain_grad[:head_dim]
    return (
        layer_output.reshape(seq_count, block_len, model_width),
        input_grad.reshape(seq_count, block_len, model_width),
        wq_grad,
        wk_grad,
        wv_grad,
        wo_grad,
        wgate_grad,
        wup_grad,
        wdown_grad,
        attngain_grad,
        ffngain_grad,
        qgain_grad,
        kgain_grad,
    )


def solution(mesh):
    placed = (
        P("seq", "ctx", None),
        P("seq", "ctx"),
        P(),
        P(),
        P(),
        P(),
        P(None, "tp"),
        P(None, "tp"),
        P(None, "tp"),
        P(None, "tp"),
        P(None, "tp"),
        P(None, "tp"),
        P(None, "tp"),
        P("seq", "ctx", None),
    )
    return jax.shard_map(
        shards,
        mesh=mesh,
        in_specs=placed,
        out_specs=(
            P("seq", "ctx", None),
            P("seq", "ctx", None),
            P(("ctx", "seq"), "tp"),
            P(("ctx", "seq"), "tp"),
            P(("ctx", "seq"), "tp"),
            P(("ctx", "seq"), "tp"),
            P(("ctx", "seq"), "tp"),
            P(("ctx", "seq"), "tp"),
            P(("ctx", "seq"), "tp"),
            P(("ctx", "seq")),
            P(("ctx", "seq")),
            P(),
            P(),
        ),
        check_vma=False,
    )
```
